32 devices in a mesh: dp: 32 (over z, y, x, core).
Axes of the slice: x: 2, y: 2, z: 4, core: 2. Of those that a mesh axis runs over, the one named last changes fastest.
Arguments:
- x_in: bfloat16 [131072, 512], P('dp'), may hold values from -6 to 6
- grad_out: bfloat16 [131072, 512], P('dp'), may hold values from -6 to 6
- seq_lengths: int32 [32, 4], P('dp'), may hold values from 0 to 4096, as said below
- partners: int32 [32, 128], P('dp'), may hold values from 0 to 127, as said below
- w_qkv: float32 [512, 1536], P('dp'), may hold values from -0.25 to 0.25
- w_attn_out: float32 [512, 512], P('dp'), may hold values from -1 to 1
- w_sort: float32 [512, 128], P('dp'), may hold values from -0.25 to 0.25
- w_ffn_in: float32 [512, 2048], P('dp'), may hold values from -0.25 to 0.25
- w_ffn_out: float32 [2048, 512], P('dp'), may hold values from -0.125 to 0.125
- norm_params: float32 [512, 4], P('dp')
- moment_qkv: float32 [512, 1536], P('dp'), may hold values from -112 to 112
- moment_attn_out: float32 [512, 512], P('dp'), may hold values from -80 to 80
- moment_sort: float32 [512, 128], P('dp'), may hold values from -40 to 40
- moment_ffn_in: float32 [512, 2048], P('dp'), may hold values from -64 to 64
- moment_ffn_out: float32 [2048, 512], P('dp'), may hold values from -112 to 112
- moment_norms: float32 [512, 4], P('dp'), may hold values from -224 to 224
- square_qkv: float32 [512, 1536], P('dp'), may hold values from 32.768 to 131.072
- square_attn_out: float32 [512, 512], P('dp'), may hold values from 15.72864 to 62.91456
- square_sort: float32 [512, 128], P('dp'), may hold values from 5.24288 to 20.97152
- square_ffn_in: float32 [512, 2048], P('dp'), may hold values from 11.79648 to 47.18592
- square_ffn_out: float32 [2048, 512], P('dp'), may hold values from 32.768 to 131.072
- square_norms: float32 [512, 4], P('dp'), may hold values from 131.072 to 524.288
Outputs:
- out_block: bfloat16 [131072, 512], P('dp')
- grad_in: float32 [131072, 512], P('dp')
- new_w_qkv: float32 [512, 1536], P('dp')
- new_moment_qkv: float32 [512, 1536], P('dp')
- new_square_qkv: float32 [512, 1536], P('dp')
- new_w_attn_out: float32 [512, 512], P('dp')
- new_moment_attn_out: float32 [512, 512], P('dp')
- new_square_attn_out: float32 [512, 512], P('dp')
- new_w_sort: float32 [512, 128], P('dp')
- new_moment_sort: float32 [512, 128], P('dp')
- new_square_sort: float32 [512, 128], P('dp')
- new_w_ffn_in: float32 [512, 2048], P('dp')
- new_moment_ffn_in: float32 [512, 2048], P('dp')
- new_square_ffn_in: float32 [512, 2048], P('dp')
- new_w_ffn_out: float32 [2048, 512], P('dp')
- new_moment_ffn_out: float32 [2048, 512], P('dp')
- new_square_ffn_out: float32 [2048, 512], P('dp')
- new_norm_params: float32 [512, 4], P('dp')
- new_moment_norms: float32 [512, 4], P('dp')
- new_square_norms: float32 [512, 4], P('dp')
The draws below stay inside these ranges and needn't reach their ends.
Inputs may be any that keep to these rules, and one draw needn't show every extreme that they name: `seq_lengths`: row r either holds one sequence of more than 1024 tokens from the row's start, its other three entries being 0, or four sequences, the k-th starting at position k * 1024 and holding 4096 // 8 to 1024 tokens. Some row holds one sequence of exactly 4096 tokens. `partners`: entry (r, b) names a block of row r: for a live block, a live block of the same sequence; for any other block, b itself.
All inputs are finite; a program needn't handle non-finite values.
Results may differ from the reference program's by a relative error of at most 0.013.
The reference program's roundings to bfloat16 on the way count: a program that leaves them out, or rounds other values in their place, can miss the bound.
Values may be sent and summed in bfloat16 or wider, within the bound.
No kernel may reach another device: no remote copies, remote signals or barrier semaphores. Data moves between devices by JAX's collectives and lax.ppermute only.
A program may use at most 448 MiB of HBM per device.

```python
import math
import jax
import jax.numpy as jnp
from jax import lax

D = 512
FF = 2048
HEADS = 8
HEAD = 64
SORT = 64
BLOCK = 32
SINK = 8
STEP = 10
TOK_DEV = 4096
SLOTS = 32
TOKENS = 131072


def row_lengths(key):
    base = jax.random.fold_in(key, 11)
    kind_key, long_key, short_key, full_key = jax.random.split(base, 4)
    quarter = TOK_DEV // 4
    is_long = jax.random.randint(kind_key, (SLOTS,), 0, 2)
    long_len = jax.random.randint(long_key, (SLOTS,), quarter + 1, TOK_DEV + 1)
    short_len = jax.random.randint(short_key, (SLOTS, 4), quarter // 2, quarter + 1)
    chosen = jax.random.randint(full_key, (), 0, SLOTS)
    rows = jnp.arange(SLOTS, dtype=jnp.int32)
    is_long = jnp.where(rows == chosen, 1, is_long)
    long_len = jnp.where(rows == chosen, TOK_DEV, long_len)
    first = jnp.where(is_long == 1, long_len, short_len[:, 0])
    rest = jnp.where(is_long[:, None] == 1, 0, short_len[:, 1:])
    return jnp.concatenate([first[:, None], rest], axis=1).astype(jnp.int32)


def draw_seq_lengths(key, part):
    return row_lengths(key)


def draw_partners(key, part):
    lengths = row_lengths(key)
    quarter = TOK_DEV // 4
    blocks = TOK_DEV // BLOCK
    per_quarter = blocks // 4
    places = jnp.arange(blocks, dtype=jnp.int32)
    is_long = lengths[:, 0] > quarter
    member = jnp.where(is_long[:, None], 0, places[None, :] // per_quarter).astype(jnp.int32)
    length = jnp.take_along_axis(lengths, member, axis=1)
    start = jnp.where(is_long[:, None], 0, member * per_quarter).astype(jnp.int32)
    used = (length + BLOCK - 1) // BLOCK
    live = places[None, :] - start < used
    pick = jax.random.randint(jax.random.fold_in(key, 23), (SLOTS, blocks), 0, 1 << 20)
    partner = jnp.where(live, start + pick % jnp.maximum(used, 1), places[None, :])
    return partner.astype(jnp.int32)


def draw_norm_params(key, part):
    gain_key, shift_key = jax.random.split(jax.random.fold_in(key, 5))
    gains = jax.random.uniform(gain_key, (D, 2), jnp.float32, 0.6, 1.4)
    shifts = jax.random.normal(shift_key, (D, 2), jnp.float32) * 0.2
    return jnp.stack([gains[:, 0], shifts[:, 0], gains[:, 1], shifts[:, 1]], axis=1)


def shard_levels(own_key, shape, shards, least, largest):
    level, own = 1.0, jax.random.fold_in(own_key, 6)
    for dim, shards_of in shards:
        draws = jnp.exp(jax.random.uniform(jax.random.fold_in(own, dim), (shards_of,), jnp.float32, least / len(shards), largest / len(shards)))
        level = level * jnp.repeat(draws, shape[dim] // shards_of).reshape([-1 if axis == dim else 1 for axis in range(len(shape))])
    return level


def bell_draw(own_key, extent, deviation, most, cuts=(), kind=jnp.bfloat16):
    values = deviation * jax.random.normal(own_key, extent, jnp.float32)
    if cuts:
        values = values * shard_levels(own_key, extent, cuts, -0.22, 0.18)
    return jnp.clip(values, -most, most).astype(kind)


def setup_inputs(seed: int = 0) -> dict:
    splits = jax.random.split(jax.random.key(seed), 23)
    return {
        "x_in": bell_draw(splits[0], (TOKENS, D), 1.0, 6.0, ((0, 32),)),
        "grad_out": bell_draw(splits[1], (TOKENS, D), 1.0, 6.0, ((0, 32),)),
        "seq_lengths": draw_seq_lengths(jax.random.fold_in(splits[22], 71), 0),
        "partners": draw_partners(jax.random.fold_in(splits[22], 71), 0),
        "w_qkv": bell_draw(splits[4], (D, 3 * D), D ** -0.5, 0.25, ((0, 32),), jnp.float32),
        "w_attn_out": bell_draw(splits[5], (D, D), (D // 16) ** -0.5, 1.0, ((0, 32),), jnp.float32),
        "w_sort": bell_draw(splits[6], (D, 2 * SORT), D ** -0.5, 0.25, ((0, 32),), jnp.float32),
        "w_ffn_in": bell_draw(splits[7], (D, FF), D ** -0.5, 0.25, ((0, 32),), jnp.float32),
        "w_ffn_out": bell_draw(splits[8], (FF, D), FF ** -0.5, 0.125, ((0, 32),), jnp.float32),
        "norm_params": draw_norm_params(jax.random.fold_in(splits[22], 71), 0),
        "moment_qkv": bell_draw(splits[10], (D, 3 * D), (0.1 * 0.5 * TOKENS ** 0.5), 112.0, ((0, 32),), jnp.float32),
        "moment_attn_out": bell_draw(splits[11], (D, D), (0.1 * 0.35 * TOKENS ** 0.5), 80.0, ((0, 32),), jnp.float32),
        "moment_sort": bell_draw(splits[12], (D, 2 * SORT), (0.1 * 0.2 * TOKENS ** 0.5), 40.0, ((0, 32),), jnp.float32),
        "moment_ffn_in": bell_draw(splits[13], (D, FF), (0.1 * 0.3 * TOKENS ** 0.5), 64.0, ((0, 32),), jnp.float32),
        "moment_ffn_out": bell_draw(splits[14], (FF, D), (0.1 * 0.5 * TOKENS ** 0.5), 112.0, ((0, 32),), jnp.float32),
        "moment_norms": bell_draw(splits[15], (D, 4), (0.1 * TOKENS ** 0.5), 224.0, ((0, 32),), jnp.float32),
        "square_qkv": jnp.clip(jnp.exp(math.log(131.072) - 1.3862944 * jax.random.uniform(splits[16], (D, 3 * D), jnp.float32) ** shard_levels(splits[16], (D, 3 * D), ((0, 32),), -0.2, 0.2)), 32.768, 131.072),
        "square_attn_out": jnp.clip(jnp.exp(math.log(62.91456) - 1.3862944 * jax.random.uniform(splits[17], (D, D), jnp.float32) ** shard_levels(splits[17], (D, D), ((0, 32),), -0.2, 0.2)), 15.72864, 62.91456),
        "square_sort": jnp.clip(jnp.exp(math.log(20.97152) - 1.3862944 * jax.random.uniform(splits[18], (D, 2 * SORT), jnp.float32) ** shard_levels(splits[18], (D, 2 * SORT), ((0, 32),), -0.2, 0.2)), 5.24288, 20.97152),
        "square_ffn_in": jnp.clip(jnp.exp(math.log(47.18592) - 1.3862944 * jax.random.uniform(splits[19], (D, FF), jnp.float32) ** shard_levels(splits[19], (D, FF), ((0, 32),), -0.2, 0.2)), 11.79648, 47.18592),
        "square_ffn_out": jnp.clip(jnp.exp(math.log(131.072) - 1.3862944 * jax.random.uniform(splits[20], (FF, D), jnp.float32) ** shard_levels(splits[20], (FF, D), ((0, 32),), -0.2, 0.2)), 32.768, 131.072),
        "square_norms": jnp.clip(jnp.exp(math.log(524.288) - 1.3862944 * jax.random.uniform(splits[21], (D, 4), jnp.float32) ** shard_levels(splits[21], (D, 4), ((0, 32),), -0.2, 0.2)), 131.072, 524.288),
    }


@jax.custom_vjp
def low(v):
    return lax.optimization_barrier(v.astype(jnp.bfloat16)).astype(jnp.float32)

@jax.custom_vjp
def low_back(v):
    return v

def low_keep(v):
    return (low(v), None)

def low_pass(kept, grad):
    return (grad,)

def back_keep(v):
    return (v, None)

def back_low(kept, grad):
    return (low(grad),)
low.defvjp(low_keep, low_pass)
low_back.defvjp(back_keep, back_low)
highest = lax.Precision.HIGHEST
masked = -1000000000.0
norm_eps = 1e-05
beta_one = 0.9
beta_two = 0.999
adam_eps = 1e-08
decay = 0.01
rates = (0.05, 0.15, 0.05, 0.05, 0.025, 0.5)

def matmul(left, right):
    return jnp.dot(left, right, precision=highest, preferred_element_type=jnp.float32)

def layer_norm(value, gain, shift):
    center = value - lax.optimization_barrier(jnp.mean(value, axis=-1, keepdims=True))
    spread = lax.optimization_barrier(jnp.mean(center * center, axis=-1, keepdims=True))
    return center * lax.rsqrt(spread + norm_eps) * gain + shift

def slot_layout(lengths, slot):
    quarter = slot // 4
    places = jnp.arange(slot, dtype=jnp.int32)
    is_long = lengths[0] > quarter
    member = jnp.where(is_long, 0, places // quarter).astype(jnp.int32)
    offset = jnp.where(is_long, places, places % quarter).astype(jnp.int32)
    choose = (member[:, None] == jnp.arange(4, dtype=jnp.int32)[None, :]).astype(jnp.int32)
    limit = lax.optimization_barrier(jnp.sum(choose * lengths[None, :], axis=1))
    live = offset < limit
    blocks = slot // BLOCK
    group = jnp.where(live[::BLOCK], member[::BLOCK], 4 + jnp.arange(blocks, dtype=jnp.int32))
    return (live.astype(jnp.float32), group.astype(jnp.int32))

def sorted_attention(query, key, value, normed, sort_w, live, group, partner):
    slot, width = query.shape
    blocks = slot // BLOCK
    counts = lax.optimization_barrier(jnp.sum(live.reshape(blocks, BLOCK), axis=1))
    summary = lax.optimization_barrier(jnp.sum((normed * live[:, None]).reshape(blocks, BLOCK, width), axis=1))
    summary = summary * lax.rsqrt(jnp.maximum(counts, 1.0))[:, None]
    sort_q = matmul(summary, sort_w[:, :SORT])
    sort_k = matmul(summary, sort_w[:, SORT:])
    same = group[:, None] == group[None, :]
    raw = lax.dot_general(sort_q, sort_k, (((1,), (1,)), ((), ())), precision=highest, preferred_element_type=jnp.float32)
    logits = jnp.where(same, raw / math.sqrt(SORT), masked)
    for turn in range(SINK):
        logits = logits - jax.nn.logsumexp(logits, axis=1, keepdims=True)
        logits = logits - jax.nn.logsumexp(logits, axis=0, keepdims=True)
    members = lax.optimization_barrier(jnp.sum(same.astype(jnp.float32), axis=1))
    pick = partner[:, None] == jnp.arange(blocks, dtype=jnp.int32)[None, :]
    bias = lax.optimization_barrier(jnp.sum(jnp.where(pick, logits, 0.0), axis=1)) + jnp.log(members)
    shaped = (blocks, BLOCK, HEADS, HEAD)
    q_blocks = query.reshape(shaped)
    k_blocks = key.reshape(shaped)
    v_blocks = value.reshape(shaped)
    k_far = jnp.take(k_blocks, partner, axis=0)
    v_far = jnp.take(v_blocks, partner, axis=0)
    live_own = live.reshape(blocks, BLOCK)
    live_far = jnp.take(live_own, partner, axis=0)
    scale = 1.0 / math.sqrt(HEAD)
    own = jnp.einsum('bqhd,bkhd->bhqk', q_blocks, k_blocks, precision=highest) * scale
    far = jnp.einsum('bqhd,bkhd->bhqk', q_blocks, k_far, precision=highest) * scale + bias[:, None, None, None]
    diagonal = jnp.eye(BLOCK, dtype=bool)
    own = jnp.where((live_own[:, None, None, :] > 0.5) | diagonal[None, None], own, masked)
    far = jnp.where(live_far[:, None, None, :] > 0.5, far, masked)
    scores = jnp.concatenate([own, far], axis=3)
    top = lax.optimization_barrier(jnp.max(scores, axis=3, keepdims=True))
    expo = jnp.exp(scores - top)
    probs = expo / lax.optimization_barrier(jnp.sum(expo, axis=3, keepdims=True))
    mixed = jnp.einsum('bhqk,bkhd->bqhd', probs[..., :BLOCK], v_blocks, precision=highest)
    mixed = mixed + jnp.einsum('bhqk,bkhd->bqhd', probs[..., BLOCK:], v_far, precision=highest)
    return mixed.reshape(slot, width)

def slot_forward(used, x_slot, lengths, partner):
    w_qkv, w_attn_out, w_sort, w_ffn_in, w_ffn_out, norms = used
    width = x_slot.shape[1]
    live, group = slot_layout(lengths, x_slot.shape[0])
    h_one = low(layer_norm(x_slot, norms[:, 0], norms[:, 1]))
    qkv = low_back(low(matmul(h_one, w_qkv)))
    attended = low(sorted_attention(qkv[:, :width], qkv[:, width:2 * width], qkv[:, 2 * width:], h_one, w_sort, live, group, partner))
    x_one = x_slot + low_back(matmul(attended, w_attn_out))
    h_two = low(layer_norm(x_one, norms[:, 2], norms[:, 3]))
    act = low_back(matmul(h_two, w_ffn_in))
    hidden = low(jax.nn.gelu(act, approximate=True))
    return x_one + matmul(hidden, w_ffn_out)

def adamw(weight, grad, moment, square, rate):
    moment = beta_one * moment + (1.0 - beta_one) * grad
    square = beta_two * square + (1.0 - beta_two) * grad * grad
    m_hat = moment / (1.0 - beta_one ** STEP)
    s_hat = square / (1.0 - beta_two ** STEP)
    weight = weight - rate * (m_hat / (jnp.sqrt(s_hat) + adam_eps) + decay * weight)
    return (weight, moment, square)

def reference(x_in, grad_out, seq_lengths, partners, w_qkv, w_attn_out, w_sort, w_ffn_in, w_ffn_out, norm_params, moment_qkv, moment_attn_out, moment_sort, moment_ffn_in, moment_ffn_out, moment_norms, square_qkv, square_attn_out, square_sort, square_ffn_in, square_ffn_out, square_norms):
    masters = (w_qkv, w_attn_out, w_sort, w_ffn_in, w_ffn_out, norm_params)
    x_rows = x_in.astype(jnp.float32).reshape(SLOTS, TOK_DEV, D)
    cot_rows = grad_out.astype(jnp.float32).reshape(SLOTS, TOK_DEV, D)

    def forward(params, inputs):
        used = tuple((low(p) for p in params))

        def one_row(item):
            x_slot, lengths, partner = item
            return slot_forward(used, x_slot, lengths, partner)
        return lax.map(jax.checkpoint(one_row), (inputs, seq_lengths, partners))
    result, pullback = jax.vjp(forward, masters, x_rows)
    grads, d_rows = pullback(cot_rows)
    out_block = result.reshape(TOKENS, D).astype(jnp.bfloat16)
    grad_in = d_rows.reshape(TOKENS, D)
    moments = (moment_qkv, moment_attn_out, moment_sort, moment_ffn_in, moment_ffn_out, moment_norms)
    squares = (square_qkv, square_attn_out, square_sort, square_ffn_in, square_ffn_out, square_norms)
    new = [adamw(masters[i], grads[i], moments[i], squares[i], rates[i]) for i in range(6)]
    return (out_block, grad_in, new[0][0], new[0][1], new[0][2], new[1][0], new[1][1], new[1][2], new[2][0], new[2][1], new[2][2], new[3][0], new[3][1], new[3][2], new[4][0], new[4][1], new[4][2], new[5][0], new[5][1], new[5][2])
```

```python
import functools
import math

import jax
import jax.numpy as jnp
from jax import lax
from jax.experimental import pallas as pl
from jax.experimental.pallas import tpu as pltpu
from jax.sharding import PartitionSpec as P

HEADS = 8
HEAD = 64
SORT = 64
BLOCK = 32
SINK = 8
STEP = 10
TILE = 512
CHUNK = 512
GROUP = 128
LANES = 128

highest = lax.Precision.HIGHEST
masked = -1000000000.0
norm_eps = 1e-05
beta_one = 0.9
beta_two = 0.999
adam_eps = 1e-08
decay = 0.01
rates = (0.05, 0.15, 0.05, 0.05, 0.025, 0.5)
f32 = jnp.float32
bf16 = jnp.bfloat16


def dot(left, right, precision=None):
    return jnp.dot(left, right, precision=precision, preferred_element_type=f32)


def dot_nt(left, right, precision=None):
    return lax.dot_general(
        left, right, (((1,), (1,)), ((), ())), precision=precision, preferred_element_type=f32
    )


def dot_tn(left, right, precision=None):
    return lax.dot_general(
        left, right, (((0,), (0,)), ((), ())), precision=precision, preferred_element_type=f32
    )


def iota(shape, axis):
    return lax.broadcasted_iota(jnp.int32, shape, axis)


def ends_of(lens, slot):
    quarter = slot // 4
    is_long = lens[0, 0] > quarter
    return [jnp.where(is_long, lens[0, 0], k * quarter + lens[0, k]) for k in range(4)]


def end_at(places, ends, slot):
    quarter = slot // 4
    return jnp.where(
        places < 2 * quarter,
        jnp.where(places < quarter, ends[0], ends[1]),
        jnp.where(places < 3 * quarter, ends[2], ends[3]),
    )


def norm_stats(value):
    center = value - jnp.mean(value, axis=-1, keepdims=True)
    spread = jnp.mean(center * center, axis=-1, keepdims=True)
    rstd = lax.rsqrt(spread + norm_eps)
    return center * rstd, rstd


def norm_back(grad, hat, rstd, gain):
    d_hat = grad * gain
    mean_d = jnp.mean(d_hat, axis=-1, keepdims=True)
    mean_dh = jnp.mean(d_hat * hat, axis=-1, keepdims=True)
    return rstd * (d_hat - mean_d - hat * mean_dh)


def params(limit=56 << 20):
    return pltpu.CompilerParams(vmem_limit_bytes=limit)


def whole(shape):
    return pl.BlockSpec(shape, lambda *_: (0,) * len(shape))


def smem():
    return pl.BlockSpec(memory_space=pltpu.SMEM)


def project_kernel(lens, x_ref, wq_ref, wk_ref, wv_ref, q_ref, k_ref, v_ref, u_ref, norms_ref, *, slot):
    tile, width = x_ref.shape
    base = pl.program_id(0) * tile

    @pl.when(pl.program_id(0) == 0)
    def _():
        norms_ref[...] = wq_ref[:, width + LANES :].astype(f32).T[:8, :]

    hat, _ = norm_stats(x_ref[...].astype(f32))
    h_one = (hat * norms_ref[0:1, :] + norms_ref[1:2, :]).astype(bf16)
    q_ref[...] = dot(h_one, wq_ref[:, :width]).astype(bf16)
    k_ref[...] = dot(h_one, wk_ref[...]).astype(bf16)
    v_ref[...] = dot(h_one, wv_ref[...]).astype(bf16)
    blocks = tile // BLOCK
    at = iota((blocks, tile), 1)
    places = at + base
    live = places < end_at(places, ends_of(lens, slot), slot)
    own = (at // BLOCK) == iota((blocks, tile), 0)
    pick = jnp.where(live & own, 1.0, 0.0).astype(bf16)
    u_ref[...] = dot(pick, h_one)


def project(lens, x, w_q, w_k, w_v):
    slot, width = x.shape
    grid = slot // TILE
    row = pl.BlockSpec((TILE, width), lambda i: (i, 0))
    out = jax.ShapeDtypeStruct((slot, width), bf16)
    return pl.pallas_call(
        functools.partial(project_kernel, slot=slot),
        grid=(grid,),
        in_specs=[smem(), row, whole(w_q.shape), whole(w_k.shape), whole(w_v.shape)],
        out_specs=[
            row,
            row,
            row,
            pl.BlockSpec((TILE // BLOCK, width), lambda i: (i, 0)),
            whole((8, width)),
        ],
        out_shape=[
            out,
            out,
            out,
            jax.ShapeDtypeStruct((slot // BLOCK, width), f32),
            jax.ShapeDtypeStruct((8, width), f32),
        ],
        compiler_params=params(),
        cost_estimate=pl.CostEstimate(
            flops=2 * slot * width * 3 * width, bytes_accessed=slot * width * 8, transcendentals=0
        ),
        name="project",
    )(lens, x, w_q, w_k, w_v)


def sort_parts(lens, u_ref, ws_ref, slot):
    blocks = u_ref.shape[0]
    ends = ends_of(lens, slot)
    quarter = slot // 4
    is_long = lens[0, 0] > quarter

    def group_of(axis, shape):
        index = iota(shape, axis)
        start = index * BLOCK
        live = start < end_at(start, ends, slot)
        member = jnp.where(is_long, 0, start // quarter)
        return jnp.where(live, member, 4 + index)

    same = group_of(0, (blocks, blocks)) == group_of(1, (blocks, blocks))
    start = iota((blocks, 1), 0) * BLOCK
    count = jnp.clip(end_at(start, ends, slot) - start, 0, BLOCK).astype(f32)
    scale = lax.rsqrt(jnp.maximum(count, 1.0))
    summary = u_ref[...] * scale
    w_sort = ws_ref[...].astype(f32)
    sort_q = dot(summary, w_sort[:, :SORT], highest)
    sort_k = dot(summary, w_sort[:, SORT:], highest)
    return same, scale, summary, w_sort, sort_q, sort_k


def sort_columns(w_q):
    return pl.BlockSpec((w_q.shape[0], 2 * SORT), lambda i: (0, w_q.shape[0] // (2 * SORT)))


def column_of(row, eye):
    return jnp.sum(jnp.where(eye, row, 0.0), axis=1, keepdims=True)


def sort_kernel(lens, u_ref, ws_ref, partner_ref, bias_ref, steps_ref, *, slot):
    blocks = u_ref.shape[0]
    same, _, _, _, sort_q, sort_k = sort_parts(lens, u_ref, ws_ref, slot)
    raw = dot_nt(sort_q, sort_k, highest)
    logits = jnp.where(same, raw / math.sqrt(SORT), masked)

    def normalize(value, axis):
        top = jnp.max(value, axis=axis, keepdims=True)
        return value - (top + jnp.log(jnp.sum(jnp.exp(value - top), axis=axis, keepdims=True)))

    for turn in range(SINK):
        logits = normalize(logits, 1)
        steps_ref[2 * turn] = logits
        logits = normalize(logits, 0)
        steps_ref[2 * turn + 1] = logits
    eye = iota((blocks, blocks), 0) == iota((blocks, blocks), 1)
    members = jnp.sum(same.astype(f32), axis=1, keepdims=True)
    partner = column_of(partner_ref[...].astype(f32), eye)
    pick = partner == iota((blocks, blocks), 1).astype(f32)
    bias = jnp.sum(jnp.where(pick, logits, 0.0), axis=1, keepdims=True) + jnp.log(members)
    bias_ref[...] = jnp.sum(jnp.where(eye, bias, 0.0), axis=0, keepdims=True)


def sort_net(lens, u, w_sort, partner, slot):
    blocks = u.shape[0]
    return pl.pallas_call(
        functools.partial(sort_kernel, slot=slot),
        in_specs=[smem(), whole(u.shape), sort_columns(w_sort), whole(partner.shape)],
        out_specs=[whole((1, blocks)), whole((2 * SINK, blocks, blocks))],
        out_shape=[
            jax.ShapeDtypeStruct((1, blocks), f32),
            jax.ShapeDtypeStruct((2 * SINK, blocks, blocks), f32),
        ],
        grid=(1,),
        compiler_params=params(),
        cost_estimate=pl.CostEstimate(flops=10**8, bytes_accessed=10**7, transcendentals=10**6),
        name="sort_net",
    )(lens, u, w_sort, partner)


def sort_back_kernel(
    lens, u_ref, ws_ref, partner_ref, d_bias_ref, steps_ref, d_u_ref, grad_ref, *, slot
):
    blocks = u_ref.shape[0]
    same, scale, summary, w_sort, sort_q, sort_k = sort_parts(lens, u_ref, ws_ref, slot)
    eye = iota((blocks, blocks), 0) == iota((blocks, blocks), 1)
    partner = column_of(partner_ref[...].astype(f32), eye)
    pick = partner == iota((blocks, blocks), 1).astype(f32)
    d_bias = column_of(d_bias_ref[...], eye)
    d_logits = jnp.where(pick, d_bias, 0.0)
    for turn in reversed(range(SINK)):
        for axis, step in ((0, 2 * turn + 1), (1, 2 * turn)):
            share = jnp.exp(steps_ref[step])
            d_logits = d_logits - share * jnp.sum(d_logits, axis=axis, keepdims=True)
    d_raw = jnp.where(same, d_logits, 0.0) / math.sqrt(SORT)
    d_sort_q = dot(d_raw, sort_k, highest)
    d_sort_k = dot_tn(d_raw, sort_q, highest)
    d_sort = jnp.concatenate([d_sort_q, d_sort_k], axis=1)
    grad_ref[...] = dot_tn(summary, d_sort, highest)
    d_u_ref[...] = dot_nt(d_sort, w_sort, highest) * scale


def sort_back(lens, u, w_sort, partner, d_bias, steps, slot):
    blocks, width = u.shape
    return pl.pallas_call(
        functools.partial(sort_back_kernel, slot=slot),
        in_specs=[
            smem(),
            whole(u.shape),
            sort_columns(w_sort),
            whole(partner.shape),
            whole(d_bias.shape),
            whole(steps.shape),
        ],
        out_specs=[whole((blocks, width)), whole((width, 2 * SORT))],
        out_shape=[
            jax.ShapeDtypeStruct((blocks, width), f32),
            jax.ShapeDtypeStruct((width, 2 * SORT), f32),
        ],
        grid=(1,),
        compiler_params=params(),
        cost_estimate=pl.CostEstimate(flops=10**8, bytes_accessed=10**7, transcendentals=10**6),
        name="sort_back",
    )(lens, u, w_sort, partner, d_bias, steps)


def lane_block(rows):
    return (iota((rows, 2 * GROUP), 1) % GROUP) // BLOCK


def compact(full):
    at = lane_block(BLOCK)
    part = [full[c * BLOCK : (c + 1) * BLOCK] for c in range(GROUP // BLOCK)]
    return jnp.where(
        at < 2,
        jnp.where(at < 1, part[0], part[1]),
        jnp.where(at < 3, part[2], part[3]),
    )


def diagonal_mask():
    rows = 2 * GROUP
    return jnp.where((iota((rows, rows), 0) % GROUP) // BLOCK == lane_block(rows), 1.0, 0.0).astype(bf16)


def spread(own, far, mask):
    own, far = own.astype(bf16), far.astype(bf16)
    times = GROUP // BLOCK
    return jnp.concatenate([own] * times + [far] * times, axis=0) * mask


def head_stack(pair, lanes):
    zero = jnp.zeros_like(pair)
    return jnp.concatenate(
        [jnp.where(lanes < HEAD, pair, zero), jnp.where(lanes < HEAD, zero, pair)], axis=0
    )


def head_lanes():
    return iota((GROUP, LANES), 1)


def by_lane(values):
    at = iota((1, GROUP), 1) // BLOCK
    return jnp.where(
        at < 2,
        jnp.where(at < 1, values[0], values[1]),
        jnp.where(at < 3, values[2], values[3]),
    )


def gather_far(dst, src, partners):
    for c, p in enumerate(partners):
        dst[GROUP + c * BLOCK : GROUP + (c + 1) * BLOCK, :] = src[pl.ds(pl.multiple_of(p * BLOCK, BLOCK), BLOCK), :]


def attend_kernel(
    lens, partner, bias, q_ref, k_ref, v_ref, o_ref, p_ref, k_cat, v_cat, mask_ref, *, slot
):
    tile, width = q_ref.shape
    step = pl.program_id(0)
    pairs = width // LANES
    per = GROUP // BLOCK

    @pl.when(step == 0)
    def _():
        mask_ref[...] = diagonal_mask()

    ends = ends_of(lens, slot)
    scale = 1.0 / math.sqrt(HEAD)

    def one_group(g, carry):
        first = step * (tile // BLOCK) + g * per
        partners = [partner[0, first + c] for c in range(per)]
        rows = pl.ds(pl.multiple_of(first * BLOCK, GROUP), GROUP)
        k_cat[0:GROUP, :] = k_ref[rows, :]
        v_cat[0:GROUP, :] = v_ref[rows, :]
        gather_far(k_cat, k_ref, partners)
        gather_far(v_cat, v_ref, partners)
        key = iota((BLOCK, GROUP), 0)
        query = iota((BLOCK, GROUP), 1)
        own_place = (first + query // BLOCK) * BLOCK + key
        far_place = by_lane(partners) * BLOCK + key
        own_live = (own_place < end_at(own_place, ends, slot)) | (query % BLOCK == key)
        far_live = far_place < end_at(far_place, ends, slot)
        own_live = jnp.concatenate([own_live.astype(f32)] * 2, axis=1) > 0.5
        far_live = jnp.concatenate([far_live.astype(f32)] * 2, axis=1) > 0.5
        lane_bias = by_lane([bias[0, first + c] for c in range(per)])
        lane_bias = jnp.concatenate([lane_bias] * 2, axis=1)
        lanes = head_lanes()
        mask = mask_ref[...]
        q_rows = pl.ds(pl.multiple_of(g * GROUP, GROUP), GROUP)
        for pair in range(pairs):
            cols = slice(pair * LANES, (pair + 1) * LANES)
            q_two = head_stack(q_ref[q_rows, cols], lanes)
            scores = dot_nt(k_cat[:, cols], q_two)
            own = jnp.where(own_live, compact(scores[:GROUP]) * scale, masked)
            far = jnp.where(far_live, compact(scores[GROUP:]) * scale + lane_bias, masked)
            top = jnp.maximum(
                jnp.max(own, axis=0, keepdims=True), jnp.max(far, axis=0, keepdims=True)
            )
            own = jnp.exp(own - top)
            far = jnp.exp(far - top)
            total = jnp.sum(own, axis=0, keepdims=True) + jnp.sum(far, axis=0, keepdims=True)
            inverse = 1.0 / total
            own = own * inverse
            far = far * inverse
            at = pl.multiple_of((g * pairs + pair) * 2 * BLOCK, 2 * BLOCK)
            p_ref[pl.ds(at, BLOCK), :] = own.astype(bf16)
            p_ref[pl.ds(at + BLOCK, BLOCK), :] = far.astype(bf16)
            mixed = dot(v_cat[:, cols].T, spread(own, far, mask))
            o_ref[pair * LANES : pair * LANES + HEAD, q_rows] = mixed[:HEAD, :GROUP].astype(bf16)
            o_ref[pair * LANES + HEAD : (pair + 1) * LANES, q_rows] = mixed[HEAD:, GROUP:].astype(bf16)
        return carry

    lax.fori_loop(0, tile // GROUP, one_group, 0)


def attend(lens, partner, bias, q, k, v):
    slot, width = q.shape
    grid = slot // TILE
    per_tile = (TILE // GROUP) * (width // LANES) * 2 * BLOCK
    return pl.pallas_call(
        functools.partial(attend_kernel, slot=slot),
        grid=(grid,),
        in_specs=[
            smem(),
            smem(),
            smem(),
            pl.BlockSpec((TILE, width), lambda i: (i, 0)),
            whole(k.shape),
            whole(v.shape),
        ],
        out_specs=[
            pl.BlockSpec((width, TILE), lambda i: (0, i)),
            pl.BlockSpec((per_tile, 2 * GROUP), lambda i: (i, 0)),
        ],
        out_shape=[
            jax.ShapeDtypeStruct((width, slot), bf16),
            jax.ShapeDtypeStruct((grid * per_tile, 2 * GROUP), bf16),
        ],
        scratch_shapes=[
            pltpu.VMEM((2 * GROUP, width), bf16),
            pltpu.VMEM((2 * GROUP, width), bf16),
            pltpu.VMEM((2 * GROUP, 2 * GROUP), bf16),
        ],
        compiler_params=params(),
        cost_estimate=pl.CostEstimate(
            flops=20 * 10**9, bytes_accessed=slot * width * 10, transcendentals=slot * 512
        ),
        name="attend",
    )(lens, partner, bias, q, k, v)


def attend_back_kernel(
    partner, q_ref, do_ref, p_ref, k_ref, v_ref,
    dq_ref, dk_ref, dv_ref, db_ref,
    k_cat, v_cat, mask_ref, dk_sum, dv_sum, db_sum,
):
    tile, width = q_ref.shape
    step = pl.program_id(0)
    pairs = width // LANES
    per = GROUP // BLOCK

    @pl.when(step == 0)
    def _():
        mask_ref[...] = diagonal_mask()
        dk_sum[...] = jnp.zeros_like(dk_sum)
        dv_sum[...] = jnp.zeros_like(dv_sum)

    scale = 1.0 / math.sqrt(HEAD)

    def one_group(g, carry):
        first = step * (tile // BLOCK) + g * per
        partners = [partner[0, first + c] for c in range(per)]
        rows = pl.ds(pl.multiple_of(first * BLOCK, GROUP), GROUP)
        k_cat[0:GROUP, :] = k_ref[rows, :]
        v_cat[0:GROUP, :] = v_ref[rows, :]
        gather_far(k_cat, k_ref, partners)
        gather_far(v_cat, v_ref, partners)
        lanes = head_lanes()
        mask = mask_ref[...]
        q_rows = pl.ds(pl.multiple_of(g * GROUP, GROUP), GROUP)
        d_bias = jnp.zeros((1, 2 * GROUP), f32)
        for pair in range(pairs):
            cols = slice(pair * LANES, (pair + 1) * LANES)
            q_two = head_stack(q_ref[q_rows, cols], lanes)
            do_two = head_stack(do_ref[q_rows, cols], lanes)
            d_prob = dot_nt(v_cat[:, cols], do_two)
            at = pl.multiple_of((g * pairs + pair) * 2 * BLOCK, 2 * BLOCK)
            own_b = p_ref[pl.ds(at, BLOCK), :]
            far_b = p_ref[pl.ds(at + BLOCK, BLOCK), :]
            own, far = own_b.astype(f32), far_b.astype(f32)
            d_own, d_far = compact(d_prob[:GROUP]), compact(d_prob[GROUP:])
            delta = jnp.sum(own * d_own, axis=0, keepdims=True) + jnp.sum(
                far * d_far, axis=0, keepdims=True
            )
            d_own = own * (d_own - delta)
            d_far = far * (d_far - delta)
            d_bias = d_bias + jnp.sum(d_far, axis=0, keepdims=True)
            d_scores = spread(d_own * scale, d_far * scale, mask)
            dk = dot(d_scores, q_two)
            dv = dot(spread(own_b, far_b, mask), do_two)
            dq = dot(k_cat[:, cols].T, d_scores)
            dq = jnp.concatenate([dq[:HEAD, :GROUP], dq[HEAD:, GROUP:]], axis=0)
            dq_ref[q_rows, cols] = dq.T.astype(bf16)
            dk_sum[rows, cols] += dk[:GROUP]
            dv_sum[rows, cols] += dv[:GROUP]
            for c, p in enumerate(partners):
                there = pl.ds(pl.multiple_of(p * BLOCK, BLOCK), BLOCK)
                here = slice(GROUP + c * BLOCK, GROUP + (c + 1) * BLOCK)
                dk_sum[there, cols] += dk[here]
                dv_sum[there, cols] += dv[here]
        db_sum[pl.ds(step * (tile // GROUP) + g, 1), :] = d_bias[:, :GROUP] + d_bias[:, GROUP:]
        return carry

    lax.fori_loop(0, tile // GROUP, one_group, 0)

    @pl.when(step == pl.num_programs(0) - 1)
    def _():
        dk_ref[...] = dk_sum[...].astype(bf16)
        dv_ref[...] = dv_sum[...].astype(bf16)
        groups = db_sum.shape[0]
        blocks = groups * per
        pick = (iota((GROUP, blocks), 0) // BLOCK == iota((GROUP, blocks), 1) % per).astype(f32)
        sums = dot(db_sum[...], pick, highest)
        mine = iota((groups, blocks), 1) // per == iota((groups, blocks), 0)
        db_ref[...] = jnp.sum(jnp.where(mine, sums, 0.0), axis=0, keepdims=True)


def attend_back(partner, q, d_o, probs, k, v):
    slot, width = q.shape
    grid = slot // TILE
    per_tile = (TILE // GROUP) * (width // LANES) * 2 * BLOCK
    row = pl.BlockSpec((TILE, width), lambda i: (i, 0))
    once = pl.BlockSpec((slot, width), lambda i: (0, 0), pipeline_mode=pl.Buffered(1))
    out = jax.ShapeDtypeStruct((slot, width), bf16)
    return pl.pallas_call(
        attend_back_kernel,
        grid=(grid,),
        in_specs=[
            smem(),
            row,
            row,
            pl.BlockSpec((per_tile, 2 * GROUP), lambda i: (i, 0)),
            once,
            once,
        ],
        out_specs=[row, once, once, whole((1, slot // BLOCK))],
        out_shape=[out, out, out, jax.ShapeDtypeStruct((1, slot // BLOCK), f32)],
        scratch_shapes=[
            pltpu.VMEM((2 * GROUP, width), bf16),
            pltpu.VMEM((2 * GROUP, width), bf16),
            pltpu.VMEM((2 * GROUP, 2 * GROUP), bf16),
            pltpu.VMEM((slot, width), f32),
            pltpu.VMEM((slot, width), f32),
            pltpu.VMEM((slot // GROUP, GROUP), f32),
        ],
        compiler_params=params(),
        cost_estimate=pl.CostEstimate(
            flops=40 * 10**9, bytes_accessed=slot * width * 16, transcendentals=0
        ),
        name="attend_back",
    )(partner, q, d_o, probs, k, v)


def ffn_kernel(
    x_ref, dy_ref, o_ref, norms_ref, wo_ref, win_ref, wout_ref,
    out_ref, dx_ref, do_ref, g_attn_ref, g_in_ref, g_out_ref, g_norm_ref,
    h_scr, ht_scr, dyt_scr, y_scr, dh_scr, gt_scr,
):
    tile, width = x_ref.shape
    hidden = win_ref.shape[1]
    step = pl.program_id(0)

    @pl.when(step == 0)
    def _():
        g_attn_ref[...] = jnp.zeros_like(g_attn_ref)
        g_in_ref[...] = jnp.zeros_like(g_in_ref)
        gt_scr[...] = jnp.zeros_like(gt_scr)
        g_norm_ref[...] = jnp.zeros_like(g_norm_ref)

    o_t = o_ref[...]
    x_one = x_ref[...].astype(f32) + dot(o_t.T, wo_ref[...])
    hat, rstd = norm_stats(x_one)
    h_two = (hat * norms_ref[2:3, :] + norms_ref[3:4, :]).astype(bf16)
    h_scr[...] = h_two
    ht_scr[...] = h_two.T
    dyt_scr[...] = dy_ref[...].T
    y_scr[...] = x_one
    dh_scr[...] = jnp.zeros_like(dh_scr)
    root = math.sqrt(2.0 / math.pi)

    def one_chunk(c, carry):
        cols = pl.ds(pl.multiple_of(c * CHUNK, CHUNK), CHUNK)
        act = dot(h_scr[...], win_ref[:, cols])
        d_hid = dot_nt(dy_ref[...], wout_ref[cols, :])
        square = act * act
        curve = jnp.tanh(act * (root + (root * 0.044715) * square))
        gate = 0.5 + 0.5 * curve
        hid = act * gate
        hid_b = hid.astype(bf16)
        slope = gate + hid * (1.0 - curve) * (root + (3.0 * root * 0.044715) * square)
        d_act = (d_hid * slope).astype(bf16)
        y_scr[...] += dot(hid_b, wout_ref[cols, :])
        gt_scr[:, cols] += dot(dyt_scr[...], hid_b)
        g_in_ref[:, cols] += dot(ht_scr[...], d_act)
        dh_scr[...] += dot_nt(d_act, win_ref[:, cols])
        return carry

    lax.fori_loop(0, hidden // CHUNK, one_chunk, 0)
    out_ref[...] = y_scr[...].astype(bf16)
    d_h = dh_scr[...]
    g_norm_ref[2:3, :] += jnp.sum(d_h * hat, axis=0, keepdims=True)
    g_norm_ref[3:4, :] += jnp.sum(d_h, axis=0, keepdims=True)
    d_x = dy_ref[...].astype(f32) + norm_back(d_h, hat, rstd, norms_ref[2:3, :])
    dx_ref[...] = d_x
    d_z = d_x.astype(bf16)
    g_attn_ref[...] += dot(o_t, d_z)
    do_ref[...] = dot_nt(d_z, wo_ref[...]).astype(bf16)

    @pl.when(step == pl.num_programs(0) - 1)
    def _():
        g_out_ref[...] = gt_scr[...].T


def ffn(x, dy, o_t, norms, w_o, w_in, w_out):
    slot, width = x.shape
    hidden = w_in.shape[1]
    grid = slot // TILE
    row = pl.BlockSpec((TILE, width), lambda i: (i, 0))

    def once(shape):
        return pl.BlockSpec(shape, lambda i: (0, 0), pipeline_mode=pl.Buffered(1))

    return pl.pallas_call(
        ffn_kernel,
        grid=(grid,),
        in_specs=[
            row,
            row,
            pl.BlockSpec((width, TILE), lambda i: (0, i)),
            once(norms.shape),
            once(w_o.shape),
            once(w_in.shape),
            once(w_out.shape),
        ],
        out_specs=[
            row,
            row,
            row,
            once((width, width)),
            once((width, hidden)),
            once((hidden, width)),
            once((8, width)),
        ],
        out_shape=[
            jax.ShapeDtypeStruct((slot, width), bf16),
            jax.ShapeDtypeStruct((slot, width), f32),
            jax.ShapeDtypeStruct((slot, width), bf16),
            jax.ShapeDtypeStruct((width, width), f32),
            jax.ShapeDtypeStruct((width, hidden), f32),
            jax.ShapeDtypeStruct((hidden, width), f32),
            jax.ShapeDtypeStruct((8, width), f32),
        ],
        scratch_shapes=[
            pltpu.VMEM((TILE, width), bf16),
            pltpu.VMEM((width, TILE), bf16),
            pltpu.VMEM((width, TILE), bf16),
            pltpu.VMEM((TILE, width), f32),
            pltpu.VMEM((TILE, width), f32),
            pltpu.VMEM((width, hidden), f32),
        ],
        compiler_params=params(),
        cost_estimate=pl.CostEstimate(
            flops=2 * slot * width * (3 * width + 6 * hidden),
            bytes_accessed=slot * width * 14,
            transcendentals=slot * hidden,
        ),
        name="ffn",
    )(x, dy, o_t, norms, w_o, w_in, w_out)


def project_back_kernel(
    lens, x_ref, dx_ref, dq_ref, dk_ref, dv_ref, du_ref, norms_ref, wq_ref, wk_ref, wv_ref,
    g_sort_ref, g_two_ref, grad_ref, gq_ref, gk_ref, gv_ref, g_norm_ref, *, slot,
):
    tile, width = x_ref.shape
    step = pl.program_id(0)

    @pl.when(step == 0)
    def _():
        gq_ref[...] = jnp.zeros_like(gq_ref)
        gk_ref[...] = jnp.zeros_like(gk_ref)
        gv_ref[...] = jnp.zeros_like(gv_ref)
        g_norm_ref[...] = jnp.zeros_like(g_norm_ref)

    hat, rstd = norm_stats(x_ref[...].astype(f32))
    h_t = (hat * norms_ref[0:1, :] + norms_ref[1:2, :]).astype(bf16).T
    blocks = tile // BLOCK
    places = step * tile + iota((tile, 1), 0)
    live = places < end_at(places, ends_of(lens, slot), slot)
    d_h = jnp.broadcast_to(du_ref[...].reshape(blocks, 1, width), (blocks, BLOCK, width))
    d_h = jnp.where(live, d_h.reshape(tile, width), 0.0)
    for ref, w_ref, g_ref in (
        (dq_ref, wq_ref, gq_ref),
        (dk_ref, wk_ref, gk_ref),
        (dv_ref, wv_ref, gv_ref),
    ):
        d_part = ref[...]
        d_h = d_h + dot_nt(d_part, w_ref[:, :width])
        g_ref[:, :width] += dot(h_t, d_part)
    g_norm_ref[0:1, :] += jnp.sum(d_h * hat, axis=0, keepdims=True)
    g_norm_ref[1:2, :] += jnp.sum(d_h, axis=0, keepdims=True)
    grad_ref[...] = dx_ref[...] + norm_back(d_h, hat, rstd, norms_ref[0:1, :])

    @pl.when(step == pl.num_programs(0) - 1)
    def _():
        gq_ref[:, width : width + LANES] = g_sort_ref[...]
        small = g_norm_ref[...] + g_two_ref[...]
        rest = jnp.zeros((LANES - small.shape[0], width), f32)
        gq_ref[:, width + LANES :] = jnp.concatenate([small, rest], axis=0).T


def project_back(lens, x, d_x, d_q, d_k, d_v, d_u, norms, w_q, w_k, w_v, g_sort, g_two):
    slot, width = x.shape
    grid = slot // TILE
    row = pl.BlockSpec((TILE, width), lambda i: (i, 0))

    def once(shape):
        return pl.BlockSpec(shape, lambda i: (0, 0), pipeline_mode=pl.Buffered(1))

    return pl.pallas_call(
        functools.partial(project_back_kernel, slot=slot),
        grid=(grid,),
        in_specs=[
            smem(), row, row, row, row, row,
            pl.BlockSpec((TILE // BLOCK, width), lambda i: (i, 0)),
            once(norms.shape),
            once(w_q.shape),
            once(w_k.shape),
            once(w_v.shape),
            once(g_sort.shape),
            once(g_two.shape),
        ],
        out_specs=[row, once(w_q.shape), once(w_k.shape), once(w_v.shape)],
        out_shape=[
            jax.ShapeDtypeStruct((slot, width), f32),
            jax.ShapeDtypeStruct(w_q.shape, f32),
            jax.ShapeDtypeStruct(w_k.shape, f32),
            jax.ShapeDtypeStruct(w_v.shape, f32),
        ],
        scratch_shapes=[pltpu.VMEM((8, width), f32)],
        compiler_params=params(),
        cost_estimate=pl.CostEstimate(
            flops=2 * slot * width * 6 * width, bytes_accessed=slot * width * 18, transcendentals=0
        ),
        name="project_back",
    )(lens, x, d_x, d_q, d_k, d_v, d_u, norms, w_q, w_k, w_v, g_sort, g_two)


def orders(count):
    bits = list(range(1, count))
    third = max(len(bits) // 4, 1)
    turns = (0, third, 2 * third)
    return [[0] + bits[t:] + bits[:t] for t in turns]


def gather(block, order, size):
    count = size.bit_length() - 1
    place = lax.axis_index("dp")
    held = block.reshape((1,) * count + block.shape)
    for bit in reversed(order):
        axis = count - 1 - bit
        came = lax.ppermute(held, "dp", [(i, i ^ (1 << bit)) for i in range(size)])
        upper = ((place >> bit) & 1) == 1
        held = jnp.concatenate(
            [jnp.where(upper, came, held), jnp.where(upper, held, came)], axis=axis
        )
    return held.reshape((size * block.shape[0],) + block.shape[1:])


def scatter_sum(value, order, size):
    count = size.bit_length() - 1
    place = lax.axis_index("dp")
    rows = value.shape[0] // size
    held = value.reshape((2,) * count + (rows,) + value.shape[1:])
    for bit in order:
        axis = count - 1 - bit
        mine = (place >> bit) & 1
        sent = lax.dynamic_index_in_dim(held, 1 - mine, axis, keepdims=True).astype(bf16)
        kept = lax.dynamic_index_in_dim(held, mine, axis, keepdims=True)
        came = lax.ppermute(sent, "dp", [(i, i ^ (1 << bit)) for i in range(size)])
        held = kept + came.astype(f32)
    return held.reshape((rows,) + value.shape[1:])


def adamw(weight, grad, moment, square, rate):
    moment = beta_one * moment + (1.0 - beta_one) * grad
    square = beta_two * square + (1.0 - beta_two) * grad * grad
    m_hat = moment / (1.0 - beta_one**STEP)
    s_hat = square / (1.0 - beta_two**STEP)
    weight = weight - rate * (m_hat / (jnp.sqrt(s_hat) + adam_eps) + decay * weight)
    return (weight, moment, square)


def body(size, x, dy, lens, partner, *state):
    slot, width = x.shape
    masters, moments, squares = state[:6], state[6:12], state[12:]
    low = [m.astype(bf16) for m in masters]
    first, second, third = orders(size.bit_length() - 1)
    norm_cols = low[5].shape[1]
    ext = jnp.concatenate(
        [low[0][:, :width], low[2], jnp.pad(low[5], ((0, 0), (0, LANES - norm_cols)))], axis=1
    )
    w_q = gather(ext, first, size)
    w_k = gather(low[0][:, width : 2 * width], second, size)
    w_v = gather(low[0][:, 2 * width :], third, size)
    w_o = gather(low[1], third, size)
    w_in = gather(low[3], first, size)
    w_out = gather(low[4], second, size)

    q, k, v, u, norms = project(lens, x, w_q, w_k, w_v)
    bias, steps = sort_net(lens, u, w_q, partner, slot)
    o_t, probs = attend(lens, partner, bias, q, k, v)
    out, d_x, d_o, g_attn, g_in, g_out, g_two = ffn(x, dy, o_t, norms, w_o, w_in, w_out)
    s_out = scatter_sum(g_out, first, size)
    s_in = scatter_sum(g_in, second, size)
    s_attn = scatter_sum(g_attn, third, size)
    d_q, d_k, d_v, d_bias = attend_back(partner, q, d_o, probs, k, v)
    d_u, g_sort = sort_back(lens, u, w_q, partner, d_bias, steps, slot)
    grad_in, g_q, g_k, g_v = project_back(
        lens, x, d_x, d_q, d_k, d_v, d_u, norms, w_q, w_k, w_v, g_sort, g_two
    )
    s_q = scatter_sum(g_q, first, size)
    s_k = scatter_sum(g_k, second, size)
    s_v = scatter_sum(g_v, third, size)
    grads = (
        jnp.concatenate([s_q[:, :width], s_k, s_v], axis=1),
        s_attn,
        s_q[:, width : width + LANES],
        s_in,
        s_out,
        s_q[:, width + LANES : width + LANES + norm_cols],
    )
    result = [out, grad_in]
    for i in range(6):
        result.extend(adamw(masters[i], grads[i], moments[i], squares[i], rates[i]))
    return tuple(result)


def solution(mesh):
    spec = P("dp", None)
    return jax.shard_map(
        functools.partial(body, mesh.shape["dp"]),
        mesh=mesh,
        in_specs=(spec,) * 22,
        out_specs=(spec,) * 20,
        check_vma=False,
    )
```

```python
import functools
import math

import jax
import jax.numpy as jnp
from jax import lax
from jax.experimental import pallas as pl
from jax.experimental.pallas import tpu as pltpu
from jax.sharding import PartitionSpec as P

HEADS = 8
HEAD = 64
SORT = 64
BLOCK = 32
SINK = 8
STEP = 10
TILE = 512
WIDE = 1024
ROWS = 16
ABREAST = 4
SUB = 256
GROUP = 128
LANES = 128

highest = lax.Precision.HIGHEST
masked = -1000000000.0
norm_eps = 1e-05
beta_one = 0.9
beta_two = 0.999
adam_eps = 1e-08
decay = 0.01
rates = (0.05, 0.15, 0.05, 0.05, 0.025, 0.5)
f32 = jnp.float32
bf16 = jnp.bfloat16


def dot(left, right, precision=None):
    return jnp.dot(left, right, precision=precision, preferred_element_type=f32)


def dot_nt(left, right, precision=None):
    return lax.dot_general(
        left, right, (((1,), (1,)), ((), ())), precision=precision, preferred_element_type=f32
    )


def dot_tn(left, right, precision=None):
    return lax.dot_general(
        left, right, (((0,), (0,)), ((), ())), precision=precision, preferred_element_type=f32
    )


def iota(shape, axis):
    return lax.broadcasted_iota(jnp.int32, shape, axis)


def ends_of(lens, slot):
    quarter = slot // 4
    is_long = lens[0, 0] > quarter
    return [jnp.where(is_long, lens[0, 0], k * quarter + lens[0, k]) for k in range(4)]


def end_at(places, ends, slot):
    quarter = slot // 4
    return jnp.where(
        places < 2 * quarter,
        jnp.where(places < quarter, ends[0], ends[1]),
        jnp.where(places < 3 * quarter, ends[2], ends[3]),
    )


def norm_stats(value):
    center = value - jnp.mean(value, axis=-1, keepdims=True)
    spread = jnp.mean(center * center, axis=-1, keepdims=True)
    rstd = lax.rsqrt(spread + norm_eps)
    return center * rstd, rstd


def norm_back(grad, hat, rstd, gain):
    d_hat = grad * gain
    mean_d = jnp.mean(d_hat, axis=-1, keepdims=True)
    mean_dh = jnp.mean(d_hat * hat, axis=-1, keepdims=True)
    return rstd * (d_hat - mean_d - hat * mean_dh)


def params(limit=56 << 20):
    return pltpu.CompilerParams(vmem_limit_bytes=limit)


def whole(shape):
    return pl.BlockSpec(shape, lambda *_: (0,) * len(shape))


def smem():
    return pl.BlockSpec(memory_space=pltpu.SMEM)


def project_kernel(lens, x_ref, w_ref, q_ref, k_ref, v_ref, u_ref, norms_ref, *, slot):
    tile, width = x_ref.shape
    base = pl.program_id(0) * tile

    @pl.when(pl.program_id(0) == 0)
    def _():
        norms_ref[...] = w_ref[:, 3 * width + LANES :].astype(f32).T[:8, :]

    parts = []
    for r in range(0, tile, SUB):
        hat, _ = norm_stats(x_ref[r : r + SUB, :].astype(f32))
        parts.append((hat * norms_ref[0:1, :] + norms_ref[1:2, :]).astype(bf16))
        for part, ref in enumerate((q_ref, k_ref, v_ref)):
            ref[r : r + SUB, :] = dot(parts[-1], w_ref[:, part * width : (part + 1) * width]).astype(bf16)
    h_one = jnp.concatenate(parts, axis=0)
    blocks = tile // BLOCK
    at = iota((blocks, tile), 1)
    places = at + base
    live = places < end_at(places, ends_of(lens, slot), slot)
    own = (at // BLOCK) == iota((blocks, tile), 0)
    pick = jnp.where(live & own, 1.0, 0.0).astype(bf16)
    u_ref[...] = dot(pick, h_one)


def project(lens, x, w_one):
    slot, width = x.shape
    grid = slot // WIDE
    row = pl.BlockSpec((WIDE, width), lambda i: (i, 0))
    out = jax.ShapeDtypeStruct((slot, width), bf16)
    return pl.pallas_call(
        functools.partial(project_kernel, slot=slot),
        grid=(grid,),
        in_specs=[smem(), row, whole(w_one.shape)],
        out_specs=[
            row,
            row,
            row,
            pl.BlockSpec((WIDE // BLOCK, width), lambda i: (i, 0)),
            whole((8, width)),
        ],
        out_shape=[
            out,
            out,
            out,
            jax.ShapeDtypeStruct((slot // BLOCK, width), f32),
            jax.ShapeDtypeStruct((8, width), f32),
        ],
        compiler_params=params(),
        cost_estimate=pl.CostEstimate(
            flops=2 * slot * width * 3 * width, bytes_accessed=slot * width * 8, transcendentals=0
        ),
        name="project",
    )(lens, x, w_one)


def sort_parts(lens, u_ref, ws_ref, slot):
    blocks = u_ref.shape[0]
    ends = ends_of(lens, slot)
    quarter = slot // 4
    is_long = lens[0, 0] > quarter

    def group_of(axis, shape):
        index = iota(shape, axis)
        start = index * BLOCK
        live = start < end_at(start, ends, slot)
        member = jnp.where(is_long, 0, start // quarter)
        return jnp.where(live, member, 4 + index)

    same = group_of(0, (blocks, blocks)) == group_of(1, (blocks, blocks))
    start = iota((blocks, 1), 0) * BLOCK
    count = jnp.clip(end_at(start, ends, slot) - start, 0, BLOCK).astype(f32)
    scale = lax.rsqrt(jnp.maximum(count, 1.0))
    summary = u_ref[...] * scale
    w_sort = ws_ref[...].astype(f32)
    sort_q = dot(summary, w_sort[:, :SORT], highest)
    sort_k = dot(summary, w_sort[:, SORT:], highest)
    return same, scale, summary, w_sort, sort_q, sort_k


def sort_columns(w_one):
    return pl.BlockSpec((w_one.shape[0], 2 * SORT), lambda i: (0, 3 * w_one.shape[0] // (2 * SORT)))


def column_of(row, eye):
    return jnp.sum(jnp.where(eye, row, 0.0), axis=1, keepdims=True)


def sort_kernel(lens, u_ref, ws_ref, partner_ref, bias_ref, steps_ref, *, slot):
    blocks = u_ref.shape[0]
    same, _, _, _, sort_q, sort_k = sort_parts(lens, u_ref, ws_ref, slot)
    raw = dot_nt(sort_q, sort_k, highest)
    logits = jnp.where(same, raw / math.sqrt(SORT), masked)

    def normalize(value, axis):
        top = jnp.max(value, axis=axis, keepdims=True)
        return value - (top + jnp.log(jnp.sum(jnp.exp(value - top), axis=axis, keepdims=True)))

    for turn in range(SINK):
        logits = normalize(logits, 1)
        steps_ref[2 * turn] = logits
        logits = normalize(logits, 0)
        steps_ref[2 * turn + 1] = logits
    eye = iota((blocks, blocks), 0) == iota((blocks, blocks), 1)
    members = jnp.sum(same.astype(f32), axis=1, keepdims=True)
    partner = column_of(partner_ref[...].astype(f32), eye)
    pick = partner == iota((blocks, blocks), 1).astype(f32)
    bias = jnp.sum(jnp.where(pick, logits, 0.0), axis=1, keepdims=True) + jnp.log(members)
    bias_ref[...] = jnp.sum(jnp.where(eye, bias, 0.0), axis=0, keepdims=True)


def sort_net(lens, u, w_sort, partner, slot):
    blocks = u.shape[0]
    return pl.pallas_call(
        functools.partial(sort_kernel, slot=slot),
        in_specs=[smem(), whole(u.shape), sort_columns(w_sort), whole(partner.shape)],
        out_specs=[whole((1, blocks)), whole((2 * SINK, blocks, blocks))],
        out_shape=[
            jax.ShapeDtypeStruct((1, blocks), f32),
            jax.ShapeDtypeStruct((2 * SINK, blocks, blocks), f32),
        ],
        grid=(1,),
        compiler_params=params(),
        cost_estimate=pl.CostEstimate(flops=10**8, bytes_accessed=10**7, transcendentals=10**6),
        name="sort_net",
    )(lens, u, w_sort, partner)


def sort_back_kernel(
    lens, u_ref, ws_ref, partner_ref, steps_ref, *refs, slot
):
    *d_bias_refs, d_u_ref, grad_ref = refs
    blocks = u_ref.shape[0]
    same, scale, summary, w_sort, sort_q, sort_k = sort_parts(lens, u_ref, ws_ref, slot)
    eye = iota((blocks, blocks), 0) == iota((blocks, blocks), 1)
    partner = column_of(partner_ref[...].astype(f32), eye)
    pick = partner == iota((blocks, blocks), 1).astype(f32)
    d_bias = column_of(sum(ref[...] for ref in d_bias_refs), eye)
    d_logits = jnp.where(pick, d_bias, 0.0)
    for turn in reversed(range(SINK)):
        for axis, step in ((0, 2 * turn + 1), (1, 2 * turn)):
            share = jnp.exp(steps_ref[step])
            d_logits = d_logits - share * jnp.sum(d_logits, axis=axis, keepdims=True)
    d_raw = jnp.where(same, d_logits, 0.0) / math.sqrt(SORT)
    d_sort_q = dot(d_raw, sort_k, highest)
    d_sort_k = dot_tn(d_raw, sort_q, highest)
    d_sort = jnp.concatenate([d_sort_q, d_sort_k], axis=1)
    grad_ref[...] = dot_tn(summary, d_sort, highest)
    d_u_ref[...] = dot_nt(d_sort, w_sort, highest) * scale


def sort_back(lens, u, w_sort, partner, d_bias, steps, slot):
    blocks, width = u.shape
    return pl.pallas_call(
        functools.partial(sort_back_kernel, slot=slot),
        in_specs=[
            smem(),
            whole(u.shape),
            sort_columns(w_sort),
            whole(partner.shape),
            whole(steps.shape),
            *[whole(part.shape) for part in d_bias],
        ],
        out_specs=[whole((blocks, width)), whole((width, 2 * SORT))],
        out_shape=[
            jax.ShapeDtypeStruct((blocks, width), f32),
            jax.ShapeDtypeStruct((width, 2 * SORT), f32),
        ],
        grid=(1,),
        compiler_params=params(),
        cost_estimate=pl.CostEstimate(flops=10**8, bytes_accessed=10**7, transcendentals=10**6),
        name="sort_back",
    )(lens, u, w_sort, partner, steps, *d_bias)


def lane_block(rows):
    return (iota((rows, 2 * GROUP), 1) % GROUP) // BLOCK


def compact(full):
    at = lane_block(BLOCK)
    part = [full[c * BLOCK : (c + 1) * BLOCK] for c in range(GROUP // BLOCK)]
    return jnp.where(
        at < 2,
        jnp.where(at < 1, part[0], part[1]),
        jnp.where(at < 3, part[2], part[3]),
    )


def diagonal_mask():
    rows = 2 * GROUP
    return jnp.where((iota((rows, rows), 0) % GROUP) // BLOCK == lane_block(rows), 1.0, 0.0).astype(bf16)


def spread(own, far, mask):
    own, far = own.astype(bf16), far.astype(bf16)
    times = GROUP // BLOCK
    return jnp.concatenate([own] * times + [far] * times, axis=0) * mask


def head_stack(pair, lanes):
    zero = jnp.zeros_like(pair)
    return jnp.concatenate(
        [jnp.where(lanes < HEAD, pair, zero), jnp.where(lanes < HEAD, zero, pair)], axis=0
    )


def head_lanes():
    return iota((GROUP, LANES), 1)


def by_lane(values):
    at = iota((1, GROUP), 1) // BLOCK
    return jnp.where(
        at < 2,
        jnp.where(at < 1, values[0], values[1]),
        jnp.where(at < 3, values[2], values[3]),
    )


def gather_far(dst, src, partners):
    for c, p in enumerate(partners):
        dst[GROUP + c * BLOCK : GROUP + (c + 1) * BLOCK, :] = src[pl.ds(pl.multiple_of(p * BLOCK, BLOCK), BLOCK), :]


def attend_kernel(lens, partner, bias, q_ref, k_ref, v_ref, o_ref, p_ref, mask_ref, *, slot):
    tile, width = q_ref.shape
    step = pl.program_id(0)
    pairs = width // LANES
    per = GROUP // BLOCK

    @pl.when(step == 0)
    def _():
        mask_ref[...] = diagonal_mask()

    ends = ends_of(lens, slot)
    scale = 1.0 / math.sqrt(HEAD)

    def some_groups(turn, carry):
        mask = mask_ref[...]
        lanes = head_lanes()
        key = iota((BLOCK, GROUP), 0)
        query = iota((BLOCK, GROUP), 1)
        work = []
        for part in range(ABREAST):
            g = turn * ABREAST + part
            first = step * (tile // BLOCK) + g * per
            partners = [partner[0, first + c] for c in range(per)]
            rows = pl.ds(pl.multiple_of(first * BLOCK, GROUP), GROUP)
            q_rows = pl.ds(pl.multiple_of(g * GROUP, GROUP), GROUP)
            spans = [rows] + [pl.ds(pl.multiple_of(p * BLOCK, BLOCK), BLOCK) for p in partners]
            own_place = (first + query // BLOCK) * BLOCK + key
            far_place = by_lane(partners) * BLOCK + key
            own_live = (own_place < end_at(own_place, ends, slot)) | (query % BLOCK == key)
            far_live = far_place < end_at(far_place, ends, slot)
            own_live = jnp.concatenate([own_live.astype(f32)] * 2, axis=1) > 0.5
            far_live = jnp.concatenate([far_live.astype(f32)] * 2, axis=1) > 0.5
            lane_bias = by_lane([bias[0, first + c] for c in range(per)])
            lane_bias = jnp.concatenate([lane_bias] * 2, axis=1)
            for pair in range(pairs):
                work.append((g, pair, spans, q_rows, own_live, far_live, lane_bias))
        scores = []
        for g, pair, spans, q_rows, *_ in work:
            cols = slice(pair * LANES, (pair + 1) * LANES)
            q_two = head_stack(q_ref[q_rows, cols], lanes)
            k_all = jnp.concatenate([k_ref[at, cols] for at in spans], axis=0)
            scores.append(dot_nt(k_all, q_two))
        probs = []
        for score, (g, pair, spans, q_rows, own_live, far_live, lane_bias) in zip(scores, work):
            own = jnp.where(own_live, compact(score[:GROUP]) * scale, masked)
            far = jnp.where(far_live, compact(score[GROUP:]) * scale + lane_bias, masked)
            top = jnp.maximum(
                jnp.max(own, axis=0, keepdims=True), jnp.max(far, axis=0, keepdims=True)
            )
            own = jnp.exp(own - top)
            far = jnp.exp(far - top)
            total = jnp.sum(own, axis=0, keepdims=True) + jnp.sum(far, axis=0, keepdims=True)
            inverse = 1.0 / total
            probs.append(((own * inverse).astype(bf16), (far * inverse).astype(bf16)))
        mixes = []
        for (own, far), (g, pair, spans, *_) in zip(probs, work):
            cols = slice(pair * LANES, (pair + 1) * LANES)
            v_all = jnp.concatenate([v_ref[at, cols] for at in spans], axis=0)
            mixes.append(dot(v_all.T, spread(own, far, mask)))
        for mixed, (own, far), (g, pair, spans, q_rows, *_) in zip(mixes, probs, work):
            at = pl.multiple_of(g * 2 * BLOCK, 2 * BLOCK)
            p_ref[pair, pl.ds(at, BLOCK), :] = own
            p_ref[pair, pl.ds(at + BLOCK, BLOCK), :] = far
            o_ref[pair * LANES : pair * LANES + HEAD, q_rows] = mixed[:HEAD, :GROUP].astype(bf16)
            o_ref[pair * LANES + HEAD : (pair + 1) * LANES, q_rows] = mixed[HEAD:, GROUP:].astype(bf16)
        return carry

    lax.fori_loop(0, tile // GROUP // ABREAST, some_groups, 0)


def attend(lens, partner, bias, q, k, v):
    slot, width = q.shape
    grid = slot // TILE
    pairs, per_tile = width // LANES, (TILE // GROUP) * 2 * BLOCK
    return pl.pallas_call(
        functools.partial(attend_kernel, slot=slot),
        grid=(grid,),
        in_specs=[
            smem(),
            smem(),
            smem(),
            pl.BlockSpec((TILE, width), lambda i: (i, 0)),
            whole(k.shape),
            whole(v.shape),
        ],
        out_specs=[
            pl.BlockSpec((width, TILE), lambda i: (0, i)),
            pl.BlockSpec((pairs, per_tile, 2 * GROUP), lambda i: (0, i, 0)),
        ],
        out_shape=[
            jax.ShapeDtypeStruct((width, slot), bf16),
            jax.ShapeDtypeStruct((pairs, grid * per_tile, 2 * GROUP), bf16),
        ],
        scratch_shapes=[
            pltpu.VMEM((2 * GROUP, 2 * GROUP), bf16),
        ],
        compiler_params=params(),
        cost_estimate=pl.CostEstimate(
            flops=20 * 10**9, bytes_accessed=slot * width * 10, transcendentals=slot * 512
        ),
        name="attend",
    )(lens, partner, bias, q, k, v)


def attend_back_kernel(
    partner, q_ref, do_ref, p_ref, k_ref, v_ref,
    dq_ref, dk_ref, dv_ref, db_ref,
    mask_ref, dk_sum, dv_sum, db_sum,
):
    tile = q_ref.shape[0]
    step = pl.program_id(0)
    per = GROUP // BLOCK

    @pl.when(step == 0)
    def _():
        mask_ref[...] = diagonal_mask()
        dk_sum[...] = jnp.zeros_like(dk_sum)
        dv_sum[...] = jnp.zeros_like(dv_sum)

    scale = 1.0 / math.sqrt(HEAD)
    lanes = head_lanes()
    mask = mask_ref[...]
    work, d_probs, seconds, thirds = [], [], [], []
    for g in range(tile // GROUP):
        first = step * (tile // BLOCK) + g * per
        partners = [partner[0, first + c] for c in range(per)]
        rows = pl.ds(pl.multiple_of(first * BLOCK, GROUP), GROUP)
        spans = [rows] + [pl.ds(pl.multiple_of(p * BLOCK, BLOCK), BLOCK) for p in partners]
        q_rows = slice(g * GROUP, (g + 1) * GROUP)
        q_two = head_stack(q_ref[q_rows, :], lanes)
        do_two = head_stack(do_ref[q_rows, :], lanes)
        v_all = jnp.concatenate([v_ref[at, :] for at in spans], axis=0)
        work.append((g, spans, q_rows, q_two, do_two))
        d_probs.append(dot_nt(v_all, do_two))
    for d_prob, (g, *_) in zip(d_probs, work):
        at = g * 2 * BLOCK
        own_b = p_ref[0, at : at + BLOCK, :]
        far_b = p_ref[0, at + BLOCK : at + 2 * BLOCK, :]
        own, far = own_b.astype(f32), far_b.astype(f32)
        d_own, d_far = compact(d_prob[:GROUP]), compact(d_prob[GROUP:])
        delta = jnp.sum(own * d_own, axis=0, keepdims=True) + jnp.sum(
            far * d_far, axis=0, keepdims=True
        )
        d_own = own * (d_own - delta)
        d_far = far * (d_far - delta)
        d_bias = jnp.sum(d_far, axis=0, keepdims=True)
        db_sum[pl.ds(step * (tile // GROUP) + g, 1), :] = d_bias[:, :GROUP] + d_bias[:, GROUP:]
        seconds.append((spread(d_own * scale, d_far * scale, mask), spread(own_b, far_b, mask)))
    for (d_scores, prob), (g, spans, q_rows, q_two, do_two) in zip(seconds, work):
        k_all = jnp.concatenate([k_ref[at, :] for at in spans], axis=0)
        thirds.append((dot(d_scores, q_two), dot(prob, do_two), dot(k_all.T, d_scores)))
    for (dk, dv, dq), (g, spans, q_rows, *_) in zip(thirds, work):
        dq = jnp.concatenate([dq[:HEAD, :GROUP], dq[HEAD:, GROUP:]], axis=0)
        dq_ref[q_rows, :] = dq.T.astype(bf16)
        dk_sum[spans[0], :] += dk[:GROUP]
        dv_sum[spans[0], :] += dv[:GROUP]
        for c in range(per):
            here = slice(GROUP + c * BLOCK, GROUP + (c + 1) * BLOCK)
            dk_sum[spans[1 + c], :] += dk[here]
            dv_sum[spans[1 + c], :] += dv[here]

    @pl.when(step == pl.num_programs(0) - 1)
    def _():
        dk_ref[...] = dk_sum[...].astype(bf16)
        dv_ref[...] = dv_sum[...].astype(bf16)
        groups = db_sum.shape[0]
        blocks = groups * per
        pick = (iota((GROUP, blocks), 0) // BLOCK == iota((GROUP, blocks), 1) % per).astype(f32)
        sums = dot(db_sum[...], pick, highest)
        mine = iota((groups, blocks), 1) // per == iota((groups, blocks), 0)
        db_ref[...] = jnp.sum(jnp.where(mine, sums, 0.0), axis=0, keepdims=True)


def attend_back(pair, partner, q, d_o, probs, k, v):
    slot = q.shape[0]
    grid = slot // WIDE
    per_tile = (WIDE // GROUP) * 2 * BLOCK
    row = pl.BlockSpec((WIDE, LANES), lambda i: (i, pair))
    once = pl.BlockSpec((slot, LANES), lambda i: (0, pair), pipeline_mode=pl.Buffered(1))
    out = jax.ShapeDtypeStruct((slot, LANES), bf16)
    return pl.pallas_call(
        attend_back_kernel,
        grid=(grid,),
        in_specs=[
            smem(),
            row,
            row,
            pl.BlockSpec((1, per_tile, 2 * GROUP), lambda i: (pair, i, 0)),
            once,
            once,
        ],
        out_specs=[
            pl.BlockSpec((WIDE, LANES), lambda i: (i, 0)),
            whole((slot, LANES)),
            whole((slot, LANES)),
            whole((1, slot // BLOCK)),
        ],
        out_shape=[out, out, out, jax.ShapeDtypeStruct((1, slot // BLOCK), f32)],
        scratch_shapes=[
            pltpu.VMEM((2 * GROUP, 2 * GROUP), bf16),
            pltpu.VMEM((slot, LANES), f32),
            pltpu.VMEM((slot, LANES), f32),
            pltpu.VMEM((slot // GROUP, GROUP), f32),
        ],
        compiler_params=params(),
        cost_estimate=pl.CostEstimate(
            flops=10 * 10**9, bytes_accessed=slot * LANES * 16, transcendentals=0
        ),
        name="attend_back",
    )(partner, q, d_o, probs, k, v)


def ffn_kernel(
    x_ref, dy_ref, o_ref, norms_ref, w_ref,
    out_ref, dx_ref, do_ref, g_ref, g_norm_ref,
    h_scr, ht_scr, dyt_scr, y_scr, dh_scr, gt_scr,
):
    tile, width = x_ref.shape
    hidden = gt_scr.shape[1]
    slabs = hidden // width
    parts = width // ROWS
    whole_rows = slice(slabs * ROWS, (slabs + 1) * ROWS)
    out_rows = slice((slabs + 1) * ROWS, (2 * slabs + 1) * ROWS)
    step = pl.program_id(0)

    @pl.when(step == 0)
    def _():
        g_ref[...] = jnp.zeros_like(g_ref)
        gt_scr[...] = jnp.zeros_like(gt_scr)
        g_norm_ref[...] = jnp.zeros_like(g_norm_ref)

    o_t = o_ref[...]
    w_o = w_ref[:, whole_rows, :].reshape(width, width)
    x_one = x_ref[...].astype(f32) + dot(o_t.T, w_o)
    hat, rstd = norm_stats(x_one)
    h_two = (hat * norms_ref[2:3, :] + norms_ref[3:4, :]).astype(bf16)
    h_scr[...] = h_two
    ht_scr[...] = h_two.T
    dyt_scr[...] = dy_ref[...].T
    y_scr[...] = x_one
    dh_scr[...] = jnp.zeros_like(dh_scr)
    root = math.sqrt(2.0 / math.pi)

    def before(c):
        w_in = w_ref[:, c * ROWS : (c + 1) * ROWS, :].reshape(width, width)
        share = parts // slabs
        w_out = w_ref[c * share : (c + 1) * share, out_rows, :].reshape(width, width)
        act = dot(h_scr[...], w_in)
        d_hid = dot_nt(dy_ref[...], w_out)
        return w_in, w_out, act, d_hid

    def between(act, d_hid):
        square = act * act
        curve = jnp.tanh(act * (root + (root * 0.044715) * square))
        gate = 0.5 + 0.5 * curve
        hid = act * gate
        slope = gate + hid * (1.0 - curve) * (root + (3.0 * root * 0.044715) * square)
        return hid.astype(bf16), (d_hid * slope).astype(bf16)

    def after(c, w_in, w_out, hid, d_act):
        cols = slice(c * width, (c + 1) * width)
        y_scr[...] += dot(hid, w_out)
        gt_scr[:, cols] += dot(dyt_scr[...], hid)
        slab = slice(c * ROWS, (c + 1) * ROWS)
        g_ref[:, slab, :] += dot(ht_scr[...], d_act).reshape(parts, ROWS, width)
        dh_scr[...] += dot_nt(d_act, w_in)

    ahead = before(0)
    for c in range(slabs):
        w_in, w_out, act, d_hid = ahead
        if c + 1 < slabs:
            ahead = before(c + 1)
        hid, d_act = between(act, d_hid)
        after(c, w_in, w_out, hid, d_act)
    out_ref[...] = y_scr[...].astype(bf16)
    d_h = dh_scr[...]
    g_norm_ref[2:3, :] += jnp.sum(d_h * hat, axis=0, keepdims=True)
    g_norm_ref[3:4, :] += jnp.sum(d_h, axis=0, keepdims=True)
    d_x = dy_ref[...].astype(f32) + norm_back(d_h, hat, rstd, norms_ref[2:3, :])
    dx_ref[...] = d_x
    d_z = d_x.astype(bf16)
    g_ref[:, whole_rows, :] += dot(o_t, d_z).reshape(parts, ROWS, width)
    do_ref[...] = dot_nt(d_z, w_o).astype(bf16)

    @pl.when(step == pl.num_programs(0) - 1)
    def _():
        share = parts // slabs
        for c in range(slabs):
            g_ref[c * share : (c + 1) * share, out_rows, :] = gt_scr[
                :, c * width : (c + 1) * width
            ].T.reshape(share, slabs * ROWS, width)


def ffn(x, dy, o_t, norms, w_two):
    slot, width = x.shape
    hidden = (w_two.shape[1] // ROWS - 1) // 2 * width
    grid = slot // TILE
    row = pl.BlockSpec((TILE, width), lambda i: (i, 0))

    def once(shape):
        return pl.BlockSpec(shape, lambda i: (0,) * len(shape), pipeline_mode=pl.Buffered(1))

    return pl.pallas_call(
        ffn_kernel,
        grid=(grid,),
        in_specs=[
            row,
            row,
            pl.BlockSpec((width, TILE), lambda i: (0, i)),
            once(norms.shape),
            once(w_two.shape),
        ],
        out_specs=[row, row, row, once(w_two.shape), once((8, width))],
        out_shape=[
            jax.ShapeDtypeStruct((slot, width), bf16),
            jax.ShapeDtypeStruct((slot, width), f32),
            jax.ShapeDtypeStruct((slot, width), bf16),
            jax.ShapeDtypeStruct(w_two.shape, f32),
            jax.ShapeDtypeStruct((8, width), f32),
        ],
        scratch_shapes=[
            pltpu.VMEM((TILE, width), bf16),
            pltpu.VMEM((width, TILE), bf16),
            pltpu.VMEM((width, TILE), bf16),
            pltpu.VMEM((TILE, width), f32),
            pltpu.VMEM((TILE, width), f32),
            pltpu.VMEM((width, hidden), f32),
        ],
        compiler_params=params(),
        cost_estimate=pl.CostEstimate(
            flops=2 * slot * width * (3 * width + 6 * hidden),
            bytes_accessed=slot * width * 14,
            transcendentals=slot * hidden,
        ),
        name="ffn",
    )(x, dy, o_t, norms, w_two)


def project_back_kernel(
    lens, x_ref, dx_ref, du_ref, norms_ref, w_ref, g_sort_ref, g_two_ref, *refs, slot
):
    *d_refs, grad_ref, g_ref, g_norm_ref = refs
    tile, width = x_ref.shape
    step = pl.program_id(0)

    @pl.when(step == 0)
    def _():
        g_ref[...] = jnp.zeros_like(g_ref)
        g_norm_ref[...] = jnp.zeros_like(g_norm_ref)

    pairs = width // LANES
    ends = ends_of(lens, slot)
    blocks = SUB // BLOCK
    first = []
    for r in range(0, tile, SUB):
        rows = slice(r, r + SUB)
        places = step * tile + r + iota((SUB, 1), 0)
        live = places < end_at(places, ends, slot)
        d_u = du_ref[r // BLOCK : r // BLOCK + blocks, :].reshape(blocks, 1, width)
        d_h = jnp.broadcast_to(d_u, (blocks, BLOCK, width)).reshape(SUB, width)
        d_h = jnp.where(live, d_h, 0.0)
        for part in range(3):
            cols = slice(part * width, (part + 1) * width)
            d_part = jnp.concatenate(
                [ref[rows, :] for ref in d_refs[part * pairs : (part + 1) * pairs]], axis=1
            )
            d_h = d_h + dot_nt(d_part, w_ref[:, cols])
        first.append(d_h)
    hats = []
    for r, d_h in zip(range(0, tile, SUB), first):
        rows = slice(r, r + SUB)
        hat, rstd = norm_stats(x_ref[rows, :].astype(f32))
        hats.append((hat * norms_ref[0:1, :] + norms_ref[1:2, :]).astype(bf16))
        g_norm_ref[0:1, :] += jnp.sum(d_h * hat, axis=0, keepdims=True)
        g_norm_ref[1:2, :] += jnp.sum(d_h, axis=0, keepdims=True)
        grad_ref[rows, :] = dx_ref[rows, :] + norm_back(d_h, hat, rstd, norms_ref[0:1, :])
    h_one = jnp.concatenate(hats, axis=0)
    for part in range(3):
        cols = slice(part * width, (part + 1) * width)
        d_part = jnp.concatenate([ref[...] for ref in d_refs[part * pairs : (part + 1) * pairs]], axis=1)
        g_ref[:, cols] += dot_tn(h_one, d_part)

    @pl.when(step == pl.num_programs(0) - 1)
    def _():
        g_ref[:, 3 * width : 3 * width + LANES] = g_sort_ref[...]
        small = g_norm_ref[...] + g_two_ref[...]
        rest = jnp.zeros((LANES - small.shape[0], width), f32)
        g_ref[:, 3 * width + LANES :] = jnp.concatenate([small, rest], axis=0).T


def project_back(lens, x, d_x, d_q, d_k, d_v, d_u, norms, w_one, g_sort, g_two):
    slot, width = x.shape
    grid = slot // WIDE
    row = pl.BlockSpec((WIDE, width), lambda i: (i, 0))

    def once(shape):
        return pl.BlockSpec(shape, lambda i: (0, 0), pipeline_mode=pl.Buffered(1))

    return pl.pallas_call(
        functools.partial(project_back_kernel, slot=slot),
        grid=(grid,),
        in_specs=[
            smem(),
            row,
            row,
            pl.BlockSpec((WIDE // BLOCK, width), lambda i: (i, 0)),
            once(norms.shape),
            once(w_one.shape),
            once(g_sort.shape),
            once(g_two.shape),
        ]
        + [pl.BlockSpec((WIDE, LANES), lambda i: (i, 0))] * (3 * width // LANES),
        out_specs=[row, once(w_one.shape)],
        out_shape=[
            jax.ShapeDtypeStruct((slot, width), f32),
            jax.ShapeDtypeStruct(w_one.shape, f32),
        ],
        scratch_shapes=[pltpu.VMEM((8, width), f32)],
        compiler_params=params(),
        cost_estimate=pl.CostEstimate(
            flops=2 * slot * width * 6 * width, bytes_accessed=slot * width * 18, transcendentals=0
        ),
        name="project_back",
    )(lens, x, d_x, d_u, norms, w_one, g_sort, g_two, *d_q, *d_k, *d_v)


def pack_kernel(wqkv, wo, wsort, win, wout, norms_t, one_ref, two_ref):
    rows, wide = wqkv.shape
    width = wo.shape[1]
    one_ref[:, :wide] = wqkv[...].astype(bf16)
    one_ref[:, wide : wide + LANES] = wsort[...].astype(bf16)
    few = norms_t.shape[0]
    tall = jnp.concatenate([norms_t[...], jnp.zeros((LANES - few, rows), f32)], axis=0)
    one_ref[:, wide + LANES :] = tall.T.astype(bf16)
    slabs = win.shape[1] // width
    for c in range(slabs):
        two_ref[c * rows : (c + 1) * rows, :] = win[:, c * width : (c + 1) * width].astype(bf16)
    two_ref[slabs * rows : (slabs + 1) * rows, :] = wo[...].astype(bf16)
    two_ref[(slabs + 1) * rows :, :] = wout[...].astype(bf16)


def pack(masters):
    wqkv, wo, wsort, win, wout, norms = masters
    rows = wqkv.shape[0]
    return pl.pallas_call(
        pack_kernel,
        out_shape=[
            jax.ShapeDtypeStruct((rows, wqkv.shape[1] + 2 * LANES), bf16),
            jax.ShapeDtypeStruct((rows * (win.shape[1] // wo.shape[1] + 1) + wout.shape[0], wo.shape[1]), bf16),
        ],
        compiler_params=params(),
        name="pack",
    )(wqkv, wo, wsort, win, wout, norms.T)


def adamw_kernel(one_ref, two_ref, *refs):
    masters, moments, squares, outs = refs[:6], refs[6:12], refs[12:18], refs[18:]
    rows, width = masters[1].shape
    wide = masters[0].shape[1]
    slabs = masters[3].shape[1] // width
    few = masters[5].shape[0]
    norm_grad = one_ref[:, wide + LANES :].T[:few, :]
    grads = (
        one_ref[:, :wide],
        two_ref[slabs * rows : (slabs + 1) * rows, :],
        one_ref[:, wide : wide + LANES],
        jnp.concatenate([two_ref[c * rows : (c + 1) * rows, :] for c in range(slabs)], axis=1),
        two_ref[(slabs + 1) * rows :, :],
        norm_grad,
    )
    for i in range(6):
        weight, grad = masters[i][...], grads[i]
        moment = beta_one * moments[i][...] + (1.0 - beta_one) * grad
        square = beta_two * squares[i][...] + (1.0 - beta_two) * grad * grad
        m_hat = moment / (1.0 - beta_one**STEP)
        s_hat = square / (1.0 - beta_two**STEP)
        outs[3 * i][...] = weight - rates[i] * (
            m_hat / (jnp.sqrt(s_hat) + adam_eps) + decay * weight
        )
        outs[3 * i + 1][...] = moment
        outs[3 * i + 2][...] = square


def adamw(one, two, masters, moments, squares):
    flip = lambda group: (*group[:5], group[5].T)
    args = (one, two, *flip(masters), *flip(moments), *flip(squares))
    shapes = [a.shape for a in flip(masters)]
    outs = pl.pallas_call(
        adamw_kernel,
        out_shape=[jax.ShapeDtypeStruct(shape, f32) for shape in shapes for _ in range(3)],
        compiler_params=params(),
        name="adamw",
    )(*args)
    return (*outs[:15], *[o.T for o in outs[15:]])


def regroup(gathered, size, rows, slabs):
    if rows == ROWS:
        return gathered
    times = ROWS // rows
    width = gathered.shape[-1]
    block = gathered.reshape(size // times, times, 2 * slabs + 1, rows, width)
    inner = block[:, :, : slabs + 1].transpose(0, 2, 1, 3, 4)
    outer = block[:, :, slabs + 1 :]
    return jnp.concatenate(
        [
            inner.reshape(size // times, (slabs + 1) * ROWS, width),
            outer.reshape(size // times, slabs * ROWS, width),
        ],
        axis=1,
    )


def ungroup(grads, size, rows, slabs):
    if rows == ROWS:
        return grads
    times = ROWS // rows
    width = grads.shape[-1]
    inner = grads[:, : (slabs + 1) * ROWS].reshape(size // times, slabs + 1, times, rows, width)
    outer = grads[:, (slabs + 1) * ROWS :].reshape(size // times, times, slabs, rows, width)
    block = jnp.concatenate([inner.transpose(0, 2, 1, 3, 4), outer], axis=2)
    return block.reshape(size, (2 * slabs + 1) * rows, width)


def swap(value, bit, size):
    return lax.ppermute(value, "dp", [(i, i ^ (1 << bit)) for i in range(size)])


def gather(block, size):
    count = size.bit_length() - 1
    place = lax.axis_index("dp")
    held = block.reshape((1,) * count + block.shape)
    for bit in reversed(range(count)):
        axis = count - 1 - bit
        came = swap(held, bit, size)
        upper = ((place >> bit) & 1) == 1
        held = jnp.concatenate(
            [jnp.where(upper, came, held), jnp.where(upper, held, came)], axis=axis
        )
    return held.reshape((size * block.shape[0],) + block.shape[1:])


class ScatterSum:
    def __init__(self, value, size):
        self.size, self.count = size, size.bit_length() - 1
        self.rest = value.shape[1:]
        self.held = value.reshape((2,) * self.count + value.shape[0:0] + (value.shape[0] // size,) + self.rest)
        self.bit = 0

    def begin(self):
        place = lax.axis_index("dp")
        axis = self.count - 1 - self.bit
        mine = (place >> self.bit) & 1
        sent = lax.dynamic_index_in_dim(self.held, 1 - mine, axis, keepdims=True).astype(bf16)
        self.kept = lax.dynamic_index_in_dim(self.held, mine, axis, keepdims=True)
        self.came = swap(sent, self.bit, self.size)
        self.bit += 1

    def end(self):
        self.held = self.kept + self.came.astype(f32)
        return self.held

    def finish(self):
        while self.bit < self.count:
            self.begin()
            self.end()
        return self.held.reshape((-1,) + self.rest)


def body(size, x, dy, lens, partner, *state):
    slot, width = x.shape
    masters, moments, squares = state[:6], state[6:12], state[12:]
    rows = masters[0].shape[0]
    slabs = masters[3].shape[1] // width
    pack_one, pack_two = pack(masters)
    w_one = gather(pack_one, size)
    w_two = regroup(lax.all_gather(pack_two, "dp", axis=0), size, rows, slabs)

    q, k, v, u, norms = project(lens, x, w_one)
    bias, steps = sort_net(lens, u, w_one, partner, slot)
    o_t, probs = attend(lens, partner, bias, q, k, v)
    out, d_x, d_o, g_rest, g_two = ffn(x, dy, o_t, norms, w_two)
    two = ungroup(g_rest, size, rows, slabs)
    two = ScatterSum(two.reshape((-1, width)), size)
    back = []
    for pair in range(width // LANES):
        two.begin()
        back.append(attend_back(pair, partner, q, d_o, probs, k, v))
        held = two.end()
        q, d_o, two.held = lax.optimization_barrier((q, d_o, held))
    d_q, d_k, d_v, d_bias = zip(*back)
    d_u, g_sort = sort_back(lens, u, w_one, partner, d_bias, steps, slot)
    two.begin()
    grad_in, g_one = project_back(lens, x, d_x, d_q, d_k, d_v, d_u, norms, w_one, g_sort, g_two)
    two.end()
    one = ScatterSum(g_one, size).finish()
    outs = adamw(one, two.finish(), masters, moments, squares)
    return (out, grad_in, *outs)


def solution(mesh):
    spec = P("dp", None)
    return jax.shard_map(
        functools.partial(body, mesh.shape["dp"]),
        mesh=mesh,
        in_specs=(spec,) * 22,
        out_specs=(spec,) * 20,
        check_vma=False,
    )
```

```python
import functools
import math

import jax
import jax.numpy as jnp
from jax import lax
from jax.experimental import pallas as pl
from jax.experimental.pallas import tpu as pltpu
from jax.sharding import PartitionSpec as P

HEADS = 8
HEAD = 64
SORT = 64
BLOCK = 32
SINK = 8
STEP = 10
TILE = 512
WIDE = 1024
ROWS = 16
ABREAST = 4
SUB = 256
GROUP = 128
LANES = 128

highest = lax.Precision.HIGHEST
masked = -1000000000.0
norm_eps = 1e-05
beta_one = 0.9
beta_two = 0.999
adam_eps = 1e-08
decay = 0.01
rates = (0.05, 0.15, 0.05, 0.05, 0.025, 0.5)
f32 = jnp.float32
bf16 = jnp.bfloat16


def dot(left, right, precision=None):
    return jnp.dot(left, right, precision=precision, preferred_element_type=f32)


def dot_nt(left, right, precision=None):
    return lax.dot_general(
        left, right, (((1,), (1,)), ((), ())), precision=precision, preferred_element_type=f32
    )


def dot_tn(left, right, precision=None):
    return lax.dot_general(
        left, right, (((0,), (0,)), ((), ())), precision=precision, preferred_element_type=f32
    )


def iota(shape, axis):
    return lax.broadcasted_iota(jnp.int32, shape, axis)


def ends_of(lens, slot):
    quarter = slot // 4
    is_long = lens[0, 0] > quarter
    return [jnp.where(is_long, lens[0, 0], k * quarter + lens[0, k]) for k in range(4)]


def end_at(places, ends, slot):
    quarter = slot // 4
    return jnp.where(
        places < 2 * quarter,
        jnp.where(places < quarter, ends[0], ends[1]),
        jnp.where(places < 3 * quarter, ends[2], ends[3]),
    )


def norm_stats(value):
    center = value - jnp.mean(value, axis=-1, keepdims=True)
    spread = jnp.mean(center * center, axis=-1, keepdims=True)
    rstd = lax.rsqrt(spread + norm_eps)
    return center * rstd, rstd


def norm_back(grad, hat, rstd, gain):
    d_hat = grad * gain
    mean_d = jnp.mean(d_hat, axis=-1, keepdims=True)
    mean_dh = jnp.mean(d_hat * hat, axis=-1, keepdims=True)
    return rstd * (d_hat - mean_d - hat * mean_dh)


def params(limit=56 << 20):
    return pltpu.CompilerParams(vmem_limit_bytes=limit)


def whole(shape):
    return pl.BlockSpec(shape, lambda *_: (0,) * len(shape))


def smem():
    return pl.BlockSpec(memory_space=pltpu.SMEM)


def project_kernel(lens, x_ref, w_ref, q_ref, k_ref, v_ref, u_ref, norms_ref, *, slot):
    tile, width = x_ref.shape
    base = pl.program_id(0) * tile

    @pl.when(pl.program_id(0) == 0)
    def _():
        norms_ref[...] = w_ref[:, 3 * width + LANES :].astype(f32).T[:8, :]

    parts = []
    for r in range(0, tile, SUB):
        hat, _ = norm_stats(x_ref[r : r + SUB, :].astype(f32))
        parts.append((hat * norms_ref[0:1, :] + norms_ref[1:2, :]).astype(bf16))
        for part, ref in enumerate((q_ref, k_ref, v_ref)):
            ref[r : r + SUB, :] = dot(parts[-1], w_ref[:, part * width : (part + 1) * width]).astype(bf16)
    h_one = jnp.concatenate(parts, axis=0)
    blocks = tile // BLOCK
    at = iota((blocks, tile), 1)
    places = at + base
    live = places < end_at(places, ends_of(lens, slot), slot)
    own = (at // BLOCK) == iota((blocks, tile), 0)
    pick = jnp.where(live & own, 1.0, 0.0).astype(bf16)
    u_ref[...] = dot(pick, h_one)


def project(lens, x, w_one):
    slot, width = x.shape
    grid = slot // WIDE
    row = pl.BlockSpec((WIDE, width), lambda i: (i, 0))
    out = jax.ShapeDtypeStruct((slot, width), bf16)
    return pl.pallas_call(
        functools.partial(project_kernel, slot=slot),
        grid=(grid,),
        in_specs=[smem(), row, whole(w_one.shape)],
        out_specs=[
            row,
            row,
            row,
            pl.BlockSpec((WIDE // BLOCK, width), lambda i: (i, 0)),
            whole((8, width)),
        ],
        out_shape=[
            out,
            out,
            out,
            jax.ShapeDtypeStruct((slot // BLOCK, width), f32),
            jax.ShapeDtypeStruct((8, width), f32),
        ],
        compiler_params=params(),
        cost_estimate=pl.CostEstimate(
            flops=2 * slot * width * 3 * width, bytes_accessed=slot * width * 8, transcendentals=0
        ),
        name="project",
    )(lens, x, w_one)


def sort_parts(lens, u_ref, ws_ref, slot):
    blocks = u_ref.shape[0]
    ends = ends_of(lens, slot)
    quarter = slot // 4
    is_long = lens[0, 0] > quarter

    def group_of(axis, shape):
        index = iota(shape, axis)
        start = index * BLOCK
        live = start < end_at(start, ends, slot)
        member = jnp.where(is_long, 0, start // quarter)
        return jnp.where(live, member, 4 + index)

    same = group_of(0, (blocks, blocks)) == group_of(1, (blocks, blocks))
    start = iota((blocks, 1), 0) * BLOCK
    count = jnp.clip(end_at(start, ends, slot) - start, 0, BLOCK).astype(f32)
    scale = lax.rsqrt(jnp.maximum(count, 1.0))
    summary = u_ref[...] * scale
    w_sort = ws_ref[...].astype(f32)
    sort_q = dot(summary, w_sort[:, :SORT], highest)
    sort_k = dot(summary, w_sort[:, SORT:], highest)
    return same, scale, summary, w_sort, sort_q, sort_k


def sort_columns(w_one):
    return pl.BlockSpec((w_one.shape[0], 2 * SORT), lambda i: (0, 3 * w_one.shape[0] // (2 * SORT)))


def column_of(row, eye):
    return jnp.sum(jnp.where(eye, row, 0.0), axis=1, keepdims=True)


def sort_kernel(lens, u_ref, ws_ref, partner_ref, bias_ref, steps_ref, *, slot):
    blocks = u_ref.shape[0]
    same, _, _, _, sort_q, sort_k = sort_parts(lens, u_ref, ws_ref, slot)
    raw = dot_nt(sort_q, sort_k, highest)
    logits = jnp.where(same, raw / math.sqrt(SORT), masked)

    def normalize(value, axis):
        top = jnp.max(value, axis=axis, keepdims=True)
        return value - (top + jnp.log(jnp.sum(jnp.exp(value - top), axis=axis, keepdims=True)))

    for turn in range(SINK):
        logits = normalize(logits, 1)
        steps_ref[2 * turn] = logits
        logits = normalize(logits, 0)
        steps_ref[2 * turn + 1] = logits
    eye = iota((blocks, blocks), 0) == iota((blocks, blocks), 1)
    members = jnp.sum(same.astype(f32), axis=1, keepdims=True)
    partner = column_of(partner_ref[...].astype(f32), eye)
    pick = partner == iota((blocks, blocks), 1).astype(f32)
    bias = jnp.sum(jnp.where(pick, logits, 0.0), axis=1, keepdims=True) + jnp.log(members)
    bias_ref[...] = jnp.sum(jnp.where(eye, bias, 0.0), axis=0, keepdims=True)


def sort_net(lens, u, w_sort, partner, slot):
    blocks = u.shape[0]
    return pl.pallas_call(
        functools.partial(sort_kernel, slot=slot),
        in_specs=[smem(), whole(u.shape), sort_columns(w_sort), whole(partner.shape)],
        out_specs=[whole((1, blocks)), whole((2 * SINK, blocks, blocks))],
        out_shape=[
            jax.ShapeDtypeStruct((1, blocks), f32),
            jax.ShapeDtypeStruct((2 * SINK, blocks, blocks), f32),
        ],
        grid=(1,),
        compiler_params=params(),
        cost_estimate=pl.CostEstimate(flops=10**8, bytes_accessed=10**7, transcendentals=10**6),
        name="sort_net",
    )(lens, u, w_sort, partner)


def sort_back_kernel(
    lens, u_ref, ws_ref, partner_ref, steps_ref, *refs, slot
):
    *d_bias_refs, d_u_ref, grad_ref = refs
    blocks = u_ref.shape[0]
    same, scale, summary, w_sort, sort_q, sort_k = sort_parts(lens, u_ref, ws_ref, slot)
    eye = iota((blocks, blocks), 0) == iota((blocks, blocks), 1)
    partner = column_of(partner_ref[...].astype(f32), eye)
    pick = partner == iota((blocks, blocks), 1).astype(f32)
    d_bias = column_of(sum(ref[...] for ref in d_bias_refs), eye)
    d_logits = jnp.where(pick, d_bias, 0.0)
    for turn in reversed(range(SINK)):
        for axis, step in ((0, 2 * turn + 1), (1, 2 * turn)):
            share = jnp.exp(steps_ref[step])
            d_logits = d_logits - share * jnp.sum(d_logits, axis=axis, keepdims=True)
    d_raw = jnp.where(same, d_logits, 0.0) / math.sqrt(SORT)
    d_sort_q = dot(d_raw, sort_k, highest)
    d_sort_k = dot_tn(d_raw, sort_q, highest)
    d_sort = jnp.concatenate([d_sort_q, d_sort_k], axis=1)
    grad_ref[...] = dot_tn(summary, d_sort, highest)
    d_u_ref[...] = dot_nt(d_sort, w_sort, highest) * scale


def sort_back(lens, u, w_sort, partner, d_bias, steps, slot):
    blocks, width = u.shape
    return pl.pallas_call(
        functools.partial(sort_back_kernel, slot=slot),
        in_specs=[
            smem(),
            whole(u.shape),
            sort_columns(w_sort),
            whole(partner.shape),
            whole(steps.shape),
            *[whole(part.shape) for part in d_bias],
        ],
        out_specs=[whole((blocks, width)), whole((width, 2 * SORT))],
        out_shape=[
            jax.ShapeDtypeStruct((blocks, width), f32),
            jax.ShapeDtypeStruct((width, 2 * SORT), f32),
        ],
        grid=(1,),
        compiler_params=params(),
        cost_estimate=pl.CostEstimate(flops=10**8, bytes_accessed=10**7, transcendentals=10**6),
        name="sort_back",
    )(lens, u, w_sort, partner, steps, *d_bias)


def lane_block(rows):
    return (iota((rows, 2 * GROUP), 1) % GROUP) // BLOCK


def compact(full):
    at = lane_block(BLOCK)
    part = [full[c * BLOCK : (c + 1) * BLOCK] for c in range(GROUP // BLOCK)]
    return jnp.where(
        at < 2,
        jnp.where(at < 1, part[0], part[1]),
        jnp.where(at < 3, part[2], part[3]),
    )


def diagonal_mask():
    rows = 2 * GROUP
    return jnp.where((iota((rows, rows), 0) % GROUP) // BLOCK == lane_block(rows), 1.0, 0.0).astype(bf16)


def spread(own, far, mask):
    own, far = own.astype(bf16), far.astype(bf16)
    times = GROUP // BLOCK
    return jnp.concatenate([own] * times + [far] * times, axis=0) * mask


def head_stack(pair, lanes):
    zero = jnp.zeros_like(pair)
    return jnp.concatenate(
        [jnp.where(lanes < HEAD, pair, zero), jnp.where(lanes < HEAD, zero, pair)], axis=0
    )


def head_lanes():
    return iota((GROUP, LANES), 1)


def by_lane(values):
    at = iota((1, GROUP), 1) // BLOCK
    return jnp.where(
        at < 2,
        jnp.where(at < 1, values[0], values[1]),
        jnp.where(at < 3, values[2], values[3]),
    )


def gather_far(dst, src, partners):
    for c, p in enumerate(partners):
        dst[GROUP + c * BLOCK : GROUP + (c + 1) * BLOCK, :] = src[pl.ds(pl.multiple_of(p * BLOCK, BLOCK), BLOCK), :]


def attend_kernel(lens, partner, bias, q_ref, k_ref, v_ref, o_ref, p_ref, mask_ref, *, slot):
    tile, width = q_ref.shape
    step = pl.program_id(0)
    pairs = width // LANES
    per = GROUP // BLOCK

    @pl.when(step == 0)
    def _():
        mask_ref[...] = diagonal_mask()

    ends = ends_of(lens, slot)
    scale = 1.0 / math.sqrt(HEAD)

    def some_groups(turn, carry):
        mask = mask_ref[...]
        lanes = head_lanes()
        key = iota((BLOCK, GROUP), 0)
        query = iota((BLOCK, GROUP), 1)
        work = []
        for part in range(ABREAST):
            g = turn * ABREAST + part
            first = step * (tile // BLOCK) + g * per
            partners = [partner[0, first + c] for c in range(per)]
            rows = pl.ds(pl.multiple_of(first * BLOCK, GROUP), GROUP)
            q_rows = pl.ds(pl.multiple_of(g * GROUP, GROUP), GROUP)
            spans = [rows] + [pl.ds(pl.multiple_of(p * BLOCK, BLOCK), BLOCK) for p in partners]
            own_place = (first + query // BLOCK) * BLOCK + key
            far_place = by_lane(partners) * BLOCK + key
            own_live = (own_place < end_at(own_place, ends, slot)) | (query % BLOCK == key)
            far_live = far_place < end_at(far_place, ends, slot)
            own_live = jnp.concatenate([own_live.astype(f32)] * 2, axis=1) > 0.5
            far_live = jnp.concatenate([far_live.astype(f32)] * 2, axis=1) > 0.5
            lane_bias = by_lane([bias[0, first + c] for c in range(per)])
            lane_bias = jnp.concatenate([lane_bias] * 2, axis=1)
            for pair in range(pairs):
                work.append((g, pair, spans, q_rows, own_live, far_live, lane_bias))
        scores = []
        for g, pair, spans, q_rows, *_ in work:
            cols = slice(pair * LANES, (pair + 1) * LANES)
            q_two = head_stack(q_ref[q_rows, cols], lanes)
            k_all = jnp.concatenate([k_ref[at, cols] for at in spans], axis=0)
            scores.append(dot_nt(k_all, q_two))
        probs = []
        for score, (g, pair, spans, q_rows, own_live, far_live, lane_bias) in zip(scores, work):
            own = jnp.where(own_live, compact(score[:GROUP]) * scale, masked)
            far = jnp.where(far_live, compact(score[GROUP:]) * scale + lane_bias, masked)
            top = jnp.maximum(
                jnp.max(own, axis=0, keepdims=True), jnp.max(far, axis=0, keepdims=True)
            )
            own = jnp.exp(own - top)
            far = jnp.exp(far - top)
            total = jnp.sum(own, axis=0, keepdims=True) + jnp.sum(far, axis=0, keepdims=True)
            inverse = 1.0 / total
            probs.append(((own * inverse).astype(bf16), (far * inverse).astype(bf16)))
        mixes = []
        for (own, far), (g, pair, spans, *_) in zip(probs, work):
            cols = slice(pair * LANES, (pair + 1) * LANES)
            v_all = jnp.concatenate([v_ref[at, cols] for at in spans], axis=0)
            mixes.append(dot(v_all.T, spread(own, far, mask)))
        for mixed, (own, far), (g, pair, spans, q_rows, *_) in zip(mixes, probs, work):
            at = pl.multiple_of(g * 2 * BLOCK, 2 * BLOCK)
            p_ref[pair, pl.ds(at, BLOCK), :] = own
            p_ref[pair, pl.ds(at + BLOCK, BLOCK), :] = far
            o_ref[pair * LANES : pair * LANES + HEAD, q_rows] = mixed[:HEAD, :GROUP].astype(bf16)
            o_ref[pair * LANES + HEAD : (pair + 1) * LANES, q_rows] = mixed[HEAD:, GROUP:].astype(bf16)
        return carry

    lax.fori_loop(0, tile // GROUP // ABREAST, some_groups, 0)


def attend(lens, partner, bias, q, k, v):
    slot, width = q.shape
    grid = slot // TILE
    pairs, per_tile = width // LANES, (TILE // GROUP) * 2 * BLOCK
    return pl.pallas_call(
        functools.partial(attend_kernel, slot=slot),
        grid=(grid,),
        in_specs=[
            smem(),
            smem(),
            smem(),
            pl.BlockSpec((TILE, width), lambda i: (i, 0)),
            whole(k.shape),
            whole(v.shape),
        ],
        out_specs=[
            pl.BlockSpec((width, TILE), lambda i: (0, i)),
            pl.BlockSpec((pairs, per_tile, 2 * GROUP), lambda i: (0, i, 0)),
        ],
        out_shape=[
            jax.ShapeDtypeStruct((width, slot), bf16),
            jax.ShapeDtypeStruct((pairs, grid * per_tile, 2 * GROUP), bf16),
        ],
        scratch_shapes=[
            pltpu.VMEM((2 * GROUP, 2 * GROUP), bf16),
        ],
        compiler_params=params(),
        cost_estimate=pl.CostEstimate(
            flops=20 * 10**9, bytes_accessed=slot * width * 10, transcendentals=slot * 512
        ),
        name="attend",
    )(lens, partner, bias, q, k, v)


def attend_back_kernel(
    partner, q_ref, do_ref, p_ref, k_ref, v_ref,
    dq_ref, dk_ref, dv_ref, db_ref,
    mask_ref, dk_sum, dv_sum, db_sum,
):
    tile = q_ref.shape[0]
    step = pl.program_id(0)
    per = GROUP // BLOCK

    @pl.when(step == 0)
    def _():
        mask_ref[...] = diagonal_mask()
        dk_sum[...] = jnp.zeros_like(dk_sum)
        dv_sum[...] = jnp.zeros_like(dv_sum)

    scale = 1.0 / math.sqrt(HEAD)
    lanes = head_lanes()
    mask = mask_ref[...]
    work, d_probs, seconds, thirds = [], [], [], []
    for g in range(tile // GROUP):
        first = step * (tile // BLOCK) + g * per
        partners = [partner[0, first + c] for c in range(per)]
        rows = pl.ds(pl.multiple_of(first * BLOCK, GROUP), GROUP)
        spans = [rows] + [pl.ds(pl.multiple_of(p * BLOCK, BLOCK), BLOCK) for p in partners]
        q_rows = slice(g * GROUP, (g + 1) * GROUP)
        q_two = head_stack(q_ref[q_rows, :], lanes)
        do_two = head_stack(do_ref[q_rows, :], lanes)
        v_all = jnp.concatenate([v_ref[at, :] for at in spans], axis=0)
        work.append((g, spans, q_rows, q_two, do_two))
        d_probs.append(dot_nt(v_all, do_two))
    for d_prob, (g, *_) in zip(d_probs, work):
        at = g * 2 * BLOCK
        own_b = p_ref[0, at : at + BLOCK, :]
        far_b = p_ref[0, at + BLOCK : at + 2 * BLOCK, :]
        own, far = own_b.astype(f32), far_b.astype(f32)
        d_own, d_far = compact(d_prob[:GROUP]), compact(d_prob[GROUP:])
        delta = jnp.sum(own * d_own, axis=0, keepdims=True) + jnp.sum(
            far * d_far, axis=0, keepdims=True
        )
        d_own = own * (d_own - delta)
        d_far = far * (d_far - delta)
        d_bias = jnp.sum(d_far, axis=0, keepdims=True)
        db_sum[pl.ds(step * (tile // GROUP) + g, 1), :] = d_bias[:, :GROUP] + d_bias[:, GROUP:]
        seconds.append((spread(d_own * scale, d_far * scale, mask), spread(own_b, far_b, mask)))
    for (d_scores, prob), (g, spans, q_rows, q_two, do_two) in zip(seconds, work):
        k_all = jnp.concatenate([k_ref[at, :] for at in spans], axis=0)
        thirds.append((dot(d_scores, q_two), dot(prob, do_two), dot(k_all.T, d_scores)))
    for (dk, dv, dq), (g, spans, q_rows, *_) in zip(thirds, work):
        dq = jnp.concatenate([dq[:HEAD, :GROUP], dq[HEAD:, GROUP:]], axis=0)
        dq_ref[q_rows, :] = dq.T.astype(bf16)
        dk_sum[spans[0], :] += dk[:GROUP]
        dv_sum[spans[0], :] += dv[:GROUP]
        for c in range(per):
            here = slice(GROUP + c * BLOCK, GROUP + (c + 1) * BLOCK)
            dk_sum[spans[1 + c], :] += dk[here]
            dv_sum[spans[1 + c], :] += dv[here]

    @pl.when(step == pl.num_programs(0) - 1)
    def _():
        dk_ref[...] = dk_sum[...].astype(bf16)
        dv_ref[...] = dv_sum[...].astype(bf16)
        groups = db_sum.shape[0]
        blocks = groups * per
        pick = (iota((GROUP, blocks), 0) // BLOCK == iota((GROUP, blocks), 1) % per).astype(f32)
        sums = dot(db_sum[...], pick, highest)
        mine = iota((groups, blocks), 1) // per == iota((groups, blocks), 0)
        db_ref[...] = jnp.sum(jnp.where(mine, sums, 0.0), axis=0, keepdims=True)


def attend_back(pair, partner, q, d_o, probs, k, v):
    slot = q.shape[0]
    grid = slot // WIDE
    per_tile = (WIDE // GROUP) * 2 * BLOCK
    row = pl.BlockSpec((WIDE, LANES), lambda i: (i, pair))
    once = pl.BlockSpec((slot, LANES), lambda i: (0, pair), pipeline_mode=pl.Buffered(1))
    out = jax.ShapeDtypeStruct((slot, LANES), bf16)
    return pl.pallas_call(
        attend_back_kernel,
        grid=(grid,),
        in_specs=[
            smem(),
            row,
            row,
            pl.BlockSpec((1, per_tile, 2 * GROUP), lambda i: (pair, i, 0)),
            once,
            once,
        ],
        out_specs=[
            pl.BlockSpec((WIDE, LANES), lambda i: (i, 0)),
            whole((slot, LANES)),
            whole((slot, LANES)),
            whole((1, slot // BLOCK)),
        ],
        out_shape=[out, out, out, jax.ShapeDtypeStruct((1, slot // BLOCK), f32)],
        scratch_shapes=[
            pltpu.VMEM((2 * GROUP, 2 * GROUP), bf16),
            pltpu.VMEM((slot, LANES), f32),
            pltpu.VMEM((slot, LANES), f32),
            pltpu.VMEM((slot // GROUP, GROUP), f32),
        ],
        compiler_params=params(),
        cost_estimate=pl.CostEstimate(
            flops=10 * 10**9, bytes_accessed=slot * LANES * 16, transcendentals=0
        ),
        name="attend_back",
    )(partner, q, d_o, probs, k, v)


def ffn_kernel(
    place, x_ref, dy_ref, o_ref, norms_ref, w_ref,
    out_ref, dx_ref, do_ref, sent_ref, kept_ref, g_norm_ref,
    g_ref, h_scr, ht_scr, dyt_scr, y_scr, dh_scr, hat_scr, gt_scr,
):
    tile, width = x_ref.shape
    hidden = gt_scr.shape[1]
    slabs = hidden // width
    parts = width // ROWS
    whole_rows = slice(slabs * ROWS, (slabs + 1) * ROWS)
    out_rows = slice((slabs + 1) * ROWS, (2 * slabs + 1) * ROWS)
    step = pl.program_id(0)

    share = parts // slabs
    fresh = step == 0

    def add_to(ref, at, value):
        ref[at] = value + jnp.where(fresh, 0.0, ref[at])

    root = math.sqrt(2.0 / math.pi)
    w_in = [w_ref[:, c * ROWS : (c + 1) * ROWS, :].reshape(width, width) for c in range(slabs)]
    w_out = [
        w_ref[c * share : (c + 1) * share, out_rows, :].reshape(width, width) for c in range(slabs)
    ]
    w_o = w_ref[:, whole_rows, :].reshape(width, width)

    def d_hidden(c):
        return dot_nt(dy_ref[...], w_out[c])

    def between(act, d_hid):
        square = act * act
        curve = jnp.tanh(act * (root + (root * 0.044715) * square))
        gate = 0.5 + 0.5 * curve
        hid = act * gate
        slope = gate + hid * (1.0 - curve) * (root + (3.0 * root * 0.044715) * square)
        return hid.astype(bf16), (d_hid * slope).astype(bf16)

    o_t = o_ref[...]
    x_one = x_ref[...].astype(f32) + dot(o_t.T, w_o)
    d_hid = d_hidden(0)
    dyt_scr[...] = dy_ref[...].T
    hat, rstd = norm_stats(x_one)
    h_two = (hat * norms_ref[2:3, :] + norms_ref[3:4, :]).astype(bf16)
    h_scr[...] = h_two
    hat_scr[...] = hat
    y_scr[...] = x_one
    act = dot(h_scr[...], w_in[0])
    ht_scr[...] = h_two.T
    for c in range(slabs):
        this_act, this_d = act, d_hid
        if c + 1 < slabs:
            d_hid = d_hidden(c + 1)
            act = dot(h_scr[...], w_in[c + 1])
        hid, d_act = between(this_act, this_d)
        more = dot_nt(d_act, w_in[c])
        dh_scr[...] = more if c == 0 else dh_scr[...] + more
        y_scr[...] += dot(hid, w_out[c])
        cols = slice(c * width, (c + 1) * width)
        add_to(gt_scr, (slice(None), cols), dot(dyt_scr[...], hid))
        slab = (slice(None), slice(c * ROWS, (c + 1) * ROWS), slice(None))
        add_to(g_ref, slab, dot(ht_scr[...], d_act).reshape(parts, ROWS, width))
    d_h = dh_scr[...]
    hat = hat_scr[...]
    d_x = dy_ref[...].astype(f32) + norm_back(d_h, hat, rstd, norms_ref[2:3, :])
    dx_ref[...] = d_x
    d_z = d_x.astype(bf16)
    do_ref[...] = dot_nt(d_z, w_o).astype(bf16)
    add_to(g_ref, (slice(None), whole_rows, slice(None)), dot(o_t, d_z).reshape(parts, ROWS, width))
    add_to(g_norm_ref, (slice(2, 3), slice(None)), jnp.sum(d_h * hat, axis=0, keepdims=True))
    add_to(g_norm_ref, (slice(3, 4), slice(None)), jnp.sum(d_h, axis=0, keepdims=True))
    out_ref[...] = y_scr[...].astype(bf16)

    @pl.when(fresh)
    def _():
        g_norm_ref[0:2, :] = jnp.zeros_like(g_norm_ref[0:2, :])
        g_norm_ref[4:, :] = jnp.zeros_like(g_norm_ref[4:, :])

    @pl.when(step == pl.num_programs(0) - 1)
    def _():
        for c in range(slabs):
            g_ref[c * share : (c + 1) * share, out_rows, :] = gt_scr[
                :, c * width : (c + 1) * width
            ].T.reshape(share, slabs * ROWS, width)
        halves(place, sent_ref, kept_ref, lambda i: g_ref[i])


def halves(place, sent_ref, kept_ref, block):
    mine = place[0] & 1

    def one(i, carry):
        sent_ref[i] = block(2 * i + 1 - mine).astype(bf16)
        kept_ref[i] = block(2 * i + mine)
        return carry

    lax.fori_loop(0, sent_ref.shape[0], one, 0)


def ffn(place, x, dy, o_t, norms, w_two):
    slot, width = x.shape
    hidden = (w_two.shape[1] // ROWS - 1) // 2 * width
    grid = slot // TILE
    half = (w_two.shape[0] // 2, *w_two.shape[1:])
    row = pl.BlockSpec((TILE, width), lambda i: (i, 0))

    def once(shape):
        return pl.BlockSpec(shape, lambda i: (0,) * len(shape), pipeline_mode=pl.Buffered(1))

    return pl.pallas_call(
        ffn_kernel,
        grid=(grid,),
        in_specs=[
            smem(),
            row,
            row,
            pl.BlockSpec((width, TILE), lambda i: (0, i)),
            once(norms.shape),
            once(w_two.shape),
        ],
        out_specs=[row, row, row, once(half), once(half), once((8, width))],
        out_shape=[
            jax.ShapeDtypeStruct((slot, width), bf16),
            jax.ShapeDtypeStruct((slot, width), f32),
            jax.ShapeDtypeStruct((slot, width), bf16),
            jax.ShapeDtypeStruct(half, bf16),
            jax.ShapeDtypeStruct(half, f32),
            jax.ShapeDtypeStruct((8, width), f32),
        ],
        scratch_shapes=[
            pltpu.VMEM(w_two.shape, f32),
            pltpu.VMEM((TILE, width), bf16),
            pltpu.VMEM((width, TILE), bf16),
            pltpu.VMEM((width, TILE), bf16),
            pltpu.VMEM((TILE, width), f32),
            pltpu.VMEM((TILE, width), f32),
            pltpu.VMEM((TILE, width), f32),
            pltpu.VMEM((width, hidden), f32),
        ],
        compiler_params=params(),
        cost_estimate=pl.CostEstimate(
            flops=2 * slot * width * (3 * width + 6 * hidden),
            bytes_accessed=slot * width * 14,
            transcendentals=slot * hidden,
        ),
        name="ffn",
    )(place, x, dy, o_t, norms, w_two)


def project_back_kernel(
    place, lens, x_ref, dx_ref, du_ref, norms_ref, w_ref, g_sort_ref, g_two_ref, *refs, slot
):
    *d_refs, grad_ref, sent_ref, kept_ref, g_ref, g_norm_ref = refs
    tile, width = x_ref.shape
    step = pl.program_id(0)

    @pl.when(step == 0)
    def _():
        g_ref[...] = jnp.zeros_like(g_ref)
        g_norm_ref[...] = jnp.zeros_like(g_norm_ref)

    pairs = width // LANES
    ends = ends_of(lens, slot)
    blocks = SUB // BLOCK
    starts = range(0, tile, SUB)
    d_hs, hats, rstds, h_ones = [], [], [], []
    for r in starts:
        rows = slice(r, r + SUB)
        places = step * tile + r + iota((SUB, 1), 0)
        live = places < end_at(places, ends, slot)
        d_u = du_ref[r // BLOCK : r // BLOCK + blocks, :].reshape(blocks, 1, width)
        d_h = jnp.broadcast_to(d_u, (blocks, BLOCK, width)).reshape(SUB, width)
        d_h = jnp.where(live, d_h, 0.0)
        for part in range(3):
            cols = slice(part * width, (part + 1) * width)
            d_part = jnp.concatenate(
                [ref[rows, :] for ref in d_refs[part * pairs : (part + 1) * pairs]], axis=1
            )
            d_h = d_h + dot_nt(d_part, w_ref[:, cols])
        d_hs.append(d_h)
        hat, rstd = norm_stats(x_ref[rows, :].astype(f32))
        hats.append(hat)
        rstds.append(rstd)
        h_ones.append((hat * norms_ref[0:1, :] + norms_ref[1:2, :]).astype(bf16))
    h_one = jnp.concatenate(h_ones, axis=0)

    def back(at):
        rows = slice(at * SUB, (at + 1) * SUB)
        g_norm_ref[0:1, :] += jnp.sum(d_hs[at] * hats[at], axis=0, keepdims=True)
        g_norm_ref[1:2, :] += jnp.sum(d_hs[at], axis=0, keepdims=True)
        grad_ref[rows, :] = dx_ref[rows, :] + norm_back(
            d_hs[at], hats[at], rstds[at], norms_ref[0:1, :]
        )

    done = 0
    for part in range(3):
        cols = slice(part * width, (part + 1) * width)
        d_part = jnp.concatenate([ref[...] for ref in d_refs[part * pairs : (part + 1) * pairs]], axis=1)
        g_ref[:, cols] += dot_tn(h_one, d_part)
        until = len(starts) * (part + 1) // 3
        for at in range(done, until):
            back(at)
        done = until

    @pl.when(step == pl.num_programs(0) - 1)
    def _():
        g_ref[:, 3 * width : 3 * width + LANES] = g_sort_ref[...]
        small = g_norm_ref[...] + g_two_ref[...]
        rest = jnp.zeros((LANES - small.shape[0], width), f32)
        g_ref[:, 3 * width + LANES :] = jnp.concatenate([small, rest], axis=0).T
        rows = sent_ref.shape[1]
        halves(
            place,
            sent_ref,
            kept_ref,
            lambda i: g_ref[pl.ds(pl.multiple_of(i * rows, rows), rows), :],
        )


def project_back(place, lens, x, d_x, d_q, d_k, d_v, d_u, norms, w_one, g_sort, g_two):
    slot, width = x.shape
    grid = slot // WIDE
    row = pl.BlockSpec((WIDE, width), lambda i: (i, 0))
    half = (width // ROWS // 2, ROWS, w_one.shape[1])

    def once(shape):
        return pl.BlockSpec(shape, lambda i: (0,) * len(shape), pipeline_mode=pl.Buffered(1))

    return pl.pallas_call(
        functools.partial(project_back_kernel, slot=slot),
        grid=(grid,),
        in_specs=[
            smem(),
            smem(),
            row,
            row,
            pl.BlockSpec((WIDE // BLOCK, width), lambda i: (i, 0)),
            once(norms.shape),
            once(w_one.shape),
            once(g_sort.shape),
            once(g_two.shape),
        ]
        + [pl.BlockSpec((WIDE, LANES), lambda i: (i, 0))] * (3 * width // LANES),
        out_specs=[row, once(half), once(half)],
        out_shape=[
            jax.ShapeDtypeStruct((slot, width), f32),
            jax.ShapeDtypeStruct(half, bf16),
            jax.ShapeDtypeStruct(half, f32),
        ],
        scratch_shapes=[pltpu.VMEM(w_one.shape, f32), pltpu.VMEM((8, width), f32)],
        compiler_params=params(),
        cost_estimate=pl.CostEstimate(
            flops=2 * slot * width * 6 * width, bytes_accessed=slot * width * 18, transcendentals=0
        ),
        name="project_back",
    )(place, lens, x, d_x, d_u, norms, w_one, g_sort, g_two, *d_q, *d_k, *d_v)


def pack_kernel(wqkv, wo, wsort, win, wout, norms_t, one_ref, two_ref):
    rows, wide = wqkv.shape
    width = wo.shape[1]
    one_ref[:, :wide] = wqkv[...].astype(bf16)
    one_ref[:, wide : wide + LANES] = wsort[...].astype(bf16)
    few = norms_t.shape[0]
    tall = jnp.concatenate([norms_t[...], jnp.zeros((LANES - few, rows), f32)], axis=0)
    one_ref[:, wide + LANES :] = tall.T.astype(bf16)
    slabs = win.shape[1] // width
    for c in range(slabs):
        two_ref[c * rows : (c + 1) * rows, :] = win[:, c * width : (c + 1) * width].astype(bf16)
    two_ref[slabs * rows : (slabs + 1) * rows, :] = wo[...].astype(bf16)
    two_ref[(slabs + 1) * rows :, :] = wout[...].astype(bf16)


def pack(masters):
    wqkv, wo, wsort, win, wout, norms = masters
    rows = wqkv.shape[0]
    return pl.pallas_call(
        pack_kernel,
        out_shape=[
            jax.ShapeDtypeStruct((rows, wqkv.shape[1] + 2 * LANES), bf16),
            jax.ShapeDtypeStruct((rows * (win.shape[1] // wo.shape[1] + 1) + wout.shape[0], wo.shape[1]), bf16),
        ],
        compiler_params=params(),
        name="pack",
    )(wqkv, wo, wsort, win, wout, norms.T)


def adamw_kernel(one_kept, one_came, two_kept, two_came, *refs):
    one_ref = one_kept[...] + one_came[...].astype(f32)
    two_ref = two_kept[...] + two_came[...].astype(f32)
    masters, moments, squares, outs = refs[:6], refs[6:12], refs[12:18], refs[18:]
    rows, width = masters[1].shape
    wide = masters[0].shape[1]
    slabs = masters[3].shape[1] // width
    few = masters[5].shape[0]
    norm_grad = one_ref[:, wide + LANES :].T[:few, :]
    grads = (
        one_ref[:, :wide],
        two_ref[slabs * rows : (slabs + 1) * rows, :],
        one_ref[:, wide : wide + LANES],
        jnp.concatenate([two_ref[c * rows : (c + 1) * rows, :] for c in range(slabs)], axis=1),
        two_ref[(slabs + 1) * rows :, :],
        norm_grad,
    )
    for i in range(6):
        weight, grad = masters[i][...], grads[i]
        moment = beta_one * moments[i][...] + (1.0 - beta_one) * grad
        square = beta_two * squares[i][...] + (1.0 - beta_two) * grad * grad
        m_hat = moment / (1.0 - beta_one**STEP)
        s_hat = square / (1.0 - beta_two**STEP)
        outs[3 * i][...] = weight - rates[i] * (
            m_hat / (jnp.sqrt(s_hat) + adam_eps) + decay * weight
        )
        outs[3 * i + 1][...] = moment
        outs[3 * i + 2][...] = square


def adamw(one, two, masters, moments, squares):
    flip = lambda group: (*group[:5], group[5].T)
    args = (*one, *two, *flip(masters), *flip(moments), *flip(squares))
    shapes = [a.shape for a in flip(masters)]
    outs = pl.pallas_call(
        adamw_kernel,
        out_shape=[jax.ShapeDtypeStruct(shape, f32) for shape in shapes for _ in range(3)],
        compiler_params=params(),
        name="adamw",
    )(*args)
    return (*outs[:15], *[o.T for o in outs[15:]])


def regroup(gathered, size, rows, slabs):
    if rows == ROWS:
        return gathered
    times = ROWS // rows
    width = gathered.shape[-1]
    block = gathered.reshape(size // times, times, 2 * slabs + 1, rows, width)
    inner = block[:, :, : slabs + 1].transpose(0, 2, 1, 3, 4)
    outer = block[:, :, slabs + 1 :]
    return jnp.concatenate(
        [
            inner.reshape(size // times, (slabs + 1) * ROWS, width),
            outer.reshape(size // times, slabs * ROWS, width),
        ],
        axis=1,
    )


def device_halves(place, sent, kept, size, rows, slabs):
    if rows == ROWS:
        return sent, kept
    mine = place[0] & 1
    low = jnp.where(mine == 0, kept, sent.astype(f32))
    high = jnp.where(mine == 0, sent.astype(f32), kept)
    grads = jnp.stack([low, high], axis=1).reshape((-1,) + kept.shape[1:])
    times = ROWS // rows
    width = grads.shape[-1]
    cut = (slabs + 1) * ROWS
    inner = grads[:, :cut].reshape(size // times, slabs + 1, times, rows, width)
    outer = grads[:, cut:].reshape(size // times, times, slabs, rows, width)
    block = jnp.concatenate([inner.transpose(0, 2, 1, 3, 4), outer], axis=2)
    block = block.reshape(size // 2, 2, (2 * slabs + 1) * rows, width)
    sent = lax.dynamic_index_in_dim(block, 1 - mine, 1, keepdims=False).astype(bf16)
    return sent, lax.dynamic_index_in_dim(block, mine, 1, keepdims=False)


def swap(value, bit, size):
    return lax.ppermute(value, "dp", [(i, i ^ (1 << bit)) for i in range(size)])


def gather(block, size):
    count = size.bit_length() - 1
    place = lax.axis_index("dp")
    held = block.reshape((1,) * count + block.shape)
    for bit in reversed(range(count)):
        axis = count - 1 - bit
        came = swap(held, bit, size)
        upper = ((place >> bit) & 1) == 1
        held = jnp.concatenate(
            [jnp.where(upper, came, held), jnp.where(upper, held, came)], axis=axis
        )
    return held.reshape((size * block.shape[0],) + block.shape[1:])


def pick(value, bit, index, lead):
    return lax.dynamic_index_in_dim(value, index, lead.index(bit), keepdims=False)


class ScatterSum:
    def __init__(self, sent, kept, size, axis):
        self.size, self.count = size, size.bit_length() - 1
        self.axis = axis
        self.bits = list(range(self.count - 1, 0, -1))
        self.place = lax.axis_index("dp")
        self.rest = kept.shape[1:]
        lead = (2,) * (self.count - 1)
        self.kept = [(kept.reshape(lead + self.rest), self.bits)]
        self.came = [swap(sent, 0, size).reshape(lead + self.rest)]
        self.plan = [(1, 2), (2, 1)] + [(bit,) for bit in range(3, self.count)]

    def step(self):
        bits = self.plan.pop(0)
        parts = []
        if len(bits) > len(self.kept):
            kept, lead = self.kept[0]
            middle = len(lead) + self.axis
            cut = kept.shape[middle] // 2
            for turn in range(2):
                at = (slice(None),) * middle + (slice(turn * cut, (turn + 1) * cut),)
                parts.append((kept[at], self.came[0][at], lead))
        elif len(bits) < len(self.kept):
            lead = self.kept[0][1]
            middle = len(lead) + self.axis
            parts = [
                (
                    jnp.concatenate([kept for kept, _ in self.kept], axis=middle),
                    jnp.concatenate(self.came, axis=middle),
                    lead,
                )
            ]
        else:
            parts = [(kept, came, lead) for (kept, lead), came in zip(self.kept, self.came)]
        self.kept, self.came, self.sent = [], [], []
        for bit, (kept, came, lead) in zip(bits, parts):
            mine = (self.place >> bit) & 1
            self.sent.append(
                (pick(kept, bit, 1 - mine, lead) + pick(came, bit, 1 - mine, lead).astype(f32)).astype(bf16)
            )
            left = [b for b in lead if b != bit]
            self.kept.append((pick(kept, bit, mine, lead) + pick(came, bit, mine, lead).astype(f32), left))
        self.bits = bits

    def send(self):
        self.came = [swap(sent, bit, self.size) for sent, bit in zip(self.sent, self.bits)]

    def after(self, values):
        self.came, values = lax.optimization_barrier((self.came, values))
        return values

    def before(self, values):
        self.sent, values = lax.optimization_barrier((self.sent, values))
        return values

    def last(self):
        return self.kept[0][0].reshape(self.rest), self.came[0].reshape(self.rest)


def body(size, x, dy, lens, partner, *state):
    slot, width = x.shape
    masters, moments, squares = state[:6], state[6:12], state[12:]
    rows = masters[0].shape[0]
    slabs = masters[3].shape[1] // width
    place = lax.axis_index("dp").astype(jnp.int32).reshape((1,))
    pack_one, pack_two = pack(masters)
    w_one = gather(pack_one, size)
    w_two = regroup(lax.all_gather(pack_two, "dp", axis=0), size, rows, slabs)

    q, k, v, u, norms = project(lens, x, w_one)
    bias, steps = sort_net(lens, u, w_one, partner, slot)
    o_t, probs = attend(lens, partner, bias, q, k, v)
    out, d_x, d_o, sent, kept, g_two = ffn(place, x, dy, o_t, norms, w_two)
    sent, kept = device_halves(place, sent, kept, size, rows, slabs)
    two = ScatterSum(sent, kept, size, 0)

    def back(pair):
        return attend_back(pair, partner, q, d_o, probs, k, v)

    back_0 = two.after(back(0))
    two.step()
    q, d_o = two.before((q, d_o))
    two.send()
    back_1 = back(1)
    back_2 = back(2)
    back_1, back_2 = two.after((back_1, back_2))
    two.step()
    q, d_o = two.before((q, d_o))
    two.send()
    back_3 = two.after(back(3))
    two.step()
    u, back_3 = two.before((u, back_3))
    two.send()
    d_q, d_k, d_v, d_bias = zip(back_0, back_1, back_2, back_3)
    d_u, g_sort = two.after(sort_back(lens, u, w_one, partner, d_bias, steps, slot))
    while two.plan:
        two.step()
        d_u = two.before(d_u)
        two.send()
    grad_in, sent, kept = project_back(
        place, lens, x, d_x, d_q, d_k, d_v, d_u, norms, w_one, g_sort, g_two
    )
    grad_in, sent, kept = two.after((grad_in, sent, kept))
    sent, kept = device_halves(place, sent, kept, size, rows, 0)
    one = ScatterSum(sent, kept, size, 1)
    while one.plan:
        one.step()
        one.send()
    outs = adamw(one.last(), two.last(), masters, moments, squares)
    return (out, grad_in, *outs)


def solution(mesh):
    spec = P("dp", None)
    return jax.shard_map(
        functools.partial(body, mesh.shape["dp"]),
        mesh=mesh,
        in_specs=(spec,) * 22,
        out_specs=(spec,) * 20,
        check_vma=False,
    )
```

```python
import functools
import math

import jax
import jax.numpy as jnp
from jax import lax
from jax.experimental import pallas as pl
from jax.experimental.pallas import tpu as pltpu
from jax.sharding import PartitionSpec as P

HEADS = 8
HEAD = 64
SORT = 64
BLOCK = 32
SINK = 8
STEP = 10
TILE = 512
WIDE = 1024
ROWS = 16
ABREAST = 4
SUB = 256
GROUP = 128
LANES = 128

highest = lax.Precision.HIGHEST
masked = -1000000000.0
norm_eps = 1e-05
beta_one = 0.9
beta_two = 0.999
adam_eps = 1e-08
decay = 0.01
rates = (0.05, 0.15, 0.05, 0.05, 0.025, 0.5)
f32 = jnp.float32
bf16 = jnp.bfloat16


def dot(left, right, precision=None):
    return jnp.dot(left, right, precision=precision, preferred_element_type=f32)


def dot_nt(left, right, precision=None):
    return lax.dot_general(
        left, right, (((1,), (1,)), ((), ())), precision=precision, preferred_element_type=f32
    )


def dot_tn(left, right, precision=None):
    return lax.dot_general(
        left, right, (((0,), (0,)), ((), ())), precision=precision, preferred_element_type=f32
    )


def iota(shape, axis):
    return lax.broadcasted_iota(jnp.int32, shape, axis)


def ends_of(lens, slot):
    quarter = slot // 4
    is_long = lens[0, 0] > quarter
    return [jnp.where(is_long, lens[0, 0], k * quarter + lens[0, k]) for k in range(4)]


def end_at(places, ends, slot):
    quarter = slot // 4
    return jnp.where(
        places < 2 * quarter,
        jnp.where(places < quarter, ends[0], ends[1]),
        jnp.where(places < 3 * quarter, ends[2], ends[3]),
    )


def norm_stats(value):
    center = value - jnp.mean(value, axis=-1, keepdims=True)
    spread = jnp.mean(center * center, axis=-1, keepdims=True)
    rstd = lax.rsqrt(spread + norm_eps)
    return center * rstd, rstd


def norm_back(grad, hat, rstd, gain):
    d_hat = grad * gain
    mean_d = jnp.mean(d_hat, axis=-1, keepdims=True)
    mean_dh = jnp.mean(d_hat * hat, axis=-1, keepdims=True)
    return rstd * (d_hat - mean_d - hat * mean_dh)


def params(limit=56 << 20):
    return pltpu.CompilerParams(vmem_limit_bytes=limit)


def whole(shape):
    return pl.BlockSpec(shape, lambda *_: (0,) * len(shape))


def smem():
    return pl.BlockSpec(memory_space=pltpu.SMEM)


def project_kernel(
    place, lens, x_ref, near_ref, far_ref, q_ref, k_ref, v_ref, u_ref, norms_ref, w_ref, *, slot
):
    tile, width = x_ref.shape
    base = pl.program_id(0) * tile

    @pl.when(pl.program_id(0) == 0)
    def _():
        rows = near_ref.shape[1]
        mine = place[0] & 1
        for half in range(near_ref.shape[0]):
            at = (place[0] >> 1) ^ half
            w_ref[2 * half * rows : (2 * half + 1) * rows, :] = jnp.where(
                mine == 0, near_ref[at], far_ref[at]
            )
            w_ref[(2 * half + 1) * rows : (2 * half + 2) * rows, :] = jnp.where(
                mine == 0, far_ref[at], near_ref[at]
            )

    @pl.when(pl.program_id(0) == 0)
    def _():
        norms_ref[...] = w_ref[:, 3 * width + LANES :].astype(f32).T[:8, :]

    parts = []
    for r in range(0, tile, SUB):
        hat, _ = norm_stats(x_ref[r : r + SUB, :].astype(f32))
        parts.append((hat * norms_ref[0:1, :] + norms_ref[1:2, :]).astype(bf16))
        for part, ref in enumerate((q_ref, k_ref, v_ref)):
            ref[r : r + SUB, :] = dot(parts[-1], w_ref[:, part * width : (part + 1) * width]).astype(bf16)
    h_one = jnp.concatenate(parts, axis=0)
    blocks = tile // BLOCK
    at = iota((blocks, tile), 1)
    places = at + base
    live = places < end_at(places, ends_of(lens, slot), slot)
    own = (at // BLOCK) == iota((blocks, tile), 0)
    pick = jnp.where(live & own, 1.0, 0.0).astype(bf16)
    u_ref[...] = dot(pick, h_one)


def project(place, lens, x, near, far):
    slot, width = x.shape
    w_shape = (2 * near.shape[0] * near.shape[1], near.shape[2])
    grid = slot // WIDE
    row = pl.BlockSpec((WIDE, width), lambda i: (i, 0))
    out = jax.ShapeDtypeStruct((slot, width), bf16)
    return pl.pallas_call(
        functools.partial(project_kernel, slot=slot),
        grid=(grid,),
        in_specs=[smem(), smem(), row, whole(near.shape), whole(far.shape)],
        out_specs=[
            row,
            row,
            row,
            pl.BlockSpec((WIDE // BLOCK, width), lambda i: (i, 0)),
            whole((8, width)),
            whole(w_shape),
        ],
        out_shape=[
            out,
            out,
            out,
            jax.ShapeDtypeStruct((slot // BLOCK, width), f32),
            jax.ShapeDtypeStruct((8, width), f32),
            jax.ShapeDtypeStruct(w_shape, bf16),
        ],
        compiler_params=params(),
        cost_estimate=pl.CostEstimate(
            flops=2 * slot * width * 3 * width, bytes_accessed=slot * width * 8, transcendentals=0
        ),
        name="project",
    )(place, lens, x, near, far)


def sort_parts(lens, u_ref, ws_ref, slot):
    blocks = u_ref.shape[0]
    ends = ends_of(lens, slot)
    quarter = slot // 4
    is_long = lens[0, 0] > quarter

    def group_of(axis, shape):
        index = iota(shape, axis)
        start = index * BLOCK
        live = start < end_at(start, ends, slot)
        member = jnp.where(is_long, 0, start // quarter)
        return jnp.where(live, member, 4 + index)

    same = group_of(0, (blocks, blocks)) == group_of(1, (blocks, blocks))
    start = iota((blocks, 1), 0) * BLOCK
    count = jnp.clip(end_at(start, ends, slot) - start, 0, BLOCK).astype(f32)
    scale = lax.rsqrt(jnp.maximum(count, 1.0))
    summary = u_ref[...] * scale
    w_sort = ws_ref[...].astype(f32)
    sort_q = dot(summary, w_sort[:, :SORT], highest)
    sort_k = dot(summary, w_sort[:, SORT:], highest)
    return same, scale, summary, w_sort, sort_q, sort_k


def sort_columns(w_one):
    return pl.BlockSpec((w_one.shape[0], 2 * SORT), lambda i: (0, 3 * w_one.shape[0] // (2 * SORT)))


def column_of(row, eye):
    return jnp.sum(jnp.where(eye, row, 0.0), axis=1, keepdims=True)


def sort_kernel(lens, u_ref, ws_ref, partner_ref, bias_ref, steps_ref, *, slot):
    blocks = u_ref.shape[0]
    same, _, _, _, sort_q, sort_k = sort_parts(lens, u_ref, ws_ref, slot)
    raw = dot_nt(sort_q, sort_k, highest)
    logits = jnp.where(same, raw / math.sqrt(SORT), masked)

    def normalize(value, axis):
        top = jnp.max(value, axis=axis, keepdims=True)
        return value - (top + jnp.log(jnp.sum(jnp.exp(value - top), axis=axis, keepdims=True)))

    for turn in range(SINK):
        logits = normalize(logits, 1)
        steps_ref[2 * turn] = logits
        logits = normalize(logits, 0)
        steps_ref[2 * turn + 1] = logits
    eye = iota((blocks, blocks), 0) == iota((blocks, blocks), 1)
    members = jnp.sum(same.astype(f32), axis=1, keepdims=True)
    partner = column_of(partner_ref[...].astype(f32), eye)
    pick = partner == iota((blocks, blocks), 1).astype(f32)
    bias = jnp.sum(jnp.where(pick, logits, 0.0), axis=1, keepdims=True) + jnp.log(members)
    bias_ref[...] = jnp.sum(jnp.where(eye, bias, 0.0), axis=0, keepdims=True)


def sort_net(lens, u, w_sort, partner, slot):
    blocks = u.shape[0]
    return pl.pallas_call(
        functools.partial(sort_kernel, slot=slot),
        in_specs=[smem(), whole(u.shape), sort_columns(w_sort), whole(partner.shape)],
        out_specs=[whole((1, blocks)), whole((2 * SINK, blocks, blocks))],
        out_shape=[
            jax.ShapeDtypeStruct((1, blocks), f32),
            jax.ShapeDtypeStruct((2 * SINK, blocks, blocks), f32),
        ],
        grid=(1,),
        compiler_params=params(),
        cost_estimate=pl.CostEstimate(flops=10**8, bytes_accessed=10**7, transcendentals=10**6),
        name="sort_net",
    )(lens, u, w_sort, partner)


def sort_back_kernel(
    lens, u_ref, ws_ref, partner_ref, steps_ref, *refs, slot
):
    *d_bias_refs, d_u_ref, grad_ref = refs
    blocks = u_ref.shape[0]
    same, scale, summary, w_sort, sort_q, sort_k = sort_parts(lens, u_ref, ws_ref, slot)
    eye = iota((blocks, blocks), 0) == iota((blocks, blocks), 1)
    partner = column_of(partner_ref[...].astype(f32), eye)
    pick = partner == iota((blocks, blocks), 1).astype(f32)
    d_bias = column_of(sum(ref[...] for ref in d_bias_refs), eye)
    d_logits = jnp.where(pick, d_bias, 0.0)
    for turn in reversed(range(SINK)):
        for axis, step in ((0, 2 * turn + 1), (1, 2 * turn)):
            share = jnp.exp(steps_ref[step])
            d_logits = d_logits - share * jnp.sum(d_logits, axis=axis, keepdims=True)
    d_raw = jnp.where(same, d_logits, 0.0) / math.sqrt(SORT)
    d_sort_q = dot(d_raw, sort_k, highest)
    d_sort_k = dot_tn(d_raw, sort_q, highest)
    d_sort = jnp.concatenate([d_sort_q, d_sort_k], axis=1)
    grad_ref[...] = dot_tn(summary, d_sort, highest)
    d_u_ref[...] = dot_nt(d_sort, w_sort, highest) * scale


def sort_back(lens, u, w_sort, partner, d_bias, steps, slot):
    blocks, width = u.shape
    return pl.pallas_call(
        functools.partial(sort_back_kernel, slot=slot),
        in_specs=[
            smem(),
            whole(u.shape),
            sort_columns(w_sort),
            whole(partner.shape),
            whole(steps.shape),
            *[whole(part.shape) for part in d_bias],
        ],
        out_specs=[whole((blocks, width)), whole((width, 2 * SORT))],
        out_shape=[
            jax.ShapeDtypeStruct((blocks, width), f32),
            jax.ShapeDtypeStruct((width, 2 * SORT), f32),
        ],
        grid=(1,),
        compiler_params=params(),
        cost_estimate=pl.CostEstimate(flops=10**8, bytes_accessed=10**7, transcendentals=10**6),
        name="sort_back",
    )(lens, u, w_sort, partner, steps, *d_bias)


def lane_block(rows):
    return (iota((rows, 2 * GROUP), 1) % GROUP) // BLOCK


def compact(full):
    at = lane_block(BLOCK)
    part = [full[c * BLOCK : (c + 1) * BLOCK] for c in range(GROUP // BLOCK)]
    return jnp.where(
        at < 2,
        jnp.where(at < 1, part[0], part[1]),
        jnp.where(at < 3, part[2], part[3]),
    )


def diagonal_mask():
    rows = 2 * GROUP
    return jnp.where((iota((rows, rows), 0) % GROUP) // BLOCK == lane_block(rows), 1.0, 0.0).astype(bf16)


def spread(own, far, mask):
    own, far = own.astype(bf16), far.astype(bf16)
    times = GROUP // BLOCK
    return jnp.concatenate([own] * times + [far] * times, axis=0) * mask


def head_stack(pair, lanes):
    zero = jnp.zeros_like(pair)
    return jnp.concatenate(
        [jnp.where(lanes < HEAD, pair, zero), jnp.where(lanes < HEAD, zero, pair)], axis=0
    )


def head_lanes():
    return iota((GROUP, LANES), 1)


def by_lane(values):
    at = iota((1, GROUP), 1) // BLOCK
    return jnp.where(
        at < 2,
        jnp.where(at < 1, values[0], values[1]),
        jnp.where(at < 3, values[2], values[3]),
    )


def gather_far(dst, src, partners):
    for c, p in enumerate(partners):
        dst[GROUP + c * BLOCK : GROUP + (c + 1) * BLOCK, :] = src[pl.ds(pl.multiple_of(p * BLOCK, BLOCK), BLOCK), :]


def attend_kernel(lens, partner, bias, q_ref, k_ref, v_ref, o_ref, p_ref, mask_ref, *, slot):
    tile, width = q_ref.shape
    step = pl.program_id(0)
    pairs = width // LANES
    per = GROUP // BLOCK

    @pl.when(step == 0)
    def _():
        mask_ref[...] = diagonal_mask()

    ends = ends_of(lens, slot)
    scale = 1.0 / math.sqrt(HEAD)

    def some_groups(turn, carry):
        mask = mask_ref[...]
        lanes = head_lanes()
        key = iota((BLOCK, GROUP), 0)
        query = iota((BLOCK, GROUP), 1)
        work = []
        for part in range(ABREAST):
            g = turn * ABREAST + part
            first = step * (tile // BLOCK) + g * per
            partners = [partner[0, first + c] for c in range(per)]
            rows = pl.ds(pl.multiple_of(first * BLOCK, GROUP), GROUP)
            q_rows = pl.ds(pl.multiple_of(g * GROUP, GROUP), GROUP)
            spans = [rows] + [pl.ds(pl.multiple_of(p * BLOCK, BLOCK), BLOCK) for p in partners]
            own_place = (first + query // BLOCK) * BLOCK + key
            far_place = by_lane(partners) * BLOCK + key
            own_live = (own_place < end_at(own_place, ends, slot)) | (query % BLOCK == key)
            far_live = far_place < end_at(far_place, ends, slot)
            own_live = jnp.concatenate([own_live.astype(f32)] * 2, axis=1) > 0.5
            far_live = jnp.concatenate([far_live.astype(f32)] * 2, axis=1) > 0.5
            lane_bias = by_lane([bias[0, first + c] for c in range(per)])
            lane_bias = jnp.concatenate([lane_bias] * 2, axis=1)
            for pair in range(pairs):
                work.append((g, pair, spans, q_rows, own_live, far_live, lane_bias))
        scores = []
        for g, pair, spans, q_rows, *_ in work:
            cols = slice(pair * LANES, (pair + 1) * LANES)
            q_two = head_stack(q_ref[q_rows, cols], lanes)
            k_all = jnp.concatenate([k_ref[at, cols] for at in spans], axis=0)
            scores.append(dot_nt(k_all, q_two))
        probs = []
        for score, (g, pair, spans, q_rows, own_live, far_live, lane_bias) in zip(scores, work):
            own = jnp.where(own_live, compact(score[:GROUP]) * scale, masked)
            far = jnp.where(far_live, compact(score[GROUP:]) * scale + lane_bias, masked)
            top = jnp.maximum(
                jnp.max(own, axis=0, keepdims=True), jnp.max(far, axis=0, keepdims=True)
            )
            own = jnp.exp(own - top)
            far = jnp.exp(far - top)
            total = jnp.sum(own, axis=0, keepdims=True) + jnp.sum(far, axis=0, keepdims=True)
            inverse = 1.0 / total
            probs.append(((own * inverse).astype(bf16), (far * inverse).astype(bf16)))
        mixes = []
        for (own, far), (g, pair, spans, *_) in zip(probs, work):
            cols = slice(pair * LANES, (pair + 1) * LANES)
            v_all = jnp.concatenate([v_ref[at, cols] for at in spans], axis=0)
            mixes.append(dot(v_all.T, spread(own, far, mask)))
        for mixed, (own, far), (g, pair, spans, q_rows, *_) in zip(mixes, probs, work):
            at = pl.multiple_of(g * 2 * BLOCK, 2 * BLOCK)
            p_ref[pair, pl.ds(at, BLOCK), :] = own
            p_ref[pair, pl.ds(at + BLOCK, BLOCK), :] = far
            o_ref[pair * LANES : pair * LANES + HEAD, q_rows] = mixed[:HEAD, :GROUP].astype(bf16)
            o_ref[pair * LANES + HEAD : (pair + 1) * LANES, q_rows] = mixed[HEAD:, GROUP:].astype(bf16)
        return carry

    lax.fori_loop(0, tile // GROUP // ABREAST, some_groups, 0)


def attend(lens, partner, bias, q, k, v):
    slot, width = q.shape
    grid = slot // TILE
    pairs, per_tile = width // LANES, (TILE // GROUP) * 2 * BLOCK
    return pl.pallas_call(
        functools.partial(attend_kernel, slot=slot),
        grid=(grid,),
        in_specs=[
            smem(),
            smem(),
            smem(),
            pl.BlockSpec((TILE, width), lambda i: (i, 0)),
            whole(k.shape),
            whole(v.shape),
        ],
        out_specs=[
            pl.BlockSpec((width, TILE), lambda i: (0, i)),
            pl.BlockSpec((pairs, per_tile, 2 * GROUP), lambda i: (0, i, 0)),
        ],
        out_shape=[
            jax.ShapeDtypeStruct((width, slot), bf16),
            jax.ShapeDtypeStruct((pairs, grid * per_tile, 2 * GROUP), bf16),
        ],
        scratch_shapes=[
            pltpu.VMEM((2 * GROUP, 2 * GROUP), bf16),
        ],
        compiler_params=params(),
        cost_estimate=pl.CostEstimate(
            flops=20 * 10**9, bytes_accessed=slot * width * 10, transcendentals=slot * 512
        ),
        name="attend",
    )(lens, partner, bias, q, k, v)


def attend_back_kernel(
    partner, q_ref, do_ref, p_ref, k_ref, v_ref,
    dq_ref, dk_ref, dv_ref, db_ref,
    mask_ref, dk_sum, dv_sum, db_sum,
):
    tile = q_ref.shape[0]
    step = pl.program_id(0)
    per = GROUP // BLOCK

    @pl.when(step == 0)
    def _():
        mask_ref[...] = diagonal_mask()
        dk_sum[...] = jnp.zeros_like(dk_sum)
        dv_sum[...] = jnp.zeros_like(dv_sum)

    scale = 1.0 / math.sqrt(HEAD)
    lanes = head_lanes()
    mask = mask_ref[...]
    work, d_probs, seconds, thirds = [], [], [], []
    for g in range(tile // GROUP):
        first = step * (tile // BLOCK) + g * per
        partners = [partner[0, first + c] for c in range(per)]
        rows = pl.ds(pl.multiple_of(first * BLOCK, GROUP), GROUP)
        spans = [rows] + [pl.ds(pl.multiple_of(p * BLOCK, BLOCK), BLOCK) for p in partners]
        q_rows = slice(g * GROUP, (g + 1) * GROUP)
        q_two = head_stack(q_ref[q_rows, :], lanes)
        do_two = head_stack(do_ref[q_rows, :], lanes)
        v_all = jnp.concatenate([v_ref[at, :] for at in spans], axis=0)
        work.append((g, spans, q_rows, q_two, do_two))
        d_probs.append(dot_nt(v_all, do_two))
    for d_prob, (g, *_) in zip(d_probs, work):
        at = g * 2 * BLOCK
        own_b = p_ref[0, at : at + BLOCK, :]
        far_b = p_ref[0, at + BLOCK : at + 2 * BLOCK, :]
        own, far = own_b.astype(f32), far_b.astype(f32)
        d_own, d_far = compact(d_prob[:GROUP]), compact(d_prob[GROUP:])
        delta = jnp.sum(own * d_own, axis=0, keepdims=True) + jnp.sum(
            far * d_far, axis=0, keepdims=True
        )
        d_own = own * (d_own - delta)
        d_far = far * (d_far - delta)
        d_bias = jnp.sum(d_far, axis=0, keepdims=True)
        db_sum[pl.ds(step * (tile // GROUP) + g, 1), :] = d_bias[:, :GROUP] + d_bias[:, GROUP:]
        seconds.append((spread(d_own * scale, d_far * scale, mask), spread(own_b, far_b, mask)))
    for (d_scores, prob), (g, spans, q_rows, q_two, do_two) in zip(seconds, work):
        k_all = jnp.concatenate([k_ref[at, :] for at in spans], axis=0)
        thirds.append((dot(d_scores, q_two), dot(prob, do_two), dot(k_all.T, d_scores)))
    for (dk, dv, dq), (g, spans, q_rows, *_) in zip(thirds, work):
        dq = jnp.concatenate([dq[:HEAD, :GROUP], dq[HEAD:, GROUP:]], axis=0)
        dq_ref[q_rows, :] = dq.T.astype(bf16)
        dk_sum[spans[0], :] += dk[:GROUP]
        dv_sum[spans[0], :] += dv[:GROUP]
        for c in range(per):
            here = slice(GROUP + c * BLOCK, GROUP + (c + 1) * BLOCK)
            dk_sum[spans[1 + c], :] += dk[here]
            dv_sum[spans[1 + c], :] += dv[here]

    @pl.when(step == pl.num_programs(0) - 1)
    def _():
        dk_ref[...] = dk_sum[...].astype(bf16)
        dv_ref[...] = dv_sum[...].astype(bf16)
        groups = db_sum.shape[0]
        blocks = groups * per
        pick = (iota((GROUP, blocks), 0) // BLOCK == iota((GROUP, blocks), 1) % per).astype(f32)
        sums = dot(db_sum[...], pick, highest)
        mine = iota((groups, blocks), 1) // per == iota((groups, blocks), 0)
        db_ref[...] = jnp.sum(jnp.where(mine, sums, 0.0), axis=0, keepdims=True)


def attend_back(pair, partner, q, d_o, probs, k, v):
    slot = q.shape[0]
    grid = slot // WIDE
    per_tile = (WIDE // GROUP) * 2 * BLOCK
    row = pl.BlockSpec((WIDE, LANES), lambda i: (i, pair))
    once = pl.BlockSpec((slot, LANES), lambda i: (0, pair), pipeline_mode=pl.Buffered(1))
    out = jax.ShapeDtypeStruct((slot, LANES), bf16)
    return pl.pallas_call(
        attend_back_kernel,
        grid=(grid,),
        in_specs=[
            smem(),
            row,
            row,
            pl.BlockSpec((1, per_tile, 2 * GROUP), lambda i: (pair, i, 0)),
            once,
            once,
        ],
        out_specs=[
            pl.BlockSpec((WIDE, LANES), lambda i: (i, 0)),
            whole((slot, LANES)),
            whole((slot, LANES)),
            whole((1, slot // BLOCK)),
        ],
        out_shape=[out, out, out, jax.ShapeDtypeStruct((1, slot // BLOCK), f32)],
        scratch_shapes=[
            pltpu.VMEM((2 * GROUP, 2 * GROUP), bf16),
            pltpu.VMEM((slot, LANES), f32),
            pltpu.VMEM((slot, LANES), f32),
            pltpu.VMEM((slot // GROUP, GROUP), f32),
        ],
        compiler_params=params(),
        cost_estimate=pl.CostEstimate(
            flops=10 * 10**9, bytes_accessed=slot * LANES * 16, transcendentals=0
        ),
        name="attend_back",
    )(partner, q, d_o, probs, k, v)


def ffn_kernel(
    place, x_ref, dy_ref, o_ref, norms_ref, w_ref,
    out_ref, dx_ref, do_ref, sent_in, sent_out, kept_in, kept_out, g_norm_ref,
    g_ref, h_scr, ht_scr, dyt_scr, y_scr, dh_scr, hat_scr, gt_scr, *, sorted_bits,
):
    tile, width = x_ref.shape
    hidden = gt_scr.shape[1]
    slabs = hidden // width
    parts = width // ROWS
    whole_rows = slice(slabs * ROWS, (slabs + 1) * ROWS)
    out_rows = slice((slabs + 1) * ROWS, (2 * slabs + 1) * ROWS)
    step = pl.program_id(0)

    share = parts // slabs
    fresh = step == 0

    def add_to(ref, at, value):
        ref[at] = value + jnp.where(fresh, 0.0, ref[at])

    root = math.sqrt(2.0 / math.pi)
    few = w_ref.shape[0]

    def blocks_of(first, count, at):
        if count <= few:
            part = slice(first % few, first % few + count)
            return w_ref[part, first // few, at, :].reshape(-1, width)
        return jnp.concatenate(
            [w_ref[:, upper, at, :].reshape(-1, width) for upper in range(count // few)], axis=0
        )

    w_in = [blocks_of(0, parts, slice(c * ROWS, (c + 1) * ROWS)) for c in range(slabs)]
    w_out = [blocks_of(c * share, share, out_rows) for c in range(slabs)]
    w_o = blocks_of(0, parts, whole_rows)

    def d_hidden(c):
        return dot_nt(dy_ref[...], w_out[c])

    def between(act, d_hid):
        square = act * act
        curve = jnp.tanh(act * (root + (root * 0.044715) * square))
        gate = 0.5 + 0.5 * curve
        hid = act * gate
        slope = gate + hid * (1.0 - curve) * (root + (3.0 * root * 0.044715) * square)
        return hid.astype(bf16), (d_hid * slope).astype(bf16)

    o_t = o_ref[...]
    x_one = x_ref[...].astype(f32) + dot(o_t.T, w_o)
    d_hid = d_hidden(0)
    dyt_scr[...] = dy_ref[...].T
    hat, rstd = norm_stats(x_one)
    h_two = (hat * norms_ref[2:3, :] + norms_ref[3:4, :]).astype(bf16)
    h_scr[...] = h_two
    hat_scr[...] = hat
    y_scr[...] = x_one
    act = dot(h_scr[...], w_in[0])
    ht_scr[...] = h_two.T
    for c in range(slabs):
        this_act, this_d = act, d_hid
        if c + 1 < slabs:
            d_hid = d_hidden(c + 1)
            act = dot(h_scr[...], w_in[c + 1])
        hid, d_act = between(this_act, this_d)
        more = dot_nt(d_act, w_in[c])
        dh_scr[...] = more if c == 0 else dh_scr[...] + more
        y_scr[...] += dot(hid, w_out[c])
        cols = slice(c * width, (c + 1) * width)
        add_to(gt_scr, (slice(None), cols), dot(dyt_scr[...], hid))
        slab = (slice(None), slice(c * ROWS, (c + 1) * ROWS), slice(None))
        add_to(g_ref, slab, dot(ht_scr[...], d_act).reshape(parts, ROWS, width))
    d_h = dh_scr[...]
    hat = hat_scr[...]
    d_x = dy_ref[...].astype(f32) + norm_back(d_h, hat, rstd, norms_ref[2:3, :])
    dx_ref[...] = d_x
    d_z = d_x.astype(bf16)
    do_ref[...] = dot_nt(d_z, w_o).astype(bf16)
    add_to(g_ref, (slice(None), whole_rows, slice(None)), dot(o_t, d_z).reshape(parts, ROWS, width))
    add_to(g_norm_ref, (slice(2, 3), slice(None)), jnp.sum(d_h * hat, axis=0, keepdims=True))
    add_to(g_norm_ref, (slice(3, 4), slice(None)), jnp.sum(d_h, axis=0, keepdims=True))
    out_ref[...] = y_scr[...].astype(bf16)

    @pl.when(fresh)
    def _():
        g_norm_ref[0:2, :] = jnp.zeros_like(g_norm_ref[0:2, :])
        g_norm_ref[4:, :] = jnp.zeros_like(g_norm_ref[4:, :])

    @pl.when(step == pl.num_programs(0) - 1)
    def _():
        for c in range(slabs):
            g_ref[c * share : (c + 1) * share, out_rows, :] = gt_scr[
                :, c * width : (c + 1) * width
            ].T.reshape(share, slabs * ROWS, width)
        first = (slabs + 1) * ROWS
        halves(
            place,
            (sent_in, sent_out, kept_in, kept_out),
            lambda i, part: g_ref[i, first:] if part else g_ref[i, :first],
            sorted_bits,
        )


def halves(place, refs, block, sorted_bits):
    mine = place[0] & 1
    parts = len(refs) // 2
    high = refs[0].shape[0] // 2

    def one(i, carry):
        low, next_low, rest = i & 1, (i >> 1) & 1, i >> 2
        spots = [low * high + next_low * (high // 2) + rest, next_low * high + low * (high // 2) + rest]
        for part in range(parts):
            at = spots[part] if sorted_bits else i
            refs[part][at] = block(2 * i + 1 - mine, part).astype(bf16)
            refs[parts + part][at] = block(2 * i + mine, part)
        return carry

    lax.fori_loop(0, 2 * high, one, 0)


def ffn(place, x, dy, o_t, norms, w_two, sorted_bits):
    slot, width = x.shape
    hidden = (w_two.shape[2] // ROWS - 1) // 2 * width
    blocks = (w_two.shape[0] * w_two.shape[1], *w_two.shape[2:])
    grid = slot // TILE
    first = hidden // width * ROWS + ROWS
    half_in = (blocks[0] // 2, first, width)
    half_out = (blocks[0] // 2, blocks[1] - first, width)
    row = pl.BlockSpec((TILE, width), lambda i: (i, 0))

    def once(shape):
        return pl.BlockSpec(shape, lambda i: (0,) * len(shape), pipeline_mode=pl.Buffered(1))

    return pl.pallas_call(
        functools.partial(ffn_kernel, sorted_bits=sorted_bits),
        grid=(grid,),
        in_specs=[
            smem(),
            row,
            row,
            pl.BlockSpec((width, TILE), lambda i: (0, i)),
            once(norms.shape),
            once(w_two.shape),
        ],
        out_specs=[
            row, row, row,
            once(half_in), once(half_out), once(half_in), once(half_out),
            once((8, width)),
        ],
        out_shape=[
            jax.ShapeDtypeStruct((slot, width), bf16),
            jax.ShapeDtypeStruct((slot, width), f32),
            jax.ShapeDtypeStruct((slot, width), bf16),
            jax.ShapeDtypeStruct(half_in, bf16),
            jax.ShapeDtypeStruct(half_out, bf16),
            jax.ShapeDtypeStruct(half_in, f32),
            jax.ShapeDtypeStruct(half_out, f32),
            jax.ShapeDtypeStruct((8, width), f32),
        ],
        scratch_shapes=[
            pltpu.VMEM(blocks, f32),
            pltpu.VMEM((TILE, width), bf16),
            pltpu.VMEM((width, TILE), bf16),
            pltpu.VMEM((width, TILE), bf16),
            pltpu.VMEM((TILE, width), f32),
            pltpu.VMEM((TILE, width), f32),
            pltpu.VMEM((TILE, width), f32),
            pltpu.VMEM((width, hidden), f32),
        ],
        compiler_params=params(),
        cost_estimate=pl.CostEstimate(
            flops=2 * slot * width * (3 * width + 6 * hidden),
            bytes_accessed=slot * width * 14,
            transcendentals=slot * hidden,
        ),
        name="ffn",
    )(place, x, dy, o_t, norms, w_two)


def project_back_kernel(
    place, lens, x_ref, dx_ref, du_ref, norms_ref, w_ref, g_sort_ref, g_two_ref, *refs, slot,
    sorted_bits,
):
    *d_refs, grad_ref, sent_a, sent_b, kept_a, kept_b, g_ref, g_norm_ref = refs
    tile, width = x_ref.shape
    step = pl.program_id(0)

    @pl.when(step == 0)
    def _():
        g_ref[...] = jnp.zeros_like(g_ref)
        g_norm_ref[...] = jnp.zeros_like(g_norm_ref)

    pairs = width // LANES
    ends = ends_of(lens, slot)
    blocks = SUB // BLOCK
    starts = range(0, tile, SUB)
    d_hs, hats, rstds, h_ones = [], [], [], []
    for r in starts:
        rows = slice(r, r + SUB)
        places = step * tile + r + iota((SUB, 1), 0)
        live = places < end_at(places, ends, slot)
        d_u = du_ref[r // BLOCK : r // BLOCK + blocks, :].reshape(blocks, 1, width)
        d_h = jnp.broadcast_to(d_u, (blocks, BLOCK, width)).reshape(SUB, width)
        d_h = jnp.where(live, d_h, 0.0)
        for part in range(3):
            cols = slice(part * width, (part + 1) * width)
            d_part = jnp.concatenate(
                [ref[rows, :] for ref in d_refs[part * pairs : (part + 1) * pairs]], axis=1
            )
            d_h = d_h + dot_nt(d_part, w_ref[:, cols])
        d_hs.append(d_h)
        hat, rstd = norm_stats(x_ref[rows, :].astype(f32))
        hats.append(hat)
        rstds.append(rstd)
        h_ones.append((hat * norms_ref[0:1, :] + norms_ref[1:2, :]).astype(bf16))
    h_one = jnp.concatenate(h_ones, axis=0)

    def back(at):
        rows = slice(at * SUB, (at + 1) * SUB)
        g_norm_ref[0:1, :] += jnp.sum(d_hs[at] * hats[at], axis=0, keepdims=True)
        g_norm_ref[1:2, :] += jnp.sum(d_hs[at], axis=0, keepdims=True)
        grad_ref[rows, :] = dx_ref[rows, :] + norm_back(
            d_hs[at], hats[at], rstds[at], norms_ref[0:1, :]
        )

    done = 0
    for part in range(3):
        cols = slice(part * width, (part + 1) * width)
        d_part = jnp.concatenate([ref[...] for ref in d_refs[part * pairs : (part + 1) * pairs]], axis=1)
        g_ref[:, cols] += dot_tn(h_one, d_part)
        until = len(starts) * (part + 1) // 3
        for at in range(done, until):
            back(at)
        done = until

    @pl.when(step == pl.num_programs(0) - 1)
    def _():
        g_ref[:, 3 * width : 3 * width + LANES] = g_sort_ref[...]
        small = g_norm_ref[...] + g_two_ref[...]
        rest = jnp.zeros((LANES - small.shape[0], width), f32)
        g_ref[:, 3 * width + LANES :] = jnp.concatenate([small, rest], axis=0).T
        cols = sent_a.shape[2]
        halves(
            place,
            (sent_a, sent_b, kept_a, kept_b),
            lambda i, part: g_ref[
                pl.ds(pl.multiple_of(i * ROWS, ROWS), ROWS), part * cols : (part + 1) * cols
            ],
            sorted_bits,
        )


def project_back(
    place, lens, x, d_x, d_q, d_k, d_v, d_u, norms, w_one, g_sort, g_two, sorted_bits
):
    slot, width = x.shape
    grid = slot // WIDE
    row = pl.BlockSpec((WIDE, width), lambda i: (i, 0))
    half = (width // ROWS // 2, ROWS, w_one.shape[1] // 2)

    def once(shape):
        return pl.BlockSpec(shape, lambda i: (0,) * len(shape), pipeline_mode=pl.Buffered(1))

    return pl.pallas_call(
        functools.partial(project_back_kernel, slot=slot, sorted_bits=sorted_bits),
        grid=(grid,),
        in_specs=[
            smem(),
            smem(),
            row,
            row,
            pl.BlockSpec((WIDE // BLOCK, width), lambda i: (i, 0)),
            once(norms.shape),
            once(w_one.shape),
            once(g_sort.shape),
            once(g_two.shape),
        ]
        + [pl.BlockSpec((WIDE, LANES), lambda i: (i, 0))] * (3 * width // LANES),
        out_specs=[row] + [once(half)] * 4,
        out_shape=[
            jax.ShapeDtypeStruct((slot, width), f32),
            jax.ShapeDtypeStruct(half, bf16),
            jax.ShapeDtypeStruct(half, bf16),
            jax.ShapeDtypeStruct(half, f32),
            jax.ShapeDtypeStruct(half, f32),
        ],
        scratch_shapes=[pltpu.VMEM(w_one.shape, f32), pltpu.VMEM((8, width), f32)],
        compiler_params=params(),
        cost_estimate=pl.CostEstimate(
            flops=2 * slot * width * 6 * width, bytes_accessed=slot * width * 18, transcendentals=0
        ),
        name="project_back",
    )(place, lens, x, d_x, d_u, norms, w_one, g_sort, g_two, *d_q, *d_k, *d_v)


def pack_kernel(wqkv, wo, wsort, win, wout, norms_t, one_ref, two_ref):
    rows, wide = wqkv.shape
    width = wo.shape[1]
    one_ref[:, :wide] = wqkv[...].astype(bf16)
    one_ref[:, wide : wide + LANES] = wsort[...].astype(bf16)
    few = norms_t.shape[0]
    tall = jnp.concatenate([norms_t[...], jnp.zeros((LANES - few, rows), f32)], axis=0)
    one_ref[:, wide + LANES :] = tall.T.astype(bf16)
    slabs = win.shape[1] // width
    for c in range(slabs):
        two_ref[c * rows : (c + 1) * rows, :] = win[:, c * width : (c + 1) * width].astype(bf16)
    two_ref[slabs * rows : (slabs + 1) * rows, :] = wo[...].astype(bf16)
    two_ref[(slabs + 1) * rows :, :] = wout[...].astype(bf16)


def pack(masters):
    wqkv, wo, wsort, win, wout, norms = masters
    rows = wqkv.shape[0]
    return pl.pallas_call(
        pack_kernel,
        out_shape=[
            jax.ShapeDtypeStruct((rows, wqkv.shape[1] + 2 * LANES), bf16),
            jax.ShapeDtypeStruct((rows * (win.shape[1] // wo.shape[1] + 1) + wout.shape[0], wo.shape[1]), bf16),
        ],
        compiler_params=params(),
        name="pack",
    )(wqkv, wo, wsort, win, wout, norms.T)


def adamw_kernel(*refs, ones, twos):
    one_ref = sum(ref[...].astype(f32) for ref in refs[:ones])
    two_ref = sum(ref[...].astype(f32) for ref in refs[ones : ones + twos])
    refs = refs[ones + twos :]
    masters, moments, squares, outs = refs[:6], refs[6:12], refs[12:18], refs[18:]
    rows, width = masters[1].shape
    wide = masters[0].shape[1]
    slabs = masters[3].shape[1] // width
    few = masters[5].shape[0]
    norm_grad = one_ref[:, wide + LANES :].T[:few, :]
    grads = (
        one_ref[:, :wide],
        two_ref[slabs * rows : (slabs + 1) * rows, :],
        one_ref[:, wide : wide + LANES],
        jnp.concatenate([two_ref[c * rows : (c + 1) * rows, :] for c in range(slabs)], axis=1),
        two_ref[(slabs + 1) * rows :, :],
        norm_grad,
    )
    for i in range(6):
        weight, grad = masters[i][...], grads[i]
        moment = beta_one * moments[i][...] + (1.0 - beta_one) * grad
        square = beta_two * squares[i][...] + (1.0 - beta_two) * grad * grad
        m_hat = moment / (1.0 - beta_one**STEP)
        s_hat = square / (1.0 - beta_two**STEP)
        outs[3 * i][...] = weight - rates[i] * (
            m_hat / (jnp.sqrt(s_hat) + adam_eps) + decay * weight
        )
        outs[3 * i + 1][...] = moment
        outs[3 * i + 2][...] = square


def adamw(one, two, masters, moments, squares):
    flip = lambda group: (*group[:5], group[5].T)
    args = (*one, *two, *flip(masters), *flip(moments), *flip(squares))
    shapes = [a.shape for a in flip(masters)]
    outs = pl.pallas_call(
        functools.partial(adamw_kernel, ones=len(one), twos=len(two)),
        out_shape=[jax.ShapeDtypeStruct(shape, f32) for shape in shapes for _ in range(3)],
        compiler_params=params(),
        name="adamw",
    )(*args)
    return (*outs[:15], *[o.T for o in outs[15:]])


def regroup(gathered, rows, slabs):
    size, width = gathered.shape[0], gathered.shape[-1]
    times = ROWS // rows
    block = gathered.reshape(size // times, times, 2 * slabs + 1, rows, width)
    inner = block[:, :, : slabs + 1].transpose(0, 2, 1, 3, 4)
    outer = block[:, :, slabs + 1 :]
    return jnp.concatenate(
        [
            inner.reshape(size // times, (slabs + 1) * ROWS, width),
            outer.reshape(size // times, slabs * ROWS, width),
        ],
        axis=1,
    )[:, None]


def device_halves(place, sent, kept, size, rows, slabs, axis):
    if rows == ROWS:
        return sent, kept
    cut = kept[0].shape[axis + 1] * rows // ROWS if slabs else kept[0].shape[axis + 1]
    sent, kept = jnp.concatenate(sent, axis=axis + 1), jnp.concatenate(kept, axis=axis + 1)
    mine = place[0] & 1
    low = jnp.where(mine == 0, kept, sent.astype(f32))
    high = jnp.where(mine == 0, sent.astype(f32), kept)
    grads = jnp.stack([low, high], axis=1).reshape((-1,) + kept.shape[1:])
    times = ROWS // rows
    width = grads.shape[-1]
    wide = (slabs + 1) * ROWS
    inner = grads[:, :wide].reshape(size // times, slabs + 1, times, rows, width)
    outer = grads[:, wide:].reshape(size // times, times, slabs, rows, width)
    block = jnp.concatenate([inner.transpose(0, 2, 1, 3, 4), outer], axis=2)
    block = block.reshape(size // 2, 2, (2 * slabs + 1) * rows, width)
    count = size.bit_length() - 1
    results = []
    for index, kind in ((1 - mine, bf16), (mine, f32)):
        half = lax.dynamic_index_in_dim(block, index, 1, keepdims=False).astype(kind)
        for part, lead in zip(jnp.split(half, [cut], axis=axis + 1), ((1, 2), (2, 1))):
            bits = part.reshape((2,) * (count - 1) + part.shape[1:])
            order = [count - 1 - bit for bit in lead] + list(range(count - 3))
            order += list(range(count - 1, bits.ndim))
            results.append(bits.transpose(order).reshape(part.shape))
    return results[:2], results[2:]


def swap(value, mask, size):
    return lax.ppermute(value, "dp", [(i, i ^ mask) for i in range(size)])


def masks_of(bits):
    return [sum(((turn >> at) & 1) << bit for at, bit in enumerate(bits)) for turn in range(2 ** len(bits))]


def fours(count):
    return [tuple(range(bit, min(bit + 2, count))) for bit in range(3, count, 2)]


def gather(block, size):
    held = block[None]
    for bits in fours(size.bit_length() - 1)[::-1] + [(2,), (1,)]:
        came = [swap(held, mask, size) for mask in masks_of(bits)[1:]]
        held = jnp.stack([held, *came], axis=1).reshape((-1,) + block.shape)
    return held, swap(held, 1, size)


class ScatterSum:
    def __init__(self, sent, kept, size, axis):
        self.size, self.axis = size, axis
        self.place = lax.axis_index("dp")
        self.plan = [(1, 2), (2, 1)] + fours(size.bit_length() - 1)[::-1]
        self.kept, self.sent, self.masks = list(kept), list(sent), [1, 1]

    def send(self):
        self.came = [swap(sent, mask, self.size) for sent, mask in zip(self.sent, self.masks)]

    def cut(self, ways, index, values):
        parts = [value.reshape((ways, -1) + value.shape[1:]) for value in values]
        parts = [lax.dynamic_index_in_dim(part, index, 0, keepdims=False) for part in parts]
        return sum(part.astype(f32) for part in parts)

    def step(self):
        bits = self.plan.pop(0)
        if bits[0] < 3:
            kept, came = self.kept, self.came
            mine = [(self.place >> bit) & 1 for bit in bits]
            self.kept = [self.cut(2, m, pair) for m, pair in zip(mine, zip(kept, came))]
            self.sent = [self.cut(2, 1 - m, pair).astype(bf16) for m, pair in zip(mine, zip(kept, came))]
            self.masks = [1 << bit for bit in bits]
            return
        values = [*self.kept, *self.came]
        if len(self.kept) == 2:
            values = [jnp.concatenate(pair, axis=self.axis + 1) for pair in (self.kept, self.came)]
        ways = 2 ** len(bits)
        mine = (self.place >> bits[0]) & (ways - 1)
        self.kept = [self.cut(ways, mine, values)]
        self.sent = [self.cut(ways, mine ^ turn, values).astype(bf16) for turn in range(1, ways)]
        self.masks = masks_of(bits)[1:]

    def after(self, values):
        self.came, values = lax.optimization_barrier((self.came, values))
        return values

    def before(self, values):
        self.sent, values = lax.optimization_barrier((self.sent, values))
        return values

    def last(self):
        return [value.reshape(value.shape[1:]) for value in (*self.kept, *self.came)]


def body(size, x, dy, lens, partner, *state):
    slot, width = x.shape
    masters, moments, squares = state[:6], state[6:12], state[12:]
    rows = masters[0].shape[0]
    slabs = masters[3].shape[1] // width
    place = lax.axis_index("dp").astype(jnp.int32).reshape((1,))
    pack_one, pack_two = pack(masters)
    near, far = gather(pack_one, size)
    if rows == ROWS:
        w_two = lax.all_gather(pack_two, "dp", axis=0)[:, None]
    else:
        w_two = regroup(lax.all_gather(pack_two, "dp", axis=0), rows, slabs)

    q, k, v, u, norms, w_one = project(place, lens, x, near, far)
    bias, steps = sort_net(lens, u, w_one, partner, slot)
    o_t, probs = attend(lens, partner, bias, q, k, v)
    direct = rows == ROWS
    out, d_x, d_o, *parts, g_two = ffn(place, x, dy, o_t, norms, w_two, direct)
    sent, kept = device_halves(place, parts[:2], parts[2:], size, rows, slabs, 0)
    two = ScatterSum(sent, kept, size, 0)
    two.send()

    def back(pair):
        return attend_back(pair, partner, q, d_o, probs, k, v)

    def next_stage(values):
        two.step()
        values = two.before(values)
        two.send()
        return values

    back_0 = two.after(back(0))
    q, d_o = next_stage((q, d_o))
    back_1, back_2 = two.after((back(1), back(2)))
    q, d_o = next_stage((q, d_o))
    back_3 = two.after(back(3))
    u, back_3 = next_stage((u, back_3))
    d_q, d_k, d_v, d_bias = zip(back_0, back_1, back_2, back_3)
    d_u, g_sort = sort_back(lens, u, w_one, partner, d_bias, steps, slot)
    while two.plan:
        d_u = next_stage(two.after(d_u))
    grad_in, *parts = project_back(
        place, lens, x, d_x, d_q, d_k, d_v, d_u, norms, w_one, g_sort, g_two, direct
    )
    grad_in, parts = two.after((grad_in, parts))
    sent, kept = device_halves(place, parts[:2], parts[2:], size, rows, 0, 1)
    one = ScatterSum(sent, kept, size, 1)
    one.send()
    while one.plan:
        one.step()
        one.send()
    outs = adamw(one.last(), two.last(), masters, moments, squares)
    return (out, grad_in, *outs)


def solution(mesh):
    spec = P("dp", None)
    return jax.shard_map(
        functools.partial(body, mesh.shape["dp"]),
        mesh=mesh,
        in_specs=(spec,) * 22,
        out_specs=(spec,) * 20,
        check_vma=False,
    )
```

```python
import functools
import math

import jax
import jax.numpy as jnp
from jax import lax
from jax.experimental import pallas as pl
from jax.experimental.pallas import tpu as pltpu
from jax.sharding import PartitionSpec as P

HEADS = 8
HEAD = 64
SORT = 64
BLOCK = 32
SINK = 8
STEP = 10
TILE = 512
WIDE = 1024
ROWS = 16
ABREAST = 4
SUB = 256
GROUP = 128
LANES = 128

highest = lax.Precision.HIGHEST
masked = -1000000000.0
norm_eps = 1e-05
beta_one = 0.9
beta_two = 0.999
adam_eps = 1e-08
decay = 0.01
rates = (0.05, 0.15, 0.05, 0.05, 0.025, 0.5)
f32 = jnp.float32
bf16 = jnp.bfloat16


def dot(left, right, precision=None):
    return jnp.dot(left, right, precision=precision, preferred_element_type=f32)


def dot_nt(left, right, precision=None):
    return lax.dot_general(
        left, right, (((1,), (1,)), ((), ())), precision=precision, preferred_element_type=f32
    )


def dot_tn(left, right, precision=None):
    return lax.dot_general(
        left, right, (((0,), (0,)), ((), ())), precision=precision, preferred_element_type=f32
    )


def iota(shape, axis):
    return lax.broadcasted_iota(jnp.int32, shape, axis)


def ends_of(lens, slot):
    quarter = slot // 4
    is_long = lens[0, 0] > quarter
    return [jnp.where(is_long, lens[0, 0], k * quarter + lens[0, k]) for k in range(4)]


def end_at(places, ends, slot):
    quarter = slot // 4
    return jnp.where(
        places < 2 * quarter,
        jnp.where(places < quarter, ends[0], ends[1]),
        jnp.where(places < 3 * quarter, ends[2], ends[3]),
    )


def norm_stats(value):
    center = value - jnp.mean(value, axis=-1, keepdims=True)
    spread = jnp.mean(center * center, axis=-1, keepdims=True)
    rstd = lax.rsqrt(spread + norm_eps)
    return center * rstd, rstd


def norm_back(grad, hat, rstd, gain):
    d_hat = grad * gain
    mean_d = jnp.mean(d_hat, axis=-1, keepdims=True)
    mean_dh = jnp.mean(d_hat * hat, axis=-1, keepdims=True)
    return rstd * (d_hat - mean_d - hat * mean_dh)


def params(mebibytes):
    return pltpu.CompilerParams(vmem_limit_bytes=mebibytes << 20)


def whole(shape):
    return pl.BlockSpec(shape, lambda *_: (0,) * len(shape))


def in_hbm(*values):
    return [pltpu.with_memory_space_constraint(value, pltpu.HBM) for value in values]


def smem():
    return pl.BlockSpec(memory_space=pltpu.SMEM)


def project_kernel(
    place, lens, x_ref, near_ref, far_ref, q_ref, k_ref, v_ref, u_ref, norms_ref, w_ref, *, slot
):
    tile, width = x_ref.shape
    base = pl.program_id(0) * tile

    @pl.when(pl.program_id(0) == 0)
    def _():
        rows = near_ref.shape[1]
        mine = place[0] & 1
        for half in range(near_ref.shape[0]):
            at = (place[0] >> 1) ^ half
            w_ref[2 * half * rows : (2 * half + 1) * rows, :] = jnp.where(
                mine == 0, near_ref[at], far_ref[at]
            )
            w_ref[(2 * half + 1) * rows : (2 * half + 2) * rows, :] = jnp.where(
                mine == 0, far_ref[at], near_ref[at]
            )

    @pl.when(pl.program_id(0) == 0)
    def _():
        norms_ref[...] = w_ref[:, 3 * width + LANES :].astype(f32).T[:8, :]

    parts = []
    for r in range(0, tile, SUB):
        hat, _ = norm_stats(x_ref[r : r + SUB, :].astype(f32))
        parts.append((hat * norms_ref[0:1, :] + norms_ref[1:2, :]).astype(bf16))
        for part, ref in enumerate((q_ref, k_ref, v_ref)):
            ref[r : r + SUB, :] = dot(parts[-1], w_ref[:, part * width : (part + 1) * width]).astype(bf16)
    h_one = jnp.concatenate(parts, axis=0)
    blocks = tile // BLOCK
    at = iota((blocks, tile), 1)
    places = at + base
    live = places < end_at(places, ends_of(lens, slot), slot)
    own = (at // BLOCK) == iota((blocks, tile), 0)
    pick = jnp.where(live & own, 1.0, 0.0).astype(bf16)
    u_ref[...] = dot(pick, h_one)


def project(place, lens, x, near, far):
    slot, width = x.shape
    w_shape = (2 * near.shape[0] * near.shape[1], near.shape[2])
    grid = slot // WIDE
    row = pl.BlockSpec((WIDE, width), lambda i: (i, 0))
    out = jax.ShapeDtypeStruct((slot, width), bf16)
    return pl.pallas_call(
        functools.partial(project_kernel, slot=slot),
        grid=(grid,),
        in_specs=[smem(), smem(), row, whole(near.shape), whole(far.shape)],
        out_specs=[
            row,
            row,
            row,
            pl.BlockSpec((WIDE // BLOCK, width), lambda i: (i, 0)),
            whole((8, width)),
            whole(w_shape),
        ],
        out_shape=[
            out,
            out,
            out,
            jax.ShapeDtypeStruct((slot // BLOCK, width), f32),
            jax.ShapeDtypeStruct((8, width), f32),
            jax.ShapeDtypeStruct(w_shape, bf16),
        ],
        compiler_params=params(12),
        cost_estimate=pl.CostEstimate(
            flops=2 * slot * width * 3 * width, bytes_accessed=slot * width * 8, transcendentals=0
        ),
        name="project",
    )(place, lens, *in_hbm(x, near, far))


def sort_parts(lens, u_ref, ws_ref, slot):
    blocks = u_ref.shape[0]
    ends = ends_of(lens, slot)
    quarter = slot // 4
    is_long = lens[0, 0] > quarter

    def group_of(axis, shape):
        index = iota(shape, axis)
        start = index * BLOCK
        live = start < end_at(start, ends, slot)
        member = jnp.where(is_long, 0, start // quarter)
        return jnp.where(live, member, 4 + index)

    same = group_of(0, (blocks, blocks)) == group_of(1, (blocks, blocks))
    start = iota((blocks, 1), 0) * BLOCK
    count = jnp.clip(end_at(start, ends, slot) - start, 0, BLOCK).astype(f32)
    scale = lax.rsqrt(jnp.maximum(count, 1.0))
    summary = u_ref[...] * scale
    w_sort = ws_ref[...].astype(f32)
    sort_q = dot(summary, w_sort[:, :SORT], highest)
    sort_k = dot(summary, w_sort[:, SORT:], highest)
    return same, scale, summary, w_sort, sort_q, sort_k


def sort_columns(w_one):
    return pl.BlockSpec((w_one.shape[0], 2 * SORT), lambda i: (0, 3 * w_one.shape[0] // (2 * SORT)))


def column_of(row, eye):
    return jnp.sum(jnp.where(eye, row, 0.0), axis=1, keepdims=True)


def sort_kernel(lens, u_ref, ws_ref, partner_ref, bias_ref, steps_ref, *, slot):
    blocks = u_ref.shape[0]
    same, _, _, _, sort_q, sort_k = sort_parts(lens, u_ref, ws_ref, slot)
    raw = dot_nt(sort_q, sort_k, highest)
    logits = jnp.where(same, raw / math.sqrt(SORT), masked)

    def normalize(value, axis):
        top = jnp.max(value, axis=axis, keepdims=True)
        return value - (top + jnp.log(jnp.sum(jnp.exp(value - top), axis=axis, keepdims=True)))

    for turn in range(SINK):
        logits = normalize(logits, 1)
        steps_ref[2 * turn] = logits
        logits = normalize(logits, 0)
        steps_ref[2 * turn + 1] = logits
    eye = iota((blocks, blocks), 0) == iota((blocks, blocks), 1)
    members = jnp.sum(same.astype(f32), axis=1, keepdims=True)
    partner = column_of(partner_ref[...].astype(f32), eye)
    pick = partner == iota((blocks, blocks), 1).astype(f32)
    bias = jnp.sum(jnp.where(pick, logits, 0.0), axis=1, keepdims=True) + jnp.log(members)
    bias_ref[...] = jnp.sum(jnp.where(eye, bias, 0.0), axis=0, keepdims=True)


def sort_net(lens, u, w_sort, partner, slot):
    blocks = u.shape[0]
    return pl.pallas_call(
        functools.partial(sort_kernel, slot=slot),
        in_specs=[smem(), whole(u.shape), sort_columns(w_sort), whole(partner.shape)],
        out_specs=[whole((1, blocks)), whole((2 * SINK, blocks, blocks))],
        out_shape=[
            jax.ShapeDtypeStruct((1, blocks), f32),
            jax.ShapeDtypeStruct((2 * SINK, blocks, blocks), f32),
        ],
        grid=(1,),
        compiler_params=params(8),
        cost_estimate=pl.CostEstimate(flops=10**8, bytes_accessed=10**7, transcendentals=10**6),
        name="sort_net",
    )(lens, u, w_sort, partner)


def sort_back_kernel(
    lens, u_ref, ws_ref, partner_ref, steps_ref, *refs, slot
):
    *d_bias_refs, d_u_ref, grad_ref = refs
    blocks = u_ref.shape[0]
    same, scale, summary, w_sort, sort_q, sort_k = sort_parts(lens, u_ref, ws_ref, slot)
    eye = iota((blocks, blocks), 0) == iota((blocks, blocks), 1)
    partner = column_of(partner_ref[...].astype(f32), eye)
    pick = partner == iota((blocks, blocks), 1).astype(f32)
    d_bias = column_of(sum(ref[...] for ref in d_bias_refs), eye)
    d_logits = jnp.where(pick, d_bias, 0.0)
    for turn in reversed(range(SINK)):
        for axis, step in ((0, 2 * turn + 1), (1, 2 * turn)):
            share = jnp.exp(steps_ref[step])
            d_logits = d_logits - share * jnp.sum(d_logits, axis=axis, keepdims=True)
    d_raw = jnp.where(same, d_logits, 0.0) / math.sqrt(SORT)
    d_sort_q = dot(d_raw, sort_k, highest)
    d_sort_k = dot_tn(d_raw, sort_q, highest)
    d_sort = jnp.concatenate([d_sort_q, d_sort_k], axis=1)
    grad_ref[...] = dot_tn(summary, d_sort, highest)
    d_u_ref[...] = dot_nt(d_sort, w_sort, highest) * scale


def sort_back(lens, u, w_sort, partner, d_bias, steps, slot):
    blocks, width = u.shape
    return pl.pallas_call(
        functools.partial(sort_back_kernel, slot=slot),
        in_specs=[
            smem(),
            whole(u.shape),
            sort_columns(w_sort),
            whole(partner.shape),
            whole(steps.shape),
            *[whole(part.shape) for part in d_bias],
        ],
        out_specs=[whole((blocks, width)), whole((width, 2 * SORT))],
        out_shape=[
            jax.ShapeDtypeStruct((blocks, width), f32),
            jax.ShapeDtypeStruct((width, 2 * SORT), f32),
        ],
        grid=(1,),
        compiler_params=params(8),
        cost_estimate=pl.CostEstimate(flops=10**8, bytes_accessed=10**7, transcendentals=10**6),
        name="sort_back",
    )(lens, u, w_sort, partner, steps, *d_bias)


def lane_block(rows):
    return (iota((rows, 2 * GROUP), 1) % GROUP) // BLOCK


def compact(full):
    at = lane_block(BLOCK)
    part = [full[c * BLOCK : (c + 1) * BLOCK] for c in range(GROUP // BLOCK)]
    return jnp.where(
        at < 2,
        jnp.where(at < 1, part[0], part[1]),
        jnp.where(at < 3, part[2], part[3]),
    )


def diagonal_mask():
    rows = 2 * GROUP
    return jnp.where((iota((rows, rows), 0) % GROUP) // BLOCK == lane_block(rows), 1.0, 0.0).astype(bf16)


def spread(own, far, mask):
    own, far = own.astype(bf16), far.astype(bf16)
    times = GROUP // BLOCK
    return jnp.concatenate([own] * times + [far] * times, axis=0) * mask


def head_stack(pair, lanes):
    zero = jnp.zeros_like(pair)
    return jnp.concatenate(
        [jnp.where(lanes < HEAD, pair, zero), jnp.where(lanes < HEAD, zero, pair)], axis=0
    )


def head_lanes():
    return iota((GROUP, LANES), 1)


def by_lane(values):
    at = iota((1, GROUP), 1) // BLOCK
    return jnp.where(
        at < 2,
        jnp.where(at < 1, values[0], values[1]),
        jnp.where(at < 3, values[2], values[3]),
    )


def gather_far(dst, src, partners):
    for c, p in enumerate(partners):
        dst[GROUP + c * BLOCK : GROUP + (c + 1) * BLOCK, :] = src[pl.ds(pl.multiple_of(p * BLOCK, BLOCK), BLOCK), :]


def attend_kernel(lens, partner, bias, q_ref, k_ref, v_ref, o_ref, p_ref, mask_ref, *, slot):
    tile, width = q_ref.shape
    step = pl.program_id(0)
    pairs = width // LANES
    per = GROUP // BLOCK

    @pl.when(step == 0)
    def _():
        mask_ref[...] = diagonal_mask()

    ends = ends_of(lens, slot)
    scale = 1.0 / math.sqrt(HEAD)

    def some_groups(turn, carry):
        mask = mask_ref[...]
        lanes = head_lanes()
        key = iota((BLOCK, GROUP), 0)
        query = iota((BLOCK, GROUP), 1)
        work = []
        for part in range(ABREAST):
            g = turn * ABREAST + part
            first = step * (tile // BLOCK) + g * per
            partners = [partner[0, first + c] for c in range(per)]
            rows = pl.ds(pl.multiple_of(first * BLOCK, GROUP), GROUP)
            q_rows = pl.ds(pl.multiple_of(g * GROUP, GROUP), GROUP)
            spans = [rows] + [pl.ds(pl.multiple_of(p * BLOCK, BLOCK), BLOCK) for p in partners]
            own_place = (first + query // BLOCK) * BLOCK + key
            far_place = by_lane(partners) * BLOCK + key
            own_live = (own_place < end_at(own_place, ends, slot)) | (query % BLOCK == key)
            far_live = far_place < end_at(far_place, ends, slot)
            own_live = jnp.concatenate([own_live.astype(f32)] * 2, axis=1) > 0.5
            far_live = jnp.concatenate([far_live.astype(f32)] * 2, axis=1) > 0.5
            lane_bias = by_lane([bias[0, first + c] for c in range(per)])
            lane_bias = jnp.concatenate([lane_bias] * 2, axis=1)
            for pair in range(pairs):
                work.append((g, pair, spans, q_rows, own_live, far_live, lane_bias))
        scores = []
        for g, pair, spans, q_rows, *_ in work:
            cols = slice(pair * LANES, (pair + 1) * LANES)
            q_two = head_stack(q_ref[q_rows, cols], lanes)
            k_all = jnp.concatenate([k_ref[at, cols] for at in spans], axis=0)
            scores.append(dot_nt(k_all, q_two))
        probs = []
        for score, (g, pair, spans, q_rows, own_live, far_live, lane_bias) in zip(scores, work):
            own = jnp.where(own_live, compact(score[:GROUP]) * scale, masked)
            far = jnp.where(far_live, compact(score[GROUP:]) * scale + lane_bias, masked)
            top = jnp.maximum(
                jnp.max(own, axis=0, keepdims=True), jnp.max(far, axis=0, keepdims=True)
            )
            own = jnp.exp(own - top)
            far = jnp.exp(far - top)
            total = jnp.sum(own, axis=0, keepdims=True) + jnp.sum(far, axis=0, keepdims=True)
            inverse = 1.0 / total
            probs.append(((own * inverse).astype(bf16), (far * inverse).astype(bf16)))
        mixes = []
        for (own, far), (g, pair, spans, *_) in zip(probs, work):
            cols = slice(pair * LANES, (pair + 1) * LANES)
            v_all = jnp.concatenate([v_ref[at, cols] for at in spans], axis=0)
            mixes.append(dot(v_all.T, spread(own, far, mask)))
        for mixed, (own, far), (g, pair, spans, q_rows, *_) in zip(mixes, probs, work):
            at = pl.multiple_of(g * 2 * BLOCK, 2 * BLOCK)
            p_ref[pair, pl.ds(at, BLOCK), :] = own
            p_ref[pair, pl.ds(at + BLOCK, BLOCK), :] = far
            o_ref[pair * LANES : pair * LANES + HEAD, q_rows] = mixed[:HEAD, :GROUP].astype(bf16)
            o_ref[pair * LANES + HEAD : (pair + 1) * LANES, q_rows] = mixed[HEAD:, GROUP:].astype(bf16)
        return carry

    lax.fori_loop(0, tile // GROUP // ABREAST, some_groups, 0)


def attend(lens, partner, bias, q, k, v):
    slot, width = q.shape
    grid = slot // TILE
    once = pl.BlockSpec((slot, width), lambda i: (0, 0), pipeline_mode=pl.Buffered(1))
    pairs, per_tile = width // LANES, (TILE // GROUP) * 2 * BLOCK
    return pl.pallas_call(
        functools.partial(attend_kernel, slot=slot),
        grid=(grid,),
        in_specs=[
            smem(),
            smem(),
            smem(),
            pl.BlockSpec((TILE, width), lambda i: (i, 0)),
            once,
            once,
        ],
        out_specs=[
            pl.BlockSpec((width, TILE), lambda i: (0, i)),
            pl.BlockSpec((pairs, per_tile, 2 * GROUP), lambda i: (0, i, 0)),
        ],
        out_shape=[
            pltpu.HBM((width, slot), bf16),
            pltpu.HBM((pairs, grid * per_tile, 2 * GROUP), bf16),
        ],
        scratch_shapes=[
            pltpu.VMEM((2 * GROUP, 2 * GROUP), bf16),
        ],
        compiler_params=params(14),
        cost_estimate=pl.CostEstimate(
            flops=20 * 10**9, bytes_accessed=slot * width * 10, transcendentals=slot * 512
        ),
        name="attend",
    )(lens, partner, bias, q, k, v)


def attend_back_kernel(
    partner, q_ref, do_ref, p_ref, k_ref, v_ref,
    dq_ref, dk_ref, dv_ref, db_ref,
    mask_ref, dk_sum, dv_sum, db_sum,
):
    tile = q_ref.shape[0]
    step = pl.program_id(0)
    per = GROUP // BLOCK

    @pl.when(step == 0)
    def _():
        mask_ref[...] = diagonal_mask()
        dk_sum[...] = jnp.zeros_like(dk_sum)
        dv_sum[...] = jnp.zeros_like(dv_sum)

    scale = 1.0 / math.sqrt(HEAD)
    lanes = head_lanes()
    mask = mask_ref[...]
    work, d_probs, seconds, thirds = [], [], [], []
    for g in range(tile // GROUP):
        first = step * (tile // BLOCK) + g * per
        partners = [partner[0, first + c] for c in range(per)]
        rows = pl.ds(pl.multiple_of(first * BLOCK, GROUP), GROUP)
        spans = [rows] + [pl.ds(pl.multiple_of(p * BLOCK, BLOCK), BLOCK) for p in partners]
        q_rows = slice(g * GROUP, (g + 1) * GROUP)
        q_two = head_stack(q_ref[q_rows, :], lanes)
        do_two = head_stack(do_ref[q_rows, :], lanes)
        v_all = jnp.concatenate([v_ref[at, :] for at in spans], axis=0)
        work.append((g, spans, q_rows, q_two, do_two))
        d_probs.append(dot_nt(v_all, do_two))
    for d_prob, (g, *_) in zip(d_probs, work):
        at = g * 2 * BLOCK
        own_b = p_ref[0, at : at + BLOCK, :]
        far_b = p_ref[0, at + BLOCK : at + 2 * BLOCK, :]
        own, far = own_b.astype(f32), far_b.astype(f32)
        d_own, d_far = compact(d_prob[:GROUP]), compact(d_prob[GROUP:])
        delta = jnp.sum(own * d_own, axis=0, keepdims=True) + jnp.sum(
            far * d_far, axis=0, keepdims=True
        )
        d_own = own * (d_own - delta)
        d_far = far * (d_far - delta)
        d_bias = jnp.sum(d_far, axis=0, keepdims=True)
        db_sum[pl.ds(step * (tile // GROUP) + g, 1), :] = d_bias[:, :GROUP] + d_bias[:, GROUP:]
        seconds.append((spread(d_own * scale, d_far * scale, mask), spread(own_b, far_b, mask)))
    for (d_scores, prob), (g, spans, q_rows, q_two, do_two) in zip(seconds, work):
        k_all = jnp.concatenate([k_ref[at, :] for at in spans], axis=0)
        thirds.append((dot(d_scores, q_two), dot(prob, do_two), dot(k_all.T, d_scores)))
    for (dk, dv, dq), (g, spans, q_rows, *_) in zip(thirds, work):
        dq = jnp.concatenate([dq[:HEAD, :GROUP], dq[HEAD:, GROUP:]], axis=0)
        dq_ref[q_rows, :] = dq.T.astype(bf16)
        dk_sum[spans[0], :] += dk[:GROUP]
        dv_sum[spans[0], :] += dv[:GROUP]
        for c in range(per):
            here = slice(GROUP + c * BLOCK, GROUP + (c + 1) * BLOCK)
            dk_sum[spans[1 + c], :] += dk[here]
            dv_sum[spans[1 + c], :] += dv[here]

    @pl.when(step == pl.num_programs(0) - 1)
    def _():
        dk_ref[...] = dk_sum[...].astype(bf16)
        dv_ref[...] = dv_sum[...].astype(bf16)
        groups = db_sum.shape[0]
        blocks = groups * per
        pick = (iota((GROUP, blocks), 0) // BLOCK == iota((GROUP, blocks), 1) % per).astype(f32)
        sums = dot(db_sum[...], pick, highest)
        mine = iota((groups, blocks), 1) // per == iota((groups, blocks), 0)
        db_ref[...] = jnp.sum(jnp.where(mine, sums, 0.0), axis=0, keepdims=True)


def attend_back(pair, partner, q, d_o, probs, k, v):
    slot = q.shape[0]
    grid = slot // WIDE
    per_tile = (WIDE // GROUP) * 2 * BLOCK
    row = pl.BlockSpec((WIDE, LANES), lambda i: (i, pair))
    once = pl.BlockSpec((slot, LANES), lambda i: (0, pair), pipeline_mode=pl.Buffered(1))
    out = jax.ShapeDtypeStruct((slot, LANES), bf16)
    return pl.pallas_call(
        attend_back_kernel,
        grid=(grid,),
        in_specs=[
            smem(),
            row,
            row,
            pl.BlockSpec((1, per_tile, 2 * GROUP), lambda i: (pair, i, 0)),
            once,
            once,
        ],
        out_specs=[
            pl.BlockSpec((WIDE, LANES), lambda i: (i, 0)),
            whole((slot, LANES)),
            whole((slot, LANES)),
            whole((1, slot // BLOCK)),
        ],
        out_shape=[out, out, out, jax.ShapeDtypeStruct((1, slot // BLOCK), f32)],
        scratch_shapes=[
            pltpu.VMEM((2 * GROUP, 2 * GROUP), bf16),
            pltpu.VMEM((slot, LANES), f32),
            pltpu.VMEM((slot, LANES), f32),
            pltpu.VMEM((slot // GROUP, GROUP), f32),
        ],
        compiler_params=params(12),
        cost_estimate=pl.CostEstimate(
            flops=10 * 10**9, bytes_accessed=slot * LANES * 16, transcendentals=0
        ),
        name="attend_back",
    )(partner, *in_hbm(q, d_o, probs, k, v))


def ffn_kernel(
    place, x_ref, dy_ref, o_ref, norms_ref, w_ref,
    out_ref, dx_ref, do_ref, sent_in, sent_out, kept_in, kept_out, g_norm_ref,
    g_ref, h_scr, ht_scr, dyt_scr, y_scr, dh_scr, hat_scr, gt_scr, *, sorted_bits,
):
    tile, width = x_ref.shape
    hidden = gt_scr.shape[1]
    slabs = hidden // width
    parts = width // ROWS
    whole_rows = slice(slabs * ROWS, (slabs + 1) * ROWS)
    out_rows = slice((slabs + 1) * ROWS, (2 * slabs + 1) * ROWS)
    step = pl.program_id(0)

    share = parts // slabs
    fresh = step == 0

    def add_to(ref, at, value):
        ref[at] = value + jnp.where(fresh, 0.0, ref[at])

    root = math.sqrt(2.0 / math.pi)
    few = w_ref.shape[0]

    def blocks_of(first, count, at):
        if count <= few:
            part = slice(first % few, first % few + count)
            return w_ref[part, first // few, at, :].reshape(-1, width)
        return jnp.concatenate(
            [w_ref[:, upper, at, :].reshape(-1, width) for upper in range(count // few)], axis=0
        )

    w_in = [blocks_of(0, parts, slice(c * ROWS, (c + 1) * ROWS)) for c in range(slabs)]
    w_out = [blocks_of(c * share, share, out_rows) for c in range(slabs)]
    w_o = blocks_of(0, parts, whole_rows)

    def d_hidden(c):
        return dot_nt(dy_ref[...], w_out[c])

    def between(act, d_hid):
        square = act * act
        curve = jnp.tanh(act * (root + (root * 0.044715) * square))
        gate = 0.5 + 0.5 * curve
        hid = act * gate
        slope = gate + hid * (1.0 - curve) * (root + (3.0 * root * 0.044715) * square)
        return hid.astype(bf16), (d_hid * slope).astype(bf16)

    o_t = o_ref[...]
    x_one = x_ref[...].astype(f32) + dot(o_t.T, w_o)
    d_hid = d_hidden(0)
    dyt_scr[...] = dy_ref[...].T
    hat, rstd = norm_stats(x_one)
    h_two = (hat * norms_ref[2:3, :] + norms_ref[3:4, :]).astype(bf16)
    h_scr[...] = h_two
    hat_scr[...] = hat
    y_scr[...] = x_one
    act = dot(h_scr[...], w_in[0])
    ht_scr[...] = h_two.T
    for c in range(slabs):
        this_act, this_d = act, d_hid
        if c + 1 < slabs:
            d_hid = d_hidden(c + 1)
            act = dot(h_scr[...], w_in[c + 1])
        hid, d_act = between(this_act, this_d)
        more = dot_nt(d_act, w_in[c])
        dh_scr[...] = more if c == 0 else dh_scr[...] + more
        y_scr[...] += dot(hid, w_out[c])
        cols = slice(c * width, (c + 1) * width)
        add_to(gt_scr, (slice(None), cols), dot(dyt_scr[...], hid))
        slab = (slice(None), slice(c * ROWS, (c + 1) * ROWS), slice(None))
        add_to(g_ref, slab, dot(ht_scr[...], d_act).reshape(parts, ROWS, width))
    d_h = dh_scr[...]
    hat = hat_scr[...]
    d_x = dy_ref[...].astype(f32) + norm_back(d_h, hat, rstd, norms_ref[2:3, :])
    d_z = d_x.astype(bf16)
    dx_ref[...] = d_z
    do_ref[...] = dot_nt(d_z, w_o).astype(bf16)
    add_to(g_ref, (slice(None), whole_rows, slice(None)), dot(o_t, d_z).reshape(parts, ROWS, width))
    add_to(g_norm_ref, (slice(2, 3), slice(None)), jnp.sum(d_h * hat, axis=0, keepdims=True))
    add_to(g_norm_ref, (slice(3, 4), slice(None)), jnp.sum(d_h, axis=0, keepdims=True))
    out_ref[...] = y_scr[...].astype(bf16)

    @pl.when(fresh)
    def _():
        g_norm_ref[0:2, :] = jnp.zeros_like(g_norm_ref[0:2, :])
        g_norm_ref[4:, :] = jnp.zeros_like(g_norm_ref[4:, :])

    @pl.when(step == pl.num_programs(0) - 1)
    def _():
        for c in range(slabs):
            g_ref[c * share : (c + 1) * share, out_rows, :] = gt_scr[
                :, c * width : (c + 1) * width
            ].T.reshape(share, slabs * ROWS, width)
        first = (slabs + 1) * ROWS
        halves(
            place,
            (sent_in, sent_out, kept_in, kept_out),
            lambda i, part: g_ref[i, first:] if part else g_ref[i, :first],
            sorted_bits,
        )


def halves(place, refs, block, sorted_bits):
    mine = place[0] & 1
    parts = len(refs) // 2
    high = refs[0].shape[0] // 2

    def one(i, carry):
        low, next_low, rest = i & 1, (i >> 1) & 1, i >> 2
        spots = [low * high + next_low * (high // 2) + rest, next_low * high + low * (high // 2) + rest]
        for part in range(parts):
            at = spots[part] if sorted_bits else i
            refs[part][at] = block(2 * i + 1 - mine, part).astype(bf16)
            refs[parts + part][at] = block(2 * i + mine, part)
        return carry

    lax.fori_loop(0, 2 * high, one, 0)


def ffn(place, x, dy, o_t, norms, w_two, sorted_bits):
    slot, width = x.shape
    hidden = (w_two.shape[2] // ROWS - 1) // 2 * width
    blocks = (w_two.shape[0] * w_two.shape[1], *w_two.shape[2:])
    grid = slot // TILE
    first = hidden // width * ROWS + ROWS
    half_in = (blocks[0] // 2, first, width)
    half_out = (blocks[0] // 2, blocks[1] - first, width)
    row = pl.BlockSpec((TILE, width), lambda i: (i, 0))

    def once(shape):
        return pl.BlockSpec(shape, lambda i: (0,) * len(shape), pipeline_mode=pl.Buffered(1))

    return pl.pallas_call(
        functools.partial(ffn_kernel, sorted_bits=sorted_bits),
        grid=(grid,),
        in_specs=[
            smem(),
            row,
            row,
            pl.BlockSpec((width, TILE), lambda i: (0, i)),
            once(norms.shape),
            once(w_two.shape),
        ],
        out_specs=[
            row, row, row,
            once(half_in), once(half_out), once(half_in), once(half_out),
            once((8, width)),
        ],
        out_shape=[
            pltpu.HBM((slot, width), bf16),
            pltpu.HBM((slot, width), bf16),
            pltpu.HBM((slot, width), bf16),
            pltpu.HBM(half_in, bf16),
            pltpu.HBM(half_out, bf16),
            pltpu.HBM(half_in, f32),
            pltpu.HBM(half_out, f32),
            pltpu.HBM((8, width), f32),
        ],
        scratch_shapes=[
            pltpu.VMEM(blocks, f32),
            pltpu.VMEM((TILE, width), bf16),
            pltpu.VMEM((width, TILE), bf16),
            pltpu.VMEM((width, TILE), bf16),
            pltpu.VMEM((TILE, width), f32),
            pltpu.VMEM((TILE, width), f32),
            pltpu.VMEM((TILE, width), f32),
            pltpu.VMEM((width, hidden), f32),
        ],
        compiler_params=params(42),
        cost_estimate=pl.CostEstimate(
            flops=2 * slot * width * (3 * width + 6 * hidden),
            bytes_accessed=slot * width * 14,
            transcendentals=slot * hidden,
        ),
        name="ffn",
    )(place, *in_hbm(x, dy, o_t), norms, *in_hbm(w_two))


def project_back_kernel(
    place, lens, x_ref, dx_ref, du_ref, norms_ref, w_ref, g_sort_ref, g_two_ref, *refs, slot,
    sorted_bits,
):
    *d_refs, grad_ref, sent_a, sent_b, kept_a, kept_b, g_ref, g_norm_ref = refs
    tile, width = x_ref.shape
    step = pl.program_id(0)

    @pl.when(step == 0)
    def _():
        g_ref[...] = jnp.zeros_like(g_ref)
        g_norm_ref[...] = jnp.zeros_like(g_norm_ref)

    pairs = width // LANES
    ends = ends_of(lens, slot)
    blocks = SUB // BLOCK
    starts = range(0, tile, SUB)
    d_hs, hats, rstds, h_ones = [], [], [], []
    for r in starts:
        rows = slice(r, r + SUB)
        places = step * tile + r + iota((SUB, 1), 0)
        live = places < end_at(places, ends, slot)
        d_u = du_ref[r // BLOCK : r // BLOCK + blocks, :].reshape(blocks, 1, width)
        d_h = jnp.broadcast_to(d_u, (blocks, BLOCK, width)).reshape(SUB, width)
        d_h = jnp.where(live, d_h, 0.0)
        for part in range(3):
            cols = slice(part * width, (part + 1) * width)
            d_part = jnp.concatenate(
                [ref[rows, :] for ref in d_refs[part * pairs : (part + 1) * pairs]], axis=1
            )
            d_h = d_h + dot_nt(d_part, w_ref[:, cols])
        d_hs.append(d_h)
        hat, rstd = norm_stats(x_ref[rows, :].astype(f32))
        hats.append(hat)
        rstds.append(rstd)
        h_ones.append((hat * norms_ref[0:1, :] + norms_ref[1:2, :]).astype(bf16))
    h_one = jnp.concatenate(h_ones, axis=0)

    def back(at):
        rows = slice(at * SUB, (at + 1) * SUB)
        g_norm_ref[0:1, :] += jnp.sum(d_hs[at] * hats[at], axis=0, keepdims=True)
        g_norm_ref[1:2, :] += jnp.sum(d_hs[at], axis=0, keepdims=True)
        grad_ref[rows, :] = dx_ref[rows, :].astype(f32) + norm_back(
            d_hs[at], hats[at], rstds[at], norms_ref[0:1, :]
        )

    done = 0
    for part in range(3):
        cols = slice(part * width, (part + 1) * width)
        d_part = jnp.concatenate([ref[...] for ref in d_refs[part * pairs : (part + 1) * pairs]], axis=1)
        g_ref[:, cols] += dot_tn(h_one, d_part)
        until = len(starts) * (part + 1) // 3
        for at in range(done, until):
            back(at)
        done = until

    @pl.when(step == pl.num_programs(0) - 1)
    def _():
        g_ref[:, 3 * width : 3 * width + LANES] = g_sort_ref[...]
        small = g_norm_ref[...] + g_two_ref[...]
        rest = jnp.zeros((LANES - small.shape[0], width), f32)
        g_ref[:, 3 * width + LANES :] = jnp.concatenate([small, rest], axis=0).T
        cols = sent_a.shape[2]
        halves(
            place,
            (sent_a, sent_b, kept_a, kept_b),
            lambda i, part: g_ref[
                pl.ds(pl.multiple_of(i * ROWS, ROWS), ROWS), part * cols : (part + 1) * cols
            ],
            sorted_bits,
        )


def project_back(
    place, lens, x, d_x, d_q, d_k, d_v, d_u, norms, w_one, g_sort, g_two, sorted_bits
):
    slot, width = x.shape
    grid = slot // WIDE
    row = pl.BlockSpec((WIDE, width), lambda i: (i, 0))
    half = (width // ROWS // 2, ROWS, w_one.shape[1] // 2)

    def once(shape):
        return pl.BlockSpec(shape, lambda i: (0,) * len(shape), pipeline_mode=pl.Buffered(1))

    return pl.pallas_call(
        functools.partial(project_back_kernel, slot=slot, sorted_bits=sorted_bits),
        grid=(grid,),
        in_specs=[
            smem(),
            smem(),
            row,
            row,
            pl.BlockSpec((WIDE // BLOCK, width), lambda i: (i, 0)),
            once(norms.shape),
            once(w_one.shape),
            once(g_sort.shape),
            once(g_two.shape),
        ]
        + [pl.BlockSpec((WIDE, LANES), lambda i: (i, 0))] * (3 * width // LANES),
        out_specs=[row] + [once(half)] * 4,
        out_shape=[
            jax.ShapeDtypeStruct((slot, width), f32),
            jax.ShapeDtypeStruct(half, bf16),
            jax.ShapeDtypeStruct(half, bf16),
            jax.ShapeDtypeStruct(half, f32),
            jax.ShapeDtypeStruct(half, f32),
        ],
        scratch_shapes=[pltpu.VMEM(w_one.shape, f32), pltpu.VMEM((8, width), f32)],
        compiler_params=params(22),
        cost_estimate=pl.CostEstimate(
            flops=2 * slot * width * 6 * width, bytes_accessed=slot * width * 18, transcendentals=0
        ),
        name="project_back",
    )(place, lens, *in_hbm(x, d_x), d_u, norms, w_one, g_sort, g_two, *d_q, *d_k, *d_v)


def pack_kernel(wqkv, wo, wsort, win, wout, norms_t, one_ref, two_ref):
    rows, wide = wqkv.shape
    width = wo.shape[1]
    one_ref[:, :wide] = wqkv[...].astype(bf16)
    one_ref[:, wide : wide + LANES] = wsort[...].astype(bf16)
    few = norms_t.shape[0]
    tall = jnp.concatenate([norms_t[...], jnp.zeros((LANES - few, rows), f32)], axis=0)
    one_ref[:, wide + LANES :] = tall.T.astype(bf16)
    slabs = win.shape[1] // width
    for c in range(slabs):
        two_ref[c * rows : (c + 1) * rows, :] = win[:, c * width : (c + 1) * width].astype(bf16)
    two_ref[slabs * rows : (slabs + 1) * rows, :] = wo[...].astype(bf16)
    two_ref[(slabs + 1) * rows :, :] = wout[...].astype(bf16)


def pack(masters):
    wqkv, wo, wsort, win, wout, norms = masters
    rows = wqkv.shape[0]
    return pl.pallas_call(
        pack_kernel,
        out_shape=[
            jax.ShapeDtypeStruct((rows, wqkv.shape[1] + 2 * LANES), bf16),
            jax.ShapeDtypeStruct((rows * (win.shape[1] // wo.shape[1] + 1) + wout.shape[0], wo.shape[1]), bf16),
        ],
        compiler_params=params(8),
        name="pack",
    )(*in_hbm(wqkv, wo, wsort, win, wout), norms.T)


def adamw_kernel(*refs, ones, twos):
    one_ref = sum(ref[...].astype(f32) for ref in refs[:ones])
    two_ref = sum(ref[...].astype(f32) for ref in refs[ones : ones + twos])
    refs = refs[ones + twos :]
    masters, moments, squares, outs = refs[:6], refs[6:12], refs[12:18], refs[18:]
    rows, width = masters[1].shape
    wide = masters[0].shape[1]
    slabs = masters[3].shape[1] // width
    few = masters[5].shape[0]
    norm_grad = one_ref[:, wide + LANES :].T[:few, :]
    grads = (
        one_ref[:, :wide],
        two_ref[slabs * rows : (slabs + 1) * rows, :],
        one_ref[:, wide : wide + LANES],
        jnp.concatenate([two_ref[c * rows : (c + 1) * rows, :] for c in range(slabs)], axis=1),
        two_ref[(slabs + 1) * rows :, :],
        norm_grad,
    )
    for i in range(6):
        weight, grad = masters[i][...], grads[i]
        moment = beta_one * moments[i][...] + (1.0 - beta_one) * grad
        square = beta_two * squares[i][...] + (1.0 - beta_two) * grad * grad
        m_hat = moment / (1.0 - beta_one**STEP)
        s_hat = square / (1.0 - beta_two**STEP)
        outs[3 * i][...] = weight - rates[i] * (
            m_hat / (jnp.sqrt(s_hat) + adam_eps) + decay * weight
        )
        outs[3 * i + 1][...] = moment
        outs[3 * i + 2][...] = square


def adamw(one, two, masters, moments, squares):
    flip = lambda group: (*group[:5], group[5].T)
    args = (*one, *two, *flip(masters), *flip(moments), *flip(squares))
    shapes = [a.shape for a in flip(masters)]
    outs = pl.pallas_call(
        functools.partial(adamw_kernel, ones=len(one), twos=len(two)),
        out_shape=[jax.ShapeDtypeStruct(shape, f32) for shape in shapes for _ in range(3)],
        compiler_params=params(12),
        name="adamw",
    )(*args)
    return (*outs[:15], *[o.T for o in outs[15:]])


def regroup(gathered, rows, slabs):
    size, width = gathered.shape[0], gathered.shape[-1]
    times = ROWS // rows
    block = gathered.reshape(size // times, times, 2 * slabs + 1, rows, width)
    inner = block[:, :, : slabs + 1].transpose(0, 2, 1, 3, 4)
    outer = block[:, :, slabs + 1 :]
    return jnp.concatenate(
        [
            inner.reshape(size // times, (slabs + 1) * ROWS, width),
            outer.reshape(size // times, slabs * ROWS, width),
        ],
        axis=1,
    )[:, None]


def device_halves(place, sent, kept, size, rows, slabs, axis):
    if rows == ROWS:
        return sent, kept
    cut = kept[0].shape[axis + 1] * rows // ROWS if slabs else kept[0].shape[axis + 1]
    sent, kept = jnp.concatenate(sent, axis=axis + 1), jnp.concatenate(kept, axis=axis + 1)
    mine = place[0] & 1
    low = jnp.where(mine == 0, kept, sent.astype(f32))
    high = jnp.where(mine == 0, sent.astype(f32), kept)
    grads = jnp.stack([low, high], axis=1).reshape((-1,) + kept.shape[1:])
    times = ROWS // rows
    width = grads.shape[-1]
    wide = (slabs + 1) * ROWS
    inner = grads[:, :wide].reshape(size // times, slabs + 1, times, rows, width)
    outer = grads[:, wide:].reshape(size // times, times, slabs, rows, width)
    block = jnp.concatenate([inner.transpose(0, 2, 1, 3, 4), outer], axis=2)
    block = block.reshape(size // 2, 2, (2 * slabs + 1) * rows, width)
    count = size.bit_length() - 1
    results = []
    for index, kind in ((1 - mine, bf16), (mine, f32)):
        half = lax.dynamic_index_in_dim(block, index, 1, keepdims=False).astype(kind)
        for part, lead in zip(jnp.split(half, [cut], axis=axis + 1), ((1, 2), (2, 1))):
            bits = part.reshape((2,) * (count - 1) + part.shape[1:])
            order = [count - 1 - bit for bit in lead] + list(range(count - 3))
            order += list(range(count - 1, bits.ndim))
            results.append(bits.transpose(order).reshape(part.shape))
    return results[:2], results[2:]


def swap(value, mask, size):
    return lax.ppermute(value, "dp", [(i, i ^ mask) for i in range(size)])


def masks_of(bits):
    return [sum(((turn >> at) & 1) << bit for at, bit in enumerate(bits)) for turn in range(2 ** len(bits))]


def fours(count):
    return [tuple(range(bit, min(bit + 2, count))) for bit in range(3, count, 2)]


def gather(block, size):
    held = block[None]
    for bits in fours(size.bit_length() - 1)[::-1] + [(2,), (1,)]:
        came = [swap(held, mask, size) for mask in masks_of(bits)[1:]]
        held = jnp.stack([held, *came], axis=1).reshape((-1,) + block.shape)
    return held, swap(held, 1, size)


class ScatterSum:
    def __init__(self, sent, kept, size, axis):
        self.size, self.axis = size, axis
        self.place = lax.axis_index("dp")
        self.plan = [(1, 2), (2, 1)] + fours(size.bit_length() - 1)[::-1]
        self.kept, self.sent, self.masks = list(kept), list(sent), [1, 1]

    def send(self):
        self.came = [swap(sent, mask, self.size) for sent, mask in zip(self.sent, self.masks)]

    def cut(self, ways, index, values):
        parts = [value.reshape((ways, -1) + value.shape[1:]) for value in values]
        parts = [lax.dynamic_index_in_dim(part, index, 0, keepdims=False) for part in parts]
        return sum(part.astype(f32) for part in parts)

    def step(self):
        bits = self.plan.pop(0)
        if bits[0] < 3:
            kept, came = self.kept, self.came
            mine = [(self.place >> bit) & 1 for bit in bits]
            self.kept = [self.cut(2, m, pair) for m, pair in zip(mine, zip(kept, came))]
            self.sent = [self.cut(2, 1 - m, pair).astype(bf16) for m, pair in zip(mine, zip(kept, came))]
            self.masks = [1 << bit for bit in bits]
            return
        values = [*self.kept, *self.came]
        if len(self.kept) == 2:
            values = [jnp.concatenate(pair, axis=self.axis + 1) for pair in (self.kept, self.came)]
        ways = 2 ** len(bits)
        mine = (self.place >> bits[0]) & (ways - 1)
        self.kept = [self.cut(ways, mine, values)]
        self.sent = [self.cut(ways, mine ^ turn, values).astype(bf16) for turn in range(1, ways)]
        self.masks = masks_of(bits)[1:]

    def after(self, values):
        self.came, values = lax.optimization_barrier((self.came, values))
        return values

    def before(self, values):
        self.sent, values = lax.optimization_barrier((self.sent, values))
        return values

    def last(self):
        return [value.reshape(value.shape[1:]) for value in (*self.kept, *self.came)]


def body(size, x, dy, lens, partner, *state):
    slot, width = x.shape
    masters, moments, squares = state[:6], state[6:12], state[12:]
    rows = masters[0].shape[0]
    slabs = masters[3].shape[1] // width
    place = lax.axis_index("dp").astype(jnp.int32).reshape((1,))
    pack_one, pack_two = pack(masters)
    near, far = gather(pack_one, size)
    if rows == ROWS:
        w_two = lax.all_gather(pack_two, "dp", axis=0)[:, None]
    else:
        w_two = regroup(lax.all_gather(pack_two, "dp", axis=0), rows, slabs)

    q, k, v, u, norms, w_one = project(place, lens, x, near, far)
    bias, steps = sort_net(lens, u, w_one, partner, slot)
    o_t, probs = attend(lens, partner, bias, q, k, v)
    direct = rows == ROWS
    out, d_x, d_o, *parts, g_two = ffn(place, x, dy, o_t, norms, w_two, direct)
    sent, kept = device_halves(place, parts[:2], parts[2:], size, rows, slabs, 0)
    two = ScatterSum(sent, kept, size, 0)
    two.send()

    def back(pair):
        return attend_back(pair, partner, q, d_o, probs, k, v)

    def next_stage(values):
        two.step()
        values = two.before(values)
        two.send()
        return values

    back_0 = two.after(back(0))
    q, d_o = next_stage((q, d_o))
    back_1, back_2 = two.after((back(1), back(2)))
    q, d_o = next_stage((q, d_o))
    back_3 = two.after(back(3))
    u, back_3 = next_stage((u, back_3))
    d_q, d_k, d_v, d_bias = zip(back_0, back_1, back_2, back_3)
    d_u, g_sort = sort_back(lens, u, w_one, partner, d_bias, steps, slot)
    while two.plan:
        d_u = next_stage(two.after(d_u))
    grad_in, *parts = project_back(
        place, lens, x, d_x, d_q, d_k, d_v, d_u, norms, w_one, g_sort, g_two, direct
    )
    grad_in, parts = two.after((grad_in, parts))
    sent, kept = device_halves(place, parts[:2], parts[2:], size, rows, 0, 1)
    one = ScatterSum(sent, kept, size, 1)
    one.send()
    while one.plan:
        one.step()
        one.send()
    outs = adamw(one.last(), two.last(), masters, moments, squares)
    return (out, grad_in, *outs)


def solution(mesh):
    spec = P("dp", None)
    return jax.shard_map(
        functools.partial(body, mesh.shape["dp"]),
        mesh=mesh,
        in_specs=(spec,) * 22,
        out_specs=(spec,) * 20,
        check_vma=False,
    )
```

```python
import functools
import math

import jax
import jax.numpy as jnp
from jax import lax
from jax.experimental import pallas as pl
from jax.experimental.pallas import tpu as pltpu
from jax.sharding import PartitionSpec as P

HEADS = 8
HEAD = 64
SORT = 64
BLOCK = 32
SINK = 8
STEP = 10
TILE = 512
WIDE = 1024
ROWS = 16
ABREAST = 4
SUB = 256
GROUP = 128
LANES = 128

highest = lax.Precision.HIGHEST
masked = -1000000000.0
norm_eps = 1e-05
beta_one = 0.9
beta_two = 0.999
adam_eps = 1e-08
decay = 0.01
rates = (0.05, 0.15, 0.05, 0.05, 0.025, 0.5)
f32 = jnp.float32
bf16 = jnp.bfloat16


def dot(left, right, precision=None):
    return jnp.dot(left, right, precision=precision, preferred_element_type=f32)


def dot_nt(left, right, precision=None):
    return lax.dot_general(
        left, right, (((1,), (1,)), ((), ())), precision=precision, preferred_element_type=f32
    )


def dot_tn(left, right, precision=None):
    return lax.dot_general(
        left, right, (((0,), (0,)), ((), ())), precision=precision, preferred_element_type=f32
    )


def iota(shape, axis):
    return lax.broadcasted_iota(jnp.int32, shape, axis)


def ends_of(lens, slot):
    quarter = slot // 4
    is_long = lens[0, 0] > quarter
    return [jnp.where(is_long, lens[0, 0], k * quarter + lens[0, k]) for k in range(4)]


def end_at(places, ends, slot):
    quarter = slot // 4
    return jnp.where(
        places < 2 * quarter,
        jnp.where(places < quarter, ends[0], ends[1]),
        jnp.where(places < 3 * quarter, ends[2], ends[3]),
    )


def norm_stats(value):
    center = value - jnp.mean(value, axis=-1, keepdims=True)
    spread = jnp.mean(center * center, axis=-1, keepdims=True)
    rstd = lax.rsqrt(spread + norm_eps)
    return center * rstd, rstd


def norm_back(grad, hat, rstd, gain):
    d_hat = grad * gain
    mean_d = jnp.mean(d_hat, axis=-1, keepdims=True)
    mean_dh = jnp.mean(d_hat * hat, axis=-1, keepdims=True)
    return rstd * (d_hat - mean_d - hat * mean_dh)


def params(mebibytes):
    return pltpu.CompilerParams(vmem_limit_bytes=mebibytes << 20)


def whole(shape):
    return pl.BlockSpec(shape, lambda *_: (0,) * len(shape))


def in_hbm(*values):
    return [pltpu.with_memory_space_constraint(value, pltpu.HBM) for value in values]


def smem():
    return pl.BlockSpec(memory_space=pltpu.SMEM)


def project_kernel(
    place, lens, x_ref, near_ref, far_ref, q_ref, k_ref, v_ref, u_ref, norms_ref, w_ref, *, slot
):
    tile, width = x_ref.shape
    base = pl.program_id(0) * tile

    @pl.when(pl.program_id(0) == 0)
    def _():
        rows = near_ref.shape[1]
        mine = place[0] & 1
        for half in range(near_ref.shape[0]):
            at = (place[0] >> 1) ^ half
            w_ref[2 * half * rows : (2 * half + 1) * rows, :] = jnp.where(
                mine == 0, near_ref[at], far_ref[at]
            )
            w_ref[(2 * half + 1) * rows : (2 * half + 2) * rows, :] = jnp.where(
                mine == 0, far_ref[at], near_ref[at]
            )

    @pl.when(pl.program_id(0) == 0)
    def _():
        norms_ref[...] = w_ref[:, 3 * width + LANES :].astype(f32).T[:8, :]

    parts = []
    for r in range(0, tile, SUB):
        hat, _ = norm_stats(x_ref[r : r + SUB, :].astype(f32))
        parts.append((hat * norms_ref[0:1, :] + norms_ref[1:2, :]).astype(bf16))
        for part, ref in enumerate((q_ref, k_ref, v_ref)):
            ref[r : r + SUB, :] = dot(parts[-1], w_ref[:, part * width : (part + 1) * width]).astype(bf16)
    h_one = jnp.concatenate(parts, axis=0)
    blocks = tile // BLOCK
    at = iota((blocks, tile), 1)
    places = at + base
    live = places < end_at(places, ends_of(lens, slot), slot)
    own = (at // BLOCK) == iota((blocks, tile), 0)
    pick = jnp.where(live & own, 1.0, 0.0).astype(bf16)
    u_ref[...] = dot(pick, h_one)


def project(place, lens, x, near, far):
    slot, width = x.shape
    w_shape = (2 * near.shape[0] * near.shape[1], near.shape[2])
    grid = slot // WIDE
    row = pl.BlockSpec((WIDE, width), lambda i: (i, 0))
    out = jax.ShapeDtypeStruct((slot, width), bf16)
    return pl.pallas_call(
        functools.partial(project_kernel, slot=slot),
        grid=(grid,),
        in_specs=[smem(), smem(), row, whole(near.shape), whole(far.shape)],
        out_specs=[
            row,
            row,
            row,
            pl.BlockSpec((WIDE // BLOCK, width), lambda i: (i, 0)),
            whole((8, width)),
            whole(w_shape),
        ],
        out_shape=[
            out,
            out,
            out,
            jax.ShapeDtypeStruct((slot // BLOCK, width), f32),
            jax.ShapeDtypeStruct((8, width), f32),
            jax.ShapeDtypeStruct(w_shape, bf16),
        ],
        compiler_params=params(12),
        cost_estimate=pl.CostEstimate(
            flops=2 * slot * width * 3 * width, bytes_accessed=slot * width * 8, transcendentals=0
        ),
        name="project",
    )(place, lens, *in_hbm(x, near, far))


def sort_parts(lens, u_ref, ws_ref, slot):
    blocks = u_ref.shape[0]
    ends = ends_of(lens, slot)
    quarter = slot // 4
    is_long = lens[0, 0] > quarter

    def group_of(axis, shape):
        index = iota(shape, axis)
        start = index * BLOCK
        live = start < end_at(start, ends, slot)
        member = jnp.where(is_long, 0, start // quarter)
        return jnp.where(live, member, 4 + index)

    same = group_of(0, (blocks, blocks)) == group_of(1, (blocks, blocks))
    start = iota((blocks, 1), 0) * BLOCK
    count = jnp.clip(end_at(start, ends, slot) - start, 0, BLOCK).astype(f32)
    scale = lax.rsqrt(jnp.maximum(count, 1.0))
    summary = u_ref[...] * scale
    w_sort = ws_ref[...].astype(f32)
    sort_q = dot(summary, w_sort[:, :SORT], highest)
    sort_k = dot(summary, w_sort[:, SORT:], highest)
    return same, scale, summary, w_sort, sort_q, sort_k


def sort_columns(w_one):
    return pl.BlockSpec((w_one.shape[0], 2 * SORT), lambda i: (0, 3 * w_one.shape[0] // (2 * SORT)))


def column_of(row, eye):
    return jnp.sum(jnp.where(eye, row, 0.0), axis=1, keepdims=True)


def sort_kernel(lens, u_ref, ws_ref, partner_ref, bias_ref, steps_ref, *, slot):
    blocks = u_ref.shape[0]
    same, _, _, _, sort_q, sort_k = sort_parts(lens, u_ref, ws_ref, slot)
    raw = dot_nt(sort_q, sort_k, highest)
    logits = jnp.where(same, raw / math.sqrt(SORT), masked)

    def normalize(value, axis):
        top = jnp.max(value, axis=axis, keepdims=True)
        return value - (top + jnp.log(jnp.sum(jnp.exp(value - top), axis=axis, keepdims=True)))

    for turn in range(SINK):
        logits = normalize(logits, 1)
        steps_ref[2 * turn] = logits
        logits = normalize(logits, 0)
        steps_ref[2 * turn + 1] = logits
    eye = iota((blocks, blocks), 0) == iota((blocks, blocks), 1)
    members = jnp.sum(same.astype(f32), axis=1, keepdims=True)
    partner = column_of(partner_ref[...].astype(f32), eye)
    pick = partner == iota((blocks, blocks), 1).astype(f32)
    bias = jnp.sum(jnp.where(pick, logits, 0.0), axis=1, keepdims=True) + jnp.log(members)
    bias_ref[...] = jnp.sum(jnp.where(eye, bias, 0.0), axis=0, keepdims=True)


def sort_net(lens, u, w_sort, partner, slot):
    blocks = u.shape[0]
    return pl.pallas_call(
        functools.partial(sort_kernel, slot=slot),
        in_specs=[smem(), whole(u.shape), sort_columns(w_sort), whole(partner.shape)],
        out_specs=[whole((1, blocks)), whole((2 * SINK, blocks, blocks))],
        out_shape=[
            jax.ShapeDtypeStruct((1, blocks), f32),
            jax.ShapeDtypeStruct((2 * SINK, blocks, blocks), f32),
        ],
        grid=(1,),
        compiler_params=params(8),
        cost_estimate=pl.CostEstimate(flops=10**8, bytes_accessed=10**7, transcendentals=10**6),
        name="sort_net",
    )(lens, u, w_sort, partner)


def sort_back_kernel(
    lens, u_ref, ws_ref, partner_ref, steps_ref, *refs, slot
):
    *d_bias_refs, d_u_ref, grad_ref = refs
    blocks = u_ref.shape[0]
    same, scale, summary, w_sort, sort_q, sort_k = sort_parts(lens, u_ref, ws_ref, slot)
    eye = iota((blocks, blocks), 0) == iota((blocks, blocks), 1)
    partner = column_of(partner_ref[...].astype(f32), eye)
    pick = partner == iota((blocks, blocks), 1).astype(f32)
    d_bias = column_of(sum(ref[...] for ref in d_bias_refs), eye)
    d_logits = jnp.where(pick, d_bias, 0.0)
    for turn in reversed(range(SINK)):
        for axis, step in ((0, 2 * turn + 1), (1, 2 * turn)):
            share = jnp.exp(steps_ref[step])
            d_logits = d_logits - share * jnp.sum(d_logits, axis=axis, keepdims=True)
    d_raw = jnp.where(same, d_logits, 0.0) / math.sqrt(SORT)
    d_sort_q = dot(d_raw, sort_k, highest)
    d_sort_k = dot_tn(d_raw, sort_q, highest)
    d_sort = jnp.concatenate([d_sort_q, d_sort_k], axis=1)
    grad_ref[...] = dot_tn(summary, d_sort, highest)
    d_u_ref[...] = dot_nt(d_sort, w_sort, highest) * scale


def sort_back(lens, u, w_sort, partner, d_bias, steps, slot):
    blocks, width = u.shape
    return pl.pallas_call(
        functools.partial(sort_back_kernel, slot=slot),
        in_specs=[
            smem(),
            whole(u.shape),
            sort_columns(w_sort),
            whole(partner.shape),
            whole(steps.shape),
            *[whole(part.shape) for part in d_bias],
        ],
        out_specs=[whole((blocks, width)), whole((width, 2 * SORT))],
        out_shape=[
            jax.ShapeDtypeStruct((blocks, width), f32),
            jax.ShapeDtypeStruct((width, 2 * SORT), f32),
        ],
        grid=(1,),
        compiler_params=params(8),
        cost_estimate=pl.CostEstimate(flops=10**8, bytes_accessed=10**7, transcendentals=10**6),
        name="sort_back",
    )(lens, u, w_sort, partner, steps, *d_bias)


def lane_block(rows):
    return (iota((rows, 2 * GROUP), 1) % GROUP) // BLOCK


def compact(full):
    at = lane_block(BLOCK)
    part = [full[c * BLOCK : (c + 1) * BLOCK] for c in range(GROUP // BLOCK)]
    return jnp.where(
        at < 2,
        jnp.where(at < 1, part[0], part[1]),
        jnp.where(at < 3, part[2], part[3]),
    )


def diagonal_mask():
    rows = 2 * GROUP
    return jnp.where((iota((rows, rows), 0) % GROUP) // BLOCK == lane_block(rows), 1.0, 0.0).astype(bf16)


def spread(own, far, mask):
    own, far = own.astype(bf16), far.astype(bf16)
    times = GROUP // BLOCK
    return jnp.concatenate([own] * times + [far] * times, axis=0) * mask


def head_stack(pair, lanes):
    zero = jnp.zeros_like(pair)
    return jnp.concatenate(
        [jnp.where(lanes < HEAD, pair, zero), jnp.where(lanes < HEAD, zero, pair)], axis=0
    )


def head_lanes():
    return iota((GROUP, LANES), 1)


def by_lane(values):
    at = iota((1, GROUP), 1) // BLOCK
    return jnp.where(
        at < 2,
        jnp.where(at < 1, values[0], values[1]),
        jnp.where(at < 3, values[2], values[3]),
    )


def gather_far(dst, src, partners):
    for c, p in enumerate(partners):
        dst[GROUP + c * BLOCK : GROUP + (c + 1) * BLOCK, :] = src[pl.ds(pl.multiple_of(p * BLOCK, BLOCK), BLOCK), :]


def attend_kernel(lens, partner, bias, q_ref, k_ref, v_ref, o_ref, p_ref, mask_ref, *, slot):
    tile, width = q_ref.shape
    step = pl.program_id(0)
    pairs = width // LANES
    per = GROUP // BLOCK

    @pl.when(step == 0)
    def _():
        mask_ref[...] = diagonal_mask()

    ends = ends_of(lens, slot)
    scale = 1.0 / math.sqrt(HEAD)

    def some_groups(turn, carry):
        mask = mask_ref[...]
        lanes = head_lanes()
        key = iota((BLOCK, GROUP), 0)
        query = iota((BLOCK, GROUP), 1)
        work = []
        for part in range(ABREAST):
            g = turn * ABREAST + part
            first = step * (tile // BLOCK) + g * per
            partners = [partner[0, first + c] for c in range(per)]
            rows = pl.ds(pl.multiple_of(first * BLOCK, GROUP), GROUP)
            q_rows = pl.ds(pl.multiple_of(g * GROUP, GROUP), GROUP)
            spans = [rows] + [pl.ds(pl.multiple_of(p * BLOCK, BLOCK), BLOCK) for p in partners]
            own_place = (first + query // BLOCK) * BLOCK + key
            far_place = by_lane(partners) * BLOCK + key
            own_live = (own_place < end_at(own_place, ends, slot)) | (query % BLOCK == key)
            far_live = far_place < end_at(far_place, ends, slot)
            own_live = jnp.concatenate([own_live.astype(f32)] * 2, axis=1) > 0.5
            far_live = jnp.concatenate([far_live.astype(f32)] * 2, axis=1) > 0.5
            lane_bias = by_lane([bias[0, first + c] for c in range(per)])
            lane_bias = jnp.concatenate([lane_bias] * 2, axis=1)
            for pair in range(pairs):
                work.append((g, pair, spans, q_rows, own_live, far_live, lane_bias))
        scores = []
        for g, pair, spans, q_rows, *_ in work:
            cols = slice(pair * LANES, (pair + 1) * LANES)
            q_two = head_stack(q_ref[q_rows, cols], lanes)
            k_all = jnp.concatenate([k_ref[at, cols] for at in spans], axis=0)
            scores.append(dot_nt(k_all, q_two))
        probs = []
        for score, (g, pair, spans, q_rows, own_live, far_live, lane_bias) in zip(scores, work):
            own = jnp.where(own_live, compact(score[:GROUP]) * scale, masked)
            far = jnp.where(far_live, compact(score[GROUP:]) * scale + lane_bias, masked)
            top = jnp.maximum(
                jnp.max(own, axis=0, keepdims=True), jnp.max(far, axis=0, keepdims=True)
            )
            own = jnp.exp(own - top)
            far = jnp.exp(far - top)
            total = jnp.sum(own, axis=0, keepdims=True) + jnp.sum(far, axis=0, keepdims=True)
            inverse = 1.0 / total
            probs.append(((own * inverse).astype(bf16), (far * inverse).astype(bf16)))
        mixes = []
        for (own, far), (g, pair, spans, *_) in zip(probs, work):
            cols = slice(pair * LANES, (pair + 1) * LANES)
            v_all = jnp.concatenate([v_ref[at, cols] for at in spans], axis=0)
            mixes.append(dot(v_all.T, spread(own, far, mask)))
        for mixed, (own, far), (g, pair, spans, q_rows, *_) in zip(mixes, probs, work):
            at = pl.multiple_of(g * 2 * BLOCK, 2 * BLOCK)
            p_ref[pair, pl.ds(at, BLOCK), :] = own
            p_ref[pair, pl.ds(at + BLOCK, BLOCK), :] = far
            o_ref[pair * LANES : pair * LANES + HEAD, q_rows] = mixed[:HEAD, :GROUP].astype(bf16)
            o_ref[pair * LANES + HEAD : (pair + 1) * LANES, q_rows] = mixed[HEAD:, GROUP:].astype(bf16)
        return carry

    lax.fori_loop(0, tile // GROUP // ABREAST, some_groups, 0)


def attend(lens, partner, bias, q, k, v):
    slot, width = q.shape
    grid = slot // TILE
    once = pl.BlockSpec((slot, width), lambda i: (0, 0), pipeline_mode=pl.Buffered(1))
    pairs, per_tile = width // LANES, (TILE // GROUP) * 2 * BLOCK
    return pl.pallas_call(
        functools.partial(attend_kernel, slot=slot),
        grid=(grid,),
        in_specs=[
            smem(),
            smem(),
            smem(),
            pl.BlockSpec((TILE, width), lambda i: (i, 0)),
            once,
            once,
        ],
        out_specs=[
            pl.BlockSpec((width, TILE), lambda i: (0, i)),
            pl.BlockSpec((pairs, per_tile, 2 * GROUP), lambda i: (0, i, 0)),
        ],
        out_shape=[
            pltpu.HBM((width, slot), bf16),
            pltpu.HBM((pairs, grid * per_tile, 2 * GROUP), bf16),
        ],
        scratch_shapes=[
            pltpu.VMEM((2 * GROUP, 2 * GROUP), bf16),
        ],
        compiler_params=params(14),
        cost_estimate=pl.CostEstimate(
            flops=20 * 10**9, bytes_accessed=slot * width * 10, transcendentals=slot * 512
        ),
        name="attend",
    )(lens, partner, bias, q, k, v)


def attend_back_kernel(
    partner, q_ref, do_ref, p_ref, k_ref, v_ref,
    dq_ref, dk_ref, dv_ref, db_ref,
    mask_ref, dk_sum, dv_sum, db_sum,
):
    tile = q_ref.shape[0]
    step = pl.program_id(0)
    per = GROUP // BLOCK

    @pl.when(step == 0)
    def _():
        mask_ref[...] = diagonal_mask()
        dk_sum[...] = jnp.zeros_like(dk_sum)
        dv_sum[...] = jnp.zeros_like(dv_sum)

    scale = 1.0 / math.sqrt(HEAD)
    lanes = head_lanes()
    mask = mask_ref[...]
    work, d_probs, seconds, thirds = [], [], [], []
    for g in range(tile // GROUP):
        first = step * (tile // BLOCK) + g * per
        partners = [partner[0, first + c] for c in range(per)]
        rows = pl.ds(pl.multiple_of(first * BLOCK, GROUP), GROUP)
        spans = [rows] + [pl.ds(pl.multiple_of(p * BLOCK, BLOCK), BLOCK) for p in partners]
        q_rows = slice(g * GROUP, (g + 1) * GROUP)
        q_two = head_stack(q_ref[q_rows, :], lanes)
        do_two = head_stack(do_ref[q_rows, :], lanes)
        v_all = jnp.concatenate([v_ref[at, :] for at in spans], axis=0)
        work.append((g, spans, q_rows, q_two, do_two))
        d_probs.append(dot_nt(v_all, do_two))
    for d_prob, (g, *_) in zip(d_probs, work):
        at = g * 2 * BLOCK
        own_b = p_ref[0, at : at + BLOCK, :]
        far_b = p_ref[0, at + BLOCK : at + 2 * BLOCK, :]
        own, far = own_b.astype(f32), far_b.astype(f32)
        d_own, d_far = compact(d_prob[:GROUP]), compact(d_prob[GROUP:])
        delta = jnp.sum(own * d_own, axis=0, keepdims=True) + jnp.sum(
            far * d_far, axis=0, keepdims=True
        )
        d_own = own * (d_own - delta)
        d_far = far * (d_far - delta)
        d_bias = jnp.sum(d_far, axis=0, keepdims=True)
        db_sum[pl.ds(step * (tile // GROUP) + g, 1), :] = d_bias[:, :GROUP] + d_bias[:, GROUP:]
        seconds.append((spread(d_own * scale, d_far * scale, mask), spread(own_b, far_b, mask)))
    for (d_scores, prob), (g, spans, q_rows, q_two, do_two) in zip(seconds, work):
        k_all = jnp.concatenate([k_ref[at, :] for at in spans], axis=0)
        thirds.append((dot(d_scores, q_two), dot(prob, do_two), dot(k_all.T, d_scores)))
    for (dk, dv, dq), (g, spans, q_rows, *_) in zip(thirds, work):
        dq = jnp.concatenate([dq[:HEAD, :GROUP], dq[HEAD:, GROUP:]], axis=0)
        dq_ref[q_rows, :] = dq.T.astype(bf16)
        dk_sum[spans[0], :] += dk[:GROUP]
        dv_sum[spans[0], :] += dv[:GROUP]
        for c in range(per):
            here = slice(GROUP + c * BLOCK, GROUP + (c + 1) * BLOCK)
            dk_sum[spans[1 + c], :] += dk[here]
            dv_sum[spans[1 + c], :] += dv[here]

    @pl.when(step == pl.num_programs(0) - 1)
    def _():
        dk_ref[...] = dk_sum[...].astype(bf16)
        dv_ref[...] = dv_sum[...].astype(bf16)
        groups = db_sum.shape[0]
        blocks = groups * per
        pick = (iota((GROUP, blocks), 0) // BLOCK == iota((GROUP, blocks), 1) % per).astype(f32)
        sums = dot(db_sum[...], pick, highest)
        mine = iota((groups, blocks), 1) // per == iota((groups, blocks), 0)
        db_ref[...] = jnp.sum(jnp.where(mine, sums, 0.0), axis=0, keepdims=True)


def attend_back(pair, partner, q, d_o, probs, k, v):
    slot = q.shape[0]
    grid = slot // WIDE
    per_tile = (WIDE // GROUP) * 2 * BLOCK
    row = pl.BlockSpec((WIDE, LANES), lambda i: (i, pair))
    once = pl.BlockSpec((slot, LANES), lambda i: (0, pair), pipeline_mode=pl.Buffered(1))
    out = jax.ShapeDtypeStruct((slot, LANES), bf16)
    return pl.pallas_call(
        attend_back_kernel,
        grid=(grid,),
        in_specs=[
            smem(),
            row,
            row,
            pl.BlockSpec((1, per_tile, 2 * GROUP), lambda i: (pair, i, 0)),
            once,
            once,
        ],
        out_specs=[
            pl.BlockSpec((WIDE, LANES), lambda i: (i, 0)),
            whole((slot, LANES)),
            whole((slot, LANES)),
            whole((1, slot // BLOCK)),
        ],
        out_shape=[out, out, out, jax.ShapeDtypeStruct((1, slot // BLOCK), f32)],
        scratch_shapes=[
            pltpu.VMEM((2 * GROUP, 2 * GROUP), bf16),
            pltpu.VMEM((slot, LANES), f32),
            pltpu.VMEM((slot, LANES), f32),
            pltpu.VMEM((slot // GROUP, GROUP), f32),
        ],
        compiler_params=params(12),
        cost_estimate=pl.CostEstimate(
            flops=10 * 10**9, bytes_accessed=slot * LANES * 16, transcendentals=0
        ),
        name="attend_back",
    )(partner, *in_hbm(q, d_o, probs, k, v))


def ffn_kernel(
    place, x_ref, dy_ref, o_ref, norms_ref, w_ref,
    out_ref, dx_ref, do_ref, sent_in, sent_out, kept_in, kept_out, g_norm_ref,
    g_ref, h_scr, ht_scr, dyt_scr, y_scr, dh_scr, hat_scr, gt_scr, *, sorted_bits,
):
    tile, width = x_ref.shape
    hidden = gt_scr.shape[1]
    slabs = hidden // width
    parts = width // ROWS
    whole_rows = slice(slabs * ROWS, (slabs + 1) * ROWS)
    out_rows = slice((slabs + 1) * ROWS, (2 * slabs + 1) * ROWS)
    step = pl.program_id(0)

    share = parts // slabs
    fresh = step == 0

    def add_to(ref, at, value):
        ref[at] = value + jnp.where(fresh, 0.0, ref[at])

    root = math.sqrt(2.0 / math.pi)
    few = w_ref.shape[0]

    def blocks_of(first, count, at):
        if count <= few:
            part = slice(first % few, first % few + count)
            return w_ref[part, first // few, at, :].reshape(-1, width)
        return jnp.concatenate(
            [w_ref[:, upper, at, :].reshape(-1, width) for upper in range(count // few)], axis=0
        )

    w_in = [blocks_of(0, parts, slice(c * ROWS, (c + 1) * ROWS)) for c in range(slabs)]
    w_out = [blocks_of(c * share, share, out_rows) for c in range(slabs)]
    w_o = blocks_of(0, parts, whole_rows)

    def d_hidden(c):
        return dot_nt(dy_ref[...], w_out[c])

    def between(act, d_hid):
        square = act * act
        curve = jnp.tanh(act * (root + (root * 0.044715) * square))
        gate = 0.5 + 0.5 * curve
        hid = act * gate
        slope = gate + hid * (1.0 - curve) * (root + (3.0 * root * 0.044715) * square)
        return hid.astype(bf16), (d_hid * slope).astype(bf16)

    o_t = o_ref[...]
    x_one = x_ref[...].astype(f32) + dot(o_t.T, w_o)
    d_hid = d_hidden(0)
    dyt_scr[...] = dy_ref[...].T
    hat, rstd = norm_stats(x_one)
    h_two = (hat * norms_ref[2:3, :] + norms_ref[3:4, :]).astype(bf16)
    h_scr[...] = h_two
    hat_scr[...] = hat
    y_scr[...] = x_one
    act = dot(h_scr[...], w_in[0])
    ht_scr[...] = h_two.T
    for c in range(slabs):
        this_act, this_d = act, d_hid
        if c + 1 < slabs:
            d_hid = d_hidden(c + 1)
            act = dot(h_scr[...], w_in[c + 1])
        hid, d_act = between(this_act, this_d)
        more = dot_nt(d_act, w_in[c])
        dh_scr[...] = more if c == 0 else dh_scr[...] + more
        y_scr[...] += dot(hid, w_out[c])
        cols = slice(c * width, (c + 1) * width)
        add_to(gt_scr, (slice(None), cols), dot(dyt_scr[...], hid))
        slab = (slice(None), slice(c * ROWS, (c + 1) * ROWS), slice(None))
        add_to(g_ref, slab, dot(ht_scr[...], d_act).reshape(parts, ROWS, width))
    d_h = dh_scr[...]
    hat = hat_scr[...]
    d_x = dy_ref[...].astype(f32) + norm_back(d_h, hat, rstd, norms_ref[2:3, :])
    d_z = d_x.astype(bf16)
    dx_ref[...] = d_z
    do_ref[...] = dot_nt(d_z, w_o).astype(bf16)
    add_to(g_ref, (slice(None), whole_rows, slice(None)), dot(o_t, d_z).reshape(parts, ROWS, width))
    add_to(g_norm_ref, (slice(2, 3), slice(None)), jnp.sum(d_h * hat, axis=0, keepdims=True))
    add_to(g_norm_ref, (slice(3, 4), slice(None)), jnp.sum(d_h, axis=0, keepdims=True))
    out_ref[...] = y_scr[...].astype(bf16)

    @pl.when(fresh)
    def _():
        g_norm_ref[0:2, :] = jnp.zeros_like(g_norm_ref[0:2, :])
        g_norm_ref[4:, :] = jnp.zeros_like(g_norm_ref[4:, :])

    @pl.when(step == pl.num_programs(0) - 1)
    def _():
        for c in range(slabs):
            g_ref[c * share : (c + 1) * share, out_rows, :] = gt_scr[
                :, c * width : (c + 1) * width
            ].T.reshape(share, slabs * ROWS, width)
        first = (slabs + 1) * ROWS
        halves(
            place,
            (sent_in, sent_out, kept_in, kept_out),
            lambda i, part: g_ref[i, first:] if part else g_ref[i, :first],
            sorted_bits,
        )


def halves(place, refs, block, sorted_bits):
    mine = place[0] & 1
    parts = len(refs) // 2
    high = refs[0].shape[0] // 2

    def one(i, carry):
        low, next_low, rest = i & 1, (i >> 1) & 1, i >> 2
        spots = [low * high + next_low * (high // 2) + rest, next_low * high + low * (high // 2) + rest]
        for part in range(parts):
            at = spots[part] if sorted_bits else i
            refs[part][at] = block(2 * i + 1 - mine, part).astype(bf16)
            refs[parts + part][at] = block(2 * i + mine, part)
        return carry

    lax.fori_loop(0, 2 * high, one, 0)


def ffn(place, x, dy, o_t, norms, w_two, sorted_bits):
    slot, width = x.shape
    hidden = (w_two.shape[2] // ROWS - 1) // 2 * width
    blocks = (w_two.shape[0] * w_two.shape[1], *w_two.shape[2:])
    grid = slot // TILE
    first = hidden // width * ROWS + ROWS
    half_in = (blocks[0] // 2, first, width)
    half_out = (blocks[0] // 2, blocks[1] - first, width)
    row = pl.BlockSpec((TILE, width), lambda i: (i, 0))

    def once(shape):
        return pl.BlockSpec(shape, lambda i: (0,) * len(shape), pipeline_mode=pl.Buffered(1))

    return pl.pallas_call(
        functools.partial(ffn_kernel, sorted_bits=sorted_bits),
        grid=(grid,),
        in_specs=[
            smem(),
            row,
            row,
            pl.BlockSpec((width, TILE), lambda i: (0, i)),
            once(norms.shape),
            once(w_two.shape),
        ],
        out_specs=[
            row, row, row,
            once(half_in), once(half_out), once(half_in), once(half_out),
            once((8, width)),
        ],
        out_shape=[
            pltpu.HBM((slot, width), bf16),
            pltpu.HBM((slot, width), bf16),
            pltpu.HBM((slot, width), bf16),
            pltpu.HBM(half_in, bf16),
            pltpu.HBM(half_out, bf16),
            pltpu.HBM(half_in, f32),
            pltpu.HBM(half_out, f32),
            pltpu.HBM((8, width), f32),
        ],
        scratch_shapes=[
            pltpu.VMEM(blocks, f32),
            pltpu.VMEM((TILE, width), bf16),
            pltpu.VMEM((width, TILE), bf16),
            pltpu.VMEM((width, TILE), bf16),
            pltpu.VMEM((TILE, width), f32),
            pltpu.VMEM((TILE, width), f32),
            pltpu.VMEM((TILE, width), f32),
            pltpu.VMEM((width, hidden), f32),
        ],
        compiler_params=params(42),
        cost_estimate=pl.CostEstimate(
            flops=2 * slot * width * (3 * width + 6 * hidden),
            bytes_accessed=slot * width * 14,
            transcendentals=slot * hidden,
        ),
        name="ffn",
    )(place, *in_hbm(x, dy, o_t), norms, *in_hbm(w_two))


def project_back_kernel(
    place, lens, x_ref, dx_ref, du_ref, norms_ref, w_ref, g_sort_ref, g_two_ref, *refs, slot,
    sorted_bits,
):
    *d_refs, grad_ref, sent_a, sent_b, kept_a, kept_b, g_ref, g_norm_ref = refs
    tile, width = x_ref.shape
    step = pl.program_id(0)

    @pl.when(step == 0)
    def _():
        g_ref[...] = jnp.zeros_like(g_ref)
        g_norm_ref[...] = jnp.zeros_like(g_norm_ref)

    pairs = width // LANES
    ends = ends_of(lens, slot)
    blocks = SUB // BLOCK
    starts = range(0, tile, SUB)
    d_hs, hats, rstds, h_ones = [], [], [], []
    for r in starts:
        rows = slice(r, r + SUB)
        places = step * tile + r + iota((SUB, 1), 0)
        live = places < end_at(places, ends, slot)
        d_u = du_ref[r // BLOCK : r // BLOCK + blocks, :].reshape(blocks, 1, width)
        d_h = jnp.broadcast_to(d_u, (blocks, BLOCK, width)).reshape(SUB, width)
        d_h = jnp.where(live, d_h, 0.0)
        for part in range(3):
            cols = slice(part * width, (part + 1) * width)
            d_part = jnp.concatenate(
                [ref[rows, :] for ref in d_refs[part * pairs : (part + 1) * pairs]], axis=1
            )
            d_h = d_h + dot_nt(d_part, w_ref[:, cols])
        d_hs.append(d_h)
        hat, rstd = norm_stats(x_ref[rows, :].astype(f32))
        hats.append(hat)
        rstds.append(rstd)
        h_ones.append((hat * norms_ref[0:1, :] + norms_ref[1:2, :]).astype(bf16))
    h_one = jnp.concatenate(h_ones, axis=0)

    def back(at):
        rows = slice(at * SUB, (at + 1) * SUB)
        g_norm_ref[0:1, :] += jnp.sum(d_hs[at] * hats[at], axis=0, keepdims=True)
        g_norm_ref[1:2, :] += jnp.sum(d_hs[at], axis=0, keepdims=True)
        grad_ref[rows, :] = dx_ref[rows, :].astype(f32) + norm_back(
            d_hs[at], hats[at], rstds[at], norms_ref[0:1, :]
        )

    done = 0
    for part in range(3):
        cols = slice(part * width, (part + 1) * width)
        d_part = jnp.concatenate([ref[...] for ref in d_refs[part * pairs : (part + 1) * pairs]], axis=1)
        g_ref[:, cols] += dot_tn(h_one, d_part)
        until = len(starts) * (part + 1) // 3
        for at in range(done, until):
            back(at)
        done = until

    @pl.when(step == pl.num_programs(0) - 1)
    def _():
        g_ref[:, 3 * width : 3 * width + LANES] = g_sort_ref[...]
        small = g_norm_ref[...] + g_two_ref[...]
        rest = jnp.zeros((LANES - small.shape[0], width), f32)
        g_ref[:, 3 * width + LANES :] = jnp.concatenate([small, rest], axis=0).T
        cols = sent_a.shape[2]
        halves(
            place,
            (sent_a, sent_b, kept_a, kept_b),
            lambda i, part: g_ref[
                pl.ds(pl.multiple_of(i * ROWS, ROWS), ROWS), part * cols : (part + 1) * cols
            ],
            sorted_bits,
        )


def project_back(
    place, lens, x, d_x, d_q, d_k, d_v, d_u, norms, w_one, g_sort, g_two, sorted_bits
):
    slot, width = x.shape
    grid = slot // TILE
    row = pl.BlockSpec((TILE, width), lambda i: (i, 0))
    half = (width // ROWS // 2, ROWS, w_one.shape[1] // 2)

    def once(shape):
        return pl.BlockSpec(shape, lambda i: (0,) * len(shape), pipeline_mode=pl.Buffered(1))

    return pl.pallas_call(
        functools.partial(project_back_kernel, slot=slot, sorted_bits=sorted_bits),
        grid=(grid,),
        in_specs=[
            smem(),
            smem(),
            row,
            row,
            pl.BlockSpec((TILE // BLOCK, width), lambda i: (i, 0)),
            once(norms.shape),
            once(w_one.shape),
            once(g_sort.shape),
            once(g_two.shape),
        ]
        + [pl.BlockSpec((TILE, LANES), lambda i: (i, 0))] * (3 * width // LANES),
        out_specs=[row] + [once(half)] * 4,
        out_shape=[
            jax.ShapeDtypeStruct((slot, width), f32),
            jax.ShapeDtypeStruct(half, bf16),
            jax.ShapeDtypeStruct(half, bf16),
            jax.ShapeDtypeStruct(half, f32),
            jax.ShapeDtypeStruct(half, f32),
        ],
        scratch_shapes=[pltpu.VMEM(w_one.shape, f32), pltpu.VMEM((8, width), f32)],
        compiler_params=params(18),
        cost_estimate=pl.CostEstimate(
            flops=2 * slot * width * 6 * width, bytes_accessed=slot * width * 18, transcendentals=0
        ),
        name="project_back",
    )(place, lens, *in_hbm(x, d_x), d_u, norms, w_one, g_sort, g_two, *d_q, *d_k, *d_v)


def pack_kernel(wqkv, wo, wsort, win, wout, norms_t, one_ref, two_ref):
    rows, wide = wqkv.shape
    width = wo.shape[1]
    one_ref[:, :wide] = wqkv[...].astype(bf16)
    one_ref[:, wide : wide + LANES] = wsort[...].astype(bf16)
    few = norms_t.shape[0]
    tall = jnp.concatenate([norms_t[...], jnp.zeros((LANES - few, rows), f32)], axis=0)
    one_ref[:, wide + LANES :] = tall.T.astype(bf16)
    slabs = win.shape[1] // width
    for c in range(slabs):
        two_ref[c * rows : (c + 1) * rows, :] = win[:, c * width : (c + 1) * width].astype(bf16)
    two_ref[slabs * rows : (slabs + 1) * rows, :] = wo[...].astype(bf16)
    two_ref[(slabs + 1) * rows :, :] = wout[...].astype(bf16)


def pack(masters):
    wqkv, wo, wsort, win, wout, norms = masters
    rows = wqkv.shape[0]
    return pl.pallas_call(
        pack_kernel,
        out_shape=[
            jax.ShapeDtypeStruct((rows, wqkv.shape[1] + 2 * LANES), bf16),
            jax.ShapeDtypeStruct((rows * (win.shape[1] // wo.shape[1] + 1) + wout.shape[0], wo.shape[1]), bf16),
        ],
        compiler_params=params(8),
        name="pack",
    )(*in_hbm(wqkv, wo, wsort, win, wout), norms.T)


def adamw_kernel(*refs, ones, twos):
    one_ref = sum(ref[...].astype(f32) for ref in refs[:ones])
    two_ref = sum(ref[...].astype(f32) for ref in refs[ones : ones + twos])
    refs = refs[ones + twos :]
    masters, moments, squares, outs = refs[:6], refs[6:12], refs[12:18], refs[18:]
    rows, width = masters[1].shape
    wide = masters[0].shape[1]
    slabs = masters[3].shape[1] // width
    few = masters[5].shape[0]
    norm_grad = one_ref[:, wide + LANES :].T[:few, :]
    grads = (
        one_ref[:, :wide],
        two_ref[slabs * rows : (slabs + 1) * rows, :],
        one_ref[:, wide : wide + LANES],
        jnp.concatenate([two_ref[c * rows : (c + 1) * rows, :] for c in range(slabs)], axis=1),
        two_ref[(slabs + 1) * rows :, :],
        norm_grad,
    )
    for i in range(6):
        weight, grad = masters[i][...], grads[i]
        moment = beta_one * moments[i][...] + (1.0 - beta_one) * grad
        square = beta_two * squares[i][...] + (1.0 - beta_two) * grad * grad
        m_hat = moment / (1.0 - beta_one**STEP)
        s_hat = square / (1.0 - beta_two**STEP)
        outs[3 * i][...] = weight - rates[i] * (
            m_hat / (jnp.sqrt(s_hat) + adam_eps) + decay * weight
        )
        outs[3 * i + 1][...] = moment
        outs[3 * i + 2][...] = square


def adamw(one, two, masters, moments, squares):
    flip = lambda group: (*group[:5], group[5].T)
    args = (*one, *two, *flip(masters), *flip(moments), *flip(squares))
    shapes = [a.shape for a in flip(masters)]
    outs = pl.pallas_call(
        functools.partial(adamw_kernel, ones=len(one), twos=len(two)),
        out_shape=[jax.ShapeDtypeStruct(shape, f32) for shape in shapes for _ in range(3)],
        compiler_params=params(12),
        name="adamw",
    )(*args)
    return (*outs[:15], *[o.T for o in outs[15:]])


def regroup(gathered, rows, slabs):
    size, width = gathered.shape[0], gathered.shape[-1]
    times = ROWS // rows
    block = gathered.reshape(size // times, times, 2 * slabs + 1, rows, width)
    inner = block[:, :, : slabs + 1].transpose(0, 2, 1, 3, 4)
    outer = block[:, :, slabs + 1 :]
    return jnp.concatenate(
        [
            inner.reshape(size // times, (slabs + 1) * ROWS, width),
            outer.reshape(size // times, slabs * ROWS, width),
        ],
        axis=1,
    )[:, None]


def device_halves(place, sent, kept, size, rows, slabs, axis):
    if rows == ROWS:
        return sent, kept
    cut = kept[0].shape[axis + 1] * rows // ROWS if slabs else kept[0].shape[axis + 1]
    sent, kept = jnp.concatenate(sent, axis=axis + 1), jnp.concatenate(kept, axis=axis + 1)
    mine = place[0] & 1
    low = jnp.where(mine == 0, kept, sent.astype(f32))
    high = jnp.where(mine == 0, sent.astype(f32), kept)
    grads = jnp.stack([low, high], axis=1).reshape((-1,) + kept.shape[1:])
    times = ROWS // rows
    width = grads.shape[-1]
    wide = (slabs + 1) * ROWS
    inner = grads[:, :wide].reshape(size // times, slabs + 1, times, rows, width)
    outer = grads[:, wide:].reshape(size // times, times, slabs, rows, width)
    block = jnp.concatenate([inner.transpose(0, 2, 1, 3, 4), outer], axis=2)
    block = block.reshape(size // 2, 2, (2 * slabs + 1) * rows, width)
    count = size.bit_length() - 1
    results = []
    for index, kind in ((1 - mine, bf16), (mine, f32)):
        half = lax.dynamic_index_in_dim(block, index, 1, keepdims=False).astype(kind)
        for part, lead in zip(jnp.split(half, [cut], axis=axis + 1), ((1, 2), (2, 1))):
            bits = part.reshape((2,) * (count - 1) + part.shape[1:])
            order = [count - 1 - bit for bit in lead] + list(range(count - 3))
            order += list(range(count - 1, bits.ndim))
            results.append(bits.transpose(order).reshape(part.shape))
    return results[:2], results[2:]


def swap(value, mask, size):
    return lax.ppermute(value, "dp", [(i, i ^ mask) for i in range(size)])


def masks_of(bits):
    return [sum(((turn >> at) & 1) << bit for at, bit in enumerate(bits)) for turn in range(2 ** len(bits))]


def fours(count):
    return [tuple(range(bit, min(bit + 2, count))) for bit in range(3, count, 2)]


def gather(block, size):
    held = block[None]
    for bits in fours(size.bit_length() - 1)[::-1] + [(2,), (1,)]:
        came = [swap(held, mask, size) for mask in masks_of(bits)[1:]]
        held = jnp.stack([held, *came], axis=1).reshape((-1,) + block.shape)
    return held, swap(held, 1, size)


class ScatterSum:
    def __init__(self, sent, kept, size, axis):
        self.size, self.axis = size, axis
        self.place = lax.axis_index("dp")
        self.plan = [(1, 2), (2, 1)] + fours(size.bit_length() - 1)[::-1]
        self.kept, self.sent, self.masks = list(kept), list(sent), [1, 1]

    def send(self):
        self.came = [swap(sent, mask, self.size) for sent, mask in zip(self.sent, self.masks)]

    def cut(self, ways, index, values):
        parts = [value.reshape((ways, -1) + value.shape[1:]) for value in values]
        parts = [lax.dynamic_index_in_dim(part, index, 0, keepdims=False) for part in parts]
        return sum(part.astype(f32) for part in parts)

    def step(self):
        bits = self.plan.pop(0)
        if bits[0] < 3:
            kept, came = self.kept, self.came
            mine = [(self.place >> bit) & 1 for bit in bits]
            self.kept = [self.cut(2, m, pair) for m, pair in zip(mine, zip(kept, came))]
            self.sent = [self.cut(2, 1 - m, pair).astype(bf16) for m, pair in zip(mine, zip(kept, came))]
            self.masks = [1 << bit for bit in bits]
            return
        values = [*self.kept, *self.came]
        if len(self.kept) == 2:
            values = [jnp.concatenate(pair, axis=self.axis + 1) for pair in (self.kept, self.came)]
        ways = 2 ** len(bits)
        mine = (self.place >> bits[0]) & (ways - 1)
        self.kept = [self.cut(ways, mine, values)]
        self.sent = [self.cut(ways, mine ^ turn, values).astype(bf16) for turn in range(1, ways)]
        self.masks = masks_of(bits)[1:]

    def after(self, values):
        self.came, values = lax.optimization_barrier((self.came, values))
        return values

    def before(self, values):
        self.sent, values = lax.optimization_barrier((self.sent, values))
        return values

    def last(self):
        return [value.reshape(value.shape[1:]) for value in (*self.kept, *self.came)]


def body(size, x, dy, lens, partner, *state):
    slot, width = x.shape
    masters, moments, squares = state[:6], state[6:12], state[12:]
    rows = masters[0].shape[0]
    slabs = masters[3].shape[1] // width
    place = lax.axis_index("dp").astype(jnp.int32).reshape((1,))
    pack_one, pack_two = pack(masters)
    near, far = gather(pack_one, size)
    if rows == ROWS:
        w_two = lax.all_gather(pack_two, "dp", axis=0)[:, None]
    else:
        w_two = regroup(lax.all_gather(pack_two, "dp", axis=0), rows, slabs)

    q, k, v, u, norms, w_one = project(place, lens, x, near, far)
    bias, steps = sort_net(lens, u, w_one, partner, slot)
    o_t, probs = attend(lens, partner, bias, q, k, v)
    direct = rows == ROWS
    out, d_x, d_o, *parts, g_two = ffn(place, x, dy, o_t, norms, w_two, direct)
    sent, kept = device_halves(place, parts[:2], parts[2:], size, rows, slabs, 0)
    two = ScatterSum(sent, kept, size, 0)
    two.send()

    def back(pair):
        return attend_back(pair, partner, q, d_o, probs, k, v)

    def next_stage(values):
        two.step()
        values = two.before(values)
        two.send()
        return values

    back_0 = two.after(back(0))
    q, d_o = next_stage((q, d_o))
    back_1, back_2 = two.after((back(1), back(2)))
    q, d_o = next_stage((q, d_o))
    back_3 = two.after(back(3))
    u, back_3 = next_stage((u, back_3))
    d_q, d_k, d_v, d_bias = zip(back_0, back_1, back_2, back_3)
    d_u, g_sort = sort_back(lens, u, w_one, partner, d_bias, steps, slot)
    while two.plan:
        d_u = next_stage(two.after(d_u))
    grad_in, *parts = project_back(
        place, lens, x, d_x, d_q, d_k, d_v, d_u, norms, w_one, g_sort, g_two, direct
    )
    grad_in, parts = two.after((grad_in, parts))
    sent, kept = device_halves(place, parts[:2], parts[2:], size, rows, 0, 1)
    one = ScatterSum(sent, kept, size, 1)
    one.send()
    while one.plan:
        one.step()
        one.send()
    outs = adamw(one.last(), two.last(), masters, moments, squares)
    return (out, grad_in, *outs)


def solution(mesh):
    spec = P("dp", None)
    return jax.shard_map(
        functools.partial(body, mesh.shape["dp"]),
        mesh=mesh,
        in_specs=(spec,) * 22,
        out_specs=(spec,) * 20,
        check_vma=False,
    )
```
